256 devices in a mesh: ang: 32 (over z_lo, x, core), strip: 8 (over z_hi, y).
Axes of the slice: x: 4, y: 4, z: 8 (z_hi: 2, z_lo: 4; z = z_hi * 4 + z_lo), core: 2. Of those that a mesh axis runs over, the one named last changes fastest.
Arguments:
- measured: float32 [32, 64, 128, 128], P('ang', 'strip'), may hold values from 0.05 to 4
- positions: int32 [32, 64], P('ang', 'strip'), may hold values from 0 to 384
- probe_field: float32 [2, 128, 128], replicated, may hold values from -6 to 6
- object_field: float32 [32, 512, 2, 128], P('ang', 'strip'), may hold values from -6 to 6
- dual_field: float32 [32, 512, 2, 128], P('ang', 'strip'), may hold values from -6 to 6
- volume: float32 [65536, 2, 128], P(('ang', 'strip')), may hold values from -6 to 6
- radon_tiles: bfloat16 [256, 32, 2, 32, 256], P(('ang', 'strip')), may hold values from -0.0625 to 0.0625
- tile_range: int32 [32, 32, 8, 1], P('ang', None, 'strip'), may hold values from 0 to 14
Outputs:
- object_next: float32 [32, 512, 2, 128], P('ang', 'strip')
- dual_next: float32 [32, 512, 2, 128], P('ang', 'strip')
- volume_next: float32 [65536, 2, 128], P(('ang', 'strip'))
The draws below stay inside these ranges and needn't reach their ends.
Inputs may be any that keep to these rules, and one draw needn't show every extreme that they name: `positions`: a frame covers 128 detector columns from its position. A pixel tile meets ray tiles tile_range to tile_range + 1 at that angle.
All inputs are finite; a program needn't handle non-finite values.
Results may differ from the reference program's by a relative error of at most 0.0027.
Values may be sent and summed in bfloat16 or wider, within the bound.
No kernel may reach another device: no remote copies, remote signals or barrier semaphores. Data moves between devices by JAX's collectives and lax.ppermute only.
A program may use at most 64 MiB of HBM per device.

```python
import math
import jax
import jax.numpy as jnp
from jax import lax

PROBE = 128
NZ = 128
NDET = 512
RAYS = 32
TILE = 256
HITS = 2
PT_DEV = 1
NANG = 32
FR = 64
NPT = 256
NPIX = 65536
NR = 16
N_ANG = 32
N_STRIP = 8


def with_ends(array, own_key, least, top_value):
    index_at = [jax.random.randint(jax.random.fold_in(own_key, axis), (), 0, length) for axis, length in enumerate(array.shape)]
    longest = array.shape.index(max(array.shape))
    next_to = index_at[:longest] + [(index_at[longest] + 1) % array.shape[longest]] + index_at[longest + 1:]
    return array.at[tuple(index_at)].set(least).at[tuple(next_to)].set(top_value)


def steps_of(stream_key, shape, split, low, largest):
    factor_of = 1.0
    for axis_at, parts in split:
        heights = jax.random.uniform(jax.random.fold_in(jax.random.fold_in(stream_key, 6), axis_at), (parts,), jnp.float32, low / len(split), largest / len(split))
        factor_of = factor_of * jnp.repeat(jnp.exp(heights), shape[axis_at] // parts).reshape((-1,) + (1,) * (len(shape) - 1 - axis_at))
    return factor_of


def noise(key, shape, scale, most, cuts=(), kind=jnp.bfloat16):
    gain = steps_of(key, shape, cuts, -0.22, 0.18) if cuts else 1.0
    result = jax.random.normal(key, shape, jnp.float32) * scale * gain
    return jnp.minimum(jnp.maximum(result, -most), most).astype(kind)


def setup_inputs(seed: int = 0) -> dict:
    key_of = jax.random.split(jax.random.key(seed), 9)
    return {
        "measured": jnp.clip(jnp.exp(math.log(4.0) - 4.3820266 * jax.random.uniform(key_of[0], (NANG, FR, PROBE, PROBE), jnp.float32) ** steps_of(key_of[0], (NANG, FR, PROBE, PROBE), ((0, 32), (1, 8)), -0.2, 0.2)), 0.05, 4.0),
        "positions": with_ends(jax.random.randint(key_of[1], (NANG, FR), 0, NDET - PROBE + 1), jax.random.fold_in(key_of[1], 1), 0, NDET - PROBE).astype(jnp.int32),
        "probe_field": noise(key_of[2], (2, PROBE, PROBE), 1.0, 6.0, (), jnp.float32),
        "object_field": noise(key_of[3], (NANG, NDET, 2, NZ), 1.0, 6.0, ((0, 32), (1, 8)), jnp.float32),
        "dual_field": noise(key_of[4], (NANG, NDET, 2, NZ), 1.0, 6.0, ((0, 32), (1, 8)), jnp.float32),
        "volume": noise(key_of[5], (NPIX, 2, NZ), 1.0, 6.0, ((0, 256),), jnp.float32),
        "radon_tiles": noise(key_of[6], (NPT, NANG, HITS, RAYS, TILE), (HITS * NPT * TILE // NR) ** -0.5, 0.0625, ((0, 256),)),
        "tile_range": with_ends(jax.random.randint(key_of[7], (NANG, N_ANG, N_STRIP, PT_DEV), 0, NR - HITS + 1), jax.random.fold_in(key_of[7], 1), 0, NR - HITS).astype(jnp.int32),
    }


penalty = 1.0
object_step = 0.1
volume_step = 1.0
precise = lax.Precision.HIGHEST

def dft_tables(length):
    indices = jnp.arange(length, dtype=jnp.int32)
    phases = indices[:, None] * indices[None, :] % length
    angles = phases.astype(jnp.float32) * (2.0 * math.pi / length)
    scaling = 1.0 / math.sqrt(length)
    return (jnp.cos(angles) * scaling, jnp.sin(angles) * scaling)

def transform(real_part, imag_part, cosine_table, sine_table, handed):
    left_re = jnp.einsum('kc,fcr->fkr', cosine_table, real_part, precision=precise) + handed * jnp.einsum('kc,fcr->fkr', sine_table, imag_part, precision=precise)
    left_im = jnp.einsum('kc,fcr->fkr', cosine_table, imag_part, precision=precise) - handed * jnp.einsum('kc,fcr->fkr', sine_table, real_part, precision=precise)
    out_re = jnp.einsum('fkr,rl->fkl', left_re, cosine_table, precision=precise) + handed * jnp.einsum('fkr,rl->fkl', left_im, sine_table, precision=precise)
    out_im = jnp.einsum('fkr,rl->fkl', left_im, cosine_table, precision=precise) - handed * jnp.einsum('fkr,rl->fkl', left_re, sine_table, precision=precise)
    return (out_re, out_im)

def intersection_gradient(intensity, starts, field, probe_field, cosine_table, sine_table):
    window = probe_field.shape[1]

    def cutout(start):
        return lax.dynamic_slice_in_dim(field, start, window, 0)
    patches = jax.vmap(cutout)(starts)
    object_re = patches[:, :, 0, :]
    object_im = patches[:, :, 1, :]
    probe_re = probe_field[0]
    probe_im = probe_field[1]
    wave_re = probe_re * object_re - probe_im * object_im
    wave_im = probe_re * object_im + probe_im * object_re
    far_re, far_im = transform(wave_re, wave_im, cosine_table, sine_table, 1.0)
    modulus = jnp.sqrt(far_re * far_re + far_im * far_im)
    shrink = 1.0 - jnp.sqrt(intensity) / jnp.maximum(modulus, 1.0)
    back_re, back_im = transform(far_re * shrink, far_im * shrink, cosine_table, sine_table, -1.0)
    grad_re = probe_re * back_re + probe_im * back_im
    grad_im = probe_re * back_im - probe_im * back_re
    frame_grads = jnp.stack([grad_re, grad_im], axis=2)

    def deposit(index, total):
        piece = lax.dynamic_slice_in_dim(total, starts[index], window, 0)
        return lax.dynamic_update_slice_in_dim(total, piece + frame_grads[index], starts[index], 0)
    return lax.fori_loop(0, starts.shape[0], deposit, jnp.zeros(field.shape, jnp.float32))

def reference(measured, positions, probe_field, object_field, dual_field, volume, radon_tiles, tile_range):
    cosine_table, sine_table = dft_tables(PROBE)

    def ptycho_angle(inputs):
        intensity, starts, field = inputs
        return intersection_gradient(intensity, starts, field, probe_field, cosine_table, sine_table)
    intersection = lax.map(ptycho_angle, (measured, positions, object_field))
    volume_half = lax.optimization_barrier(volume.astype(jnp.bfloat16)).astype(jnp.float32).reshape(NPT, TILE, 2 * NZ)
    ranges = tile_range.reshape(NANG, NPT)
    hit_offsets = jnp.arange(HITS, dtype=jnp.int32)
    range_ids = jnp.arange(NR, dtype=jnp.int32)

    def tiles_at(angle_index):
        return lax.dynamic_index_in_dim(radon_tiles, angle_index, 1, keepdims=False).astype(jnp.float32)

    def targets_at(angle_index):
        return (ranges[angle_index][:, None] + hit_offsets[None, :]).reshape(NPT * HITS)

    def project_angle(angle_index):
        partials = jnp.einsum('phrt,ptc->phrc', tiles_at(angle_index), volume_half, precision=precise)
        selector = (range_ids[:, None] == targets_at(angle_index)[None, :]).astype(jnp.float32)
        dense_rows = jnp.dot(selector, partials.reshape(NPT * HITS, RAYS * 2 * NZ), precision=precise)
        return dense_rows.reshape(NDET, 2, NZ)
    projection = lax.map(project_angle, jnp.arange(NANG, dtype=jnp.int32))
    object_next = object_field - object_step * (intersection + dual_field + penalty * (object_field - projection))
    dual_next = dual_field + penalty * (object_next - projection)
    residual = lax.optimization_barrier((penalty * (projection - object_next) - dual_field).astype(jnp.bfloat16)).astype(jnp.float32)

    def back_angle(total, angle_index):
        selector = (targets_at(angle_index)[:, None] == range_ids[None, :]).astype(jnp.float32)
        rows = residual[angle_index].reshape(NR, RAYS * 2 * NZ)
        picked = jnp.dot(selector, rows, precision=precise).reshape(NPT, HITS, RAYS, 2 * NZ)
        return (total + jnp.einsum('phrt,phrc->ptc', tiles_at(angle_index), picked, precision=precise), None)
    gradient, unused = lax.scan(back_angle, jnp.zeros((NPT, TILE, 2 * NZ), jnp.float32), jnp.arange(NANG, dtype=jnp.int32))
    volume_next = volume - volume_step * gradient.reshape(NPIX, 2, NZ)
    return (object_next, dual_next, volume_next)
```

```python
import math

import jax
import jax.numpy as jnp
import numpy as np
from jax import lax
from jax.experimental import pallas as pl
from jax.experimental.pallas import tpu as pltpu
from jax.sharding import Mesh
from jax.sharding import PartitionSpec as P

PROBE = 128
NZ = 128
NDET = 512
RAYS = 32
TILE = 256
HITS = 2
NR = 16

ZL, X, C, ZH, Y = 4, 4, 2, 2, 4
XC = X * C
CROSS = ("x", "c", "y")
ALONG = ("zh", "zl")
NEAR = XC * Y
DEEP = ZH * ZL
QR = RAYS // Y
FR_DEV = 8

penalty = 1.0
object_step = 0.1
volume_step = 1.0
f32 = jnp.float32
bf16 = jnp.bfloat16

VM = pl.BlockSpec(memory_space=pltpu.VMEM)
SM = pl.BlockSpec(memory_space=pltpu.SMEM)


def call(kernel, outs, n_smem, n_vmem, scratch=(), flops=0, moved=1 << 20, limit=48 << 20):
    many = isinstance(outs, tuple)
    return pl.pallas_call(
        kernel,
        out_shape=outs,
        in_specs=[SM] * n_smem + [VM] * n_vmem,
        out_specs=tuple(VM for _ in outs) if many else VM,
        scratch_shapes=list(scratch),
        compiler_params=pltpu.CompilerParams(vmem_limit_bytes=limit),
        cost_estimate=pl.CostEstimate(flops=flops, bytes_accessed=moved, transcendentals=0),
        name=kernel.__name__,
    )


def shape(*dims, dtype=f32):
    return jax.ShapeDtypeStruct(dims, dtype)


def dft_blocks():
    k = np.arange(PROBE)
    angles = (k[:, None] * k[None, :] % PROBE) * (2.0 * math.pi / PROBE)
    cosine = np.cos(angles) / math.sqrt(PROBE)
    sine = np.sin(angles) / math.sqrt(PROBE)
    left = np.block([[cosine, sine], [-sine, cosine]]).astype(np.float32)
    high = left.astype(jnp.bfloat16)
    low = (left - high.astype(np.float32)).astype(jnp.bfloat16)
    return jnp.asarray(high), jnp.asarray(low), jnp.asarray(high.T.copy()), jnp.asarray(low.T.copy())


def ray_sums(radon_ref, volume_ref, out_ref):
    volume_half = jnp.concatenate(
        [volume_ref[pl.ds(0, TILE, stride=2), :], volume_ref[pl.ds(1, TILE, stride=2), :]], axis=1
    ).astype(bf16)
    for zl in range(ZL):
        for xc in range(XC):
            rows = radon_ref[zl * XC + xc].reshape(HITS * RAYS, TILE)
            sums = jnp.dot(rows, volume_half, preferred_element_type=f32)
            for y in range(Y):
                low = sums[y * QR : (y + 1) * QR]
                high = sums[RAYS + y * QR : RAYS + (y + 1) * QR]
                out_ref[xc * Y + y, zl] = jnp.concatenate([low, high], axis=0).astype(bf16)


def add_tiles(target_ref, sums_ref, out_ref, total):
    total[...] = jnp.zeros(total.shape, f32)

    def step(source, carry):
        for zl in range(ZL):
            row = pl.multiple_of(target_ref[zl, source] * QR, QR)
            total[zl, pl.ds(row, HITS * QR), :] += sums_ref[source, zl].astype(f32)
        return carry

    lax.fori_loop(0, NEAR, step, 0, unroll=4)
    for zh in range(ZH):
        for zl in range(ZL):
            out_ref[zh * ZL + zl] = total[zl, :, zh * NZ : (zh + 1) * NZ].astype(bf16)


def residual_part(sums_ref, inter_ref, drift_ref, residual_ref, keep_ref):
    projection = sums_ref[0].astype(f32)
    for source in range(1, DEEP):
        projection = projection + sums_ref[source].astype(f32)
    inter = inter_ref[...]
    gap = projection - drift_ref[...]
    residual_ref[...] = (gap + object_step * (inter - gap)).astype(bf16)
    keep_ref[0] = projection
    keep_ref[1] = inter


def pick_tiles(target_ref, residual_ref, out_ref, rows_ref):
    for zl in range(ZL):
        rows_ref[zl] = jnp.concatenate(
            [residual_ref[zl].astype(f32), residual_ref[ZL + zl].astype(f32)], axis=1
        )

    def step(dest, carry):
        for zl in range(ZL):
            row = pl.multiple_of(target_ref[zl, dest] * QR, QR)
            out_ref[dest, zl] = rows_ref[zl, pl.ds(row, HITS * QR), :].astype(bf16)
        return carry

    lax.fori_loop(0, NEAR, step, 0, unroll=4)


def back_project(radon_ref, picked_ref, volume_ref, out_ref):
    gradient = jnp.dot(
        radon_ref[...],
        picked_ref[...].reshape(NEAR * ZL * HITS * QR, 2 * NZ),
        preferred_element_type=f32,
    )
    for part in range(2):
        rows = pl.ds(part, TILE, stride=2)
        out_ref[rows, :] = volume_ref[rows, :] - volume_step * gradient[:, part * NZ : (part + 1) * NZ]


def updates(place_ref, kept_ref, object_ref, dual_ref, object_out, dual_out):
    zh = place_ref[0]
    y = place_ref[1]
    for other in range(ZH):
        part = lax.rem(zh + other, ZH)
        for back in range(Y):
            source = lax.rem(y + Y - back, Y)
            for tile in range(2):
                rows = pl.ds((tile * RAYS + source * QR) * 2 + part, QR, stride=2)
                projection = kept_ref[other, back, 0, tile * QR : (tile + 1) * QR, :]
                inter = kept_ref[other, back, 1, tile * QR : (tile + 1) * QR, :]
                field = object_ref[rows, :]
                dual = dual_ref[rows, :]
                object_next = field - object_step * (inter + dual + penalty * (field - projection))
                object_out[rows, :] = object_next
                dual_out[rows, :] = dual + penalty * (object_next - projection)


def split(value):
    high = value.astype(bf16)
    return high, (value - high.astype(f32)).astype(bf16)


def from_left(high_table, low_table, value):
    high, low = split(value)
    return (
        jnp.dot(high_table, high, preferred_element_type=f32)
        + jnp.dot(high_table, low, preferred_element_type=f32)
        + jnp.dot(low_table, high, preferred_element_type=f32)
    )


def from_right(value, high_table, low_table):
    high, low = split(value)
    return (
        jnp.dot(high, high_table, preferred_element_type=f32)
        + jnp.dot(low, high_table, preferred_element_type=f32)
        + jnp.dot(high, low_table, preferred_element_type=f32)
    )


def frame_gradients(
    place_ref, starts_ref, field_ref, probe_ref, measured_ref, ah_ref, al_ref, bh_ref, bl_ref,
    own_ref, sent_ref, field_re, field_im, total_re, total_im, staged,
):
    zh = place_ref[0]
    y = place_ref[1]
    for back in range(Y):
        for other in range(ZH):
            owner = lax.rem(zh + other, ZH) * Y + lax.rem(y + Y - back, Y)
            rows = pl.ds(pl.multiple_of(owner * 64, 64), 64)
            staged[...] = field_ref[back, other]
            field_re[rows, :] = staged[pl.ds(0, 64, stride=2), :]
            field_im[rows, :] = staged[pl.ds(1, 64, stride=2), :]
    total_re[...] = jnp.zeros(total_re.shape, f32)
    total_im[...] = jnp.zeros(total_im.shape, f32)
    probe_re = probe_ref[0]
    probe_im = probe_ref[1]
    ah, al, bh, bl = ah_ref[...], al_ref[...], bh_ref[...], bl_ref[...]
    for pair in range(FR_DEV // 2):
        waves = []
        for frame in (2 * pair, 2 * pair + 1):
            rows = pl.ds(starts_ref[0, frame], PROBE)
            object_re = field_re[rows, :]
            object_im = field_im[rows, :]
            waves.append(
                jnp.concatenate(
                    [
                        probe_re * object_re - probe_im * object_im,
                        probe_re * object_im + probe_im * object_re,
                    ],
                    axis=0,
                )
            )
        lefts = from_left(ah, al, jnp.concatenate(waves, axis=1))
        sides = jnp.concatenate(
            [
                jnp.concatenate([lefts[:PROBE, i * NZ : (i + 1) * NZ], lefts[PROBE:, i * NZ : (i + 1) * NZ]], axis=1)
                for i in range(2)
            ],
            axis=0,
        )
        far = from_right(sides, bh, bl)
        far_re = far[:, :NZ]
        far_im = far[:, NZ:]
        modulus = jnp.sqrt(far_re * far_re + far_im * far_im)
        intensity = measured_ref[2 * pair : 2 * pair + 2].reshape(2 * PROBE, NZ)
        shrink = 1.0 - jnp.sqrt(intensity) / jnp.maximum(modulus, 1.0)
        diff = jnp.concatenate([far_re * shrink, far_im * shrink], axis=1)
        half = from_right(diff, ah, al)
        stacked = jnp.concatenate(
            [
                jnp.concatenate([half[i * PROBE : (i + 1) * PROBE, :NZ], half[i * PROBE : (i + 1) * PROBE, NZ:]], axis=0)
                for i in range(2)
            ],
            axis=1,
        )
        backs = from_left(bh, bl, stacked)
        for i in range(2):
            back_re = backs[:PROBE, i * NZ : (i + 1) * NZ]
            back_im = backs[PROBE:, i * NZ : (i + 1) * NZ]
            rows = pl.ds(starts_ref[0, 2 * pair + i], PROBE)
            total_re[rows, :] += probe_re * back_re + probe_im * back_im
            total_im[rows, :] += probe_re * back_im - probe_im * back_re
    for ahead in range(Y):
        owner = lax.rem(y + ahead, Y)
        for tile in range(0, NR, 2):
            low = pl.ds(pl.multiple_of(tile * RAYS + owner * QR, QR), QR)
            high = pl.ds(pl.multiple_of((tile + 1) * RAYS + owner * QR, QR), QR)
            rows = slice(tile * QR, (tile + 2) * QR)
            for part, total in enumerate((total_re, total_im)):
                piece = jnp.concatenate([total[low, :], total[high, :]], axis=0)
                if ahead == 0:
                    own_ref[part, rows, :] = piece
                else:
                    sent_ref[ahead - 1, part, rows, :] = piece.astype(bf16)


def shifted(value, axis, length, step):
    return lax.ppermute(value, axis, [(i, (i + step) % length) for i in range(length)])


def across(value):
    return shifted(value, "zh", ZH, 1)


def round_y(pieces):
    return [pieces[0]] + [shifted(pieces[k], "y", Y, k) for k in range(1, Y)]


def body(measured, positions, probe_field, object_field, dual_field, volume, radon_tiles, tile_range):
    zh = lax.axis_index("zh")
    zl = lax.axis_index("zl")
    y = lax.axis_index("y")
    place = jnp.stack([zh, y]).astype(jnp.int32)
    order = (y + jnp.arange(Y)) % Y
    back_order = (y - jnp.arange(Y)) % Y
    ah, al, bh, bl = dft_blocks()
    radon = radon_tiles.reshape(ZL * XC, HITS, RAYS, TILE)
    volume_rows = volume.reshape(2 * TILE, NZ)
    object_rows = object_field.reshape(128, NZ)
    dual_rows = dual_field.reshape(128, NZ)

    with jax.named_scope("ray_sums"):
        sums = call(ray_sums, shape(NEAR, ZL, HITS * QR, 2 * NZ, dtype=bf16), 0, 2, flops=2 * 2048 * 256 * 256)(
            radon, volume_rows
        )
        near_sums = lax.all_to_all(sums, CROSS, 0, 0, tiled=True)

    with jax.named_scope("fields"):
        pair = jnp.stack([object_rows, across(object_rows)])
        fields = jnp.stack(round_y([pair] * Y))

    with jax.named_scope("targets"):
        own_targets = tile_range.reshape(ZL, XC)
        ahead = [lax.dynamic_index_in_dim(own_targets, (zl + k) % ZL, 0, keepdims=False) for k in range(ZL)]
        rounds = [ahead[0]] + [shifted(ahead[k], "zl", ZL, k) for k in range(1, ZL)]
        targets = jnp.stack(rounds)
        targets = jnp.stack(round_y([targets] * Y))
        targets = jnp.take(jnp.take(targets, back_order, axis=0), (zl - jnp.arange(ZL)) % ZL, axis=1)
        targets = targets.transpose(1, 2, 0).reshape(ZL, NEAR)

    with jax.named_scope("drift"):
        drift = (object_field + dual_field).reshape(2, Y, QR, 2, NZ)
        drift = jnp.take(drift.transpose(1, 3, 0, 2, 4).reshape(Y, 2, 2 * QR, NZ), order, axis=0)
        drift = jnp.stack(round_y([drift[k] for k in range(Y)]))
        mine = lax.dynamic_index_in_dim(drift, zh, 1, keepdims=False)
        theirs = across(lax.dynamic_index_in_dim(drift, 1 - zh, 1, keepdims=False))
        both = jnp.where(zh == 0, jnp.stack([mine, theirs]), jnp.stack([theirs, mine]))
        drift_part = jnp.take(both, back_order, axis=1).reshape(128, NZ)

    with jax.named_scope("frames"):
        inter_own, inter_others = call(
            frame_gradients,
            (shape(2, 128, NZ), shape(Y - 1, 2, 128, NZ, dtype=bf16)),
            2,
            7,
            scratch=[pltpu.VMEM((NDET, NZ), f32)] * 4 + [pltpu.VMEM((128, NZ), f32)],
            flops=1_600_000_000,
        )(place, positions, fields, probe_field, measured[0], ah, al, bh, bl)
        arrived = round_y([inter_own] + [inter_others[k] for k in range(Y - 1)])
        inter_sum = sum(piece.astype(f32) for piece in arrived)
        inter_mine = lax.dynamic_index_in_dim(inter_sum, zh, 0, keepdims=False)
        inter_sent = lax.dynamic_index_in_dim(inter_sum, 1 - zh, 0, keepdims=False)
        inter = inter_mine + across(inter_sent)

    with jax.named_scope("near_sum"):
        dense = call(
            add_tiles,
            shape(DEEP, 128, NZ, dtype=bf16),
            1,
            1,
            scratch=[pltpu.VMEM((ZL, 128, 2 * NZ), f32)],
            flops=1_000_000,
        )(targets, near_sums)
        far_sums = lax.all_to_all(dense, ALONG, 0, 0, tiled=True)

    with jax.named_scope("residual"):
        residual, kept = call(
            residual_part, (shape(128, NZ, dtype=bf16), shape(2, 128, NZ)), 0, 3, flops=1_000_000
        )(far_sums, inter, drift_part)
        copies = jnp.broadcast_to(residual, (DEEP, 128, NZ))
        residuals = lax.all_to_all(copies, ALONG, 0, 0, tiled=True)

    with jax.named_scope("pick"):
        picked = call(
            pick_tiles,
            shape(NEAR, ZL, HITS * QR, 2 * NZ, dtype=bf16),
            1,
            1,
            scratch=[pltpu.VMEM((ZL, 128, 2 * NZ), f32)],
            flops=1_000_000,
        )(targets, residuals)
        returned = lax.all_to_all(picked, CROSS, 0, 0, tiled=True)

    with jax.named_scope("updates"):
        kept = jnp.take(kept.reshape(2, ZH, Y, 2 * QR, NZ).transpose(2, 1, 0, 3, 4), order, axis=0)
        kept = jnp.stack(round_y([kept[k] for k in range(Y)]))
        mine = lax.dynamic_index_in_dim(kept, zh, 1, keepdims=False)
        theirs = across(lax.dynamic_index_in_dim(kept, 1 - zh, 1, keepdims=False))
        object_next, dual_next = call(updates, (shape(128, NZ), shape(128, NZ)), 1, 3, flops=1_000_000)(
            place, jnp.stack([mine, theirs]), object_rows, dual_rows
        )

    with jax.named_scope("back_project"):
        ordered = radon.reshape(ZL, XC, HITS, Y, QR, TILE).transpose(5, 1, 3, 0, 2, 4).reshape(TILE, -1)
        volume_next = call(back_project, shape(2 * TILE, NZ), 0, 3, flops=2 * 2048 * 256 * 256)(
            ordered, returned, volume_rows
        )
    return (
        object_next.reshape(object_field.shape),
        dual_next.reshape(dual_field.shape),
        volume_next.reshape(volume.shape),
    )


def solution(mesh):
    fine = Mesh(mesh.devices.reshape(ZL, X, C, ZH, Y), ("zl", "x", "c", "zh", "y"))
    ang = ("zl", "x", "c")
    strip = ("zh", "y")
    return jax.shard_map(
        body,
        mesh=fine,
        in_specs=(
            P(ang, strip, None, None),
            P(ang, strip),
            P(),
            P(ang, strip, None, None),
            P(ang, strip, None, None),
            P(ang + strip, None, None),
            P(ang + strip, None, None, None, None),
            P(ang, None, strip, None),
        ),
        out_specs=(
            P(ang, strip, None, None),
            P(ang, strip, None, None),
            P(ang + strip, None, None),
        ),
        check_vma=False,
    )
```

```python
import math

import jax
import jax.numpy as jnp
import numpy as np
from jax import lax
from jax.experimental import pallas as pl
from jax.experimental.pallas import tpu as pltpu
from jax.sharding import Mesh
from jax.sharding import PartitionSpec as P

PROBE = 128
NZ = 128
NDET = 512
RAYS = 32
TILE = 256
HITS = 2
NR = 16

ZL, X, C, ZH, Y = 4, 4, 2, 2, 4
XC = X * C
CROSS = ("x", "c", "y")
ALONG = ("zh", "zl")
NEAR = XC * Y
DEEP = ZH * ZL
QR = RAYS // Y
FR_DEV = 8

penalty = 1.0
object_step = 0.1
volume_step = 1.0
f32 = jnp.float32
bf16 = jnp.bfloat16

VM = pl.BlockSpec(memory_space=pltpu.VMEM)
SM = pl.BlockSpec(memory_space=pltpu.SMEM)


def call(kernel, outs, n_smem, n_vmem, scratch=(), flops=0, moved=1 << 20, limit=48 << 20):
    many = isinstance(outs, tuple)
    return pl.pallas_call(
        kernel,
        out_shape=outs,
        in_specs=[SM] * n_smem + [VM] * n_vmem,
        out_specs=tuple(VM for _ in outs) if many else VM,
        scratch_shapes=list(scratch),
        compiler_params=pltpu.CompilerParams(vmem_limit_bytes=limit),
        cost_estimate=pl.CostEstimate(flops=flops, bytes_accessed=moved, transcendentals=0),
        name=kernel.__name__,
    )


def shape(*dims, dtype=f32):
    return jax.ShapeDtypeStruct(dims, dtype)


def dft_blocks():
    k = np.arange(PROBE)
    angles = (k[:, None] * k[None, :] % PROBE) * (2.0 * math.pi / PROBE)
    cosine = np.cos(angles) / math.sqrt(PROBE)
    sine = np.sin(angles) / math.sqrt(PROBE)
    left = np.block([[cosine, sine], [-sine, cosine]]).astype(np.float32)
    high = left.astype(jnp.bfloat16)
    low = (left - high.astype(np.float32)).astype(jnp.bfloat16)
    return jnp.asarray(high), jnp.asarray(low), jnp.asarray(high.T.copy()), jnp.asarray(low.T.copy())


def ray_sums(radon_ref, volume_ref, out_ref):
    volume_half = jnp.concatenate(
        [volume_ref[pl.ds(0, TILE, stride=2), :], volume_ref[pl.ds(1, TILE, stride=2), :]], axis=1
    ).astype(bf16)
    for zl in range(ZL):
        for xc in range(XC):
            rows = radon_ref[zl * XC + xc].reshape(HITS * RAYS, TILE)
            sums = jnp.dot(rows, volume_half, preferred_element_type=f32)
            for y in range(Y):
                low = sums[y * QR : (y + 1) * QR]
                high = sums[RAYS + y * QR : RAYS + (y + 1) * QR]
                out_ref[xc * Y + y, zl] = jnp.concatenate([low, high], axis=0).astype(bf16)


def first_row(place_ref, target_ref, zl, y, xc):
    back_zl = lax.rem(place_ref[2] + ZL - zl, ZL)
    back_y = lax.rem(place_ref[1] + Y - y, Y)
    return pl.multiple_of(target_ref[back_zl, back_y * XC + xc] * QR, QR)


def add_tiles(place_ref, target_ref, sums_ref, out_ref, total):
    total[...] = jnp.zeros(total.shape, f32)

    def step(xc, carry):
        for y in range(Y):
            for zl in range(ZL):
                row = first_row(place_ref, target_ref, zl, y, xc)
                total[zl, pl.ds(row, HITS * QR), :] += sums_ref[xc * Y + y, zl].astype(f32)
        return carry

    lax.fori_loop(0, XC, step, 0)
    for zh in range(ZH):
        for zl in range(ZL):
            out_ref[zh * ZL + zl] = total[zl, :, zh * NZ : (zh + 1) * NZ].astype(bf16)


def residual_part(
    place_ref, sums_ref, inter_ref, mine_ref, theirs_ref, residual_ref, own_ref, one_ref, two_ref, three_ref, both
):
    zh = place_ref[0]
    y = place_ref[1]
    projection = sums_ref[0].astype(f32)
    for source in range(1, DEEP):
        projection = projection + sums_ref[source].astype(f32)
    inter = inter_ref[...]
    both[0] = projection
    both[1] = inter
    first = zh == 0
    drift = jnp.concatenate(
        [
            jnp.where(first, mine_ref[...], theirs_ref[...]),
            jnp.where(first, theirs_ref[...], mine_ref[...]),
        ],
        axis=0,
    )
    gap = projection - drift
    residual_ref[...] = (gap + object_step * (inter - gap)).astype(bf16)
    for ahead, ref in enumerate((own_ref, one_ref, two_ref, three_ref)):
        for other in range(ZH):
            owner = lax.rem(zh + other, ZH) * Y + lax.rem(y + ahead, Y)
            rows = pl.ds(pl.multiple_of(owner * 2 * QR, 2 * QR), 2 * QR)
            ref[other, 0] = both[0, rows, :]
            ref[other, 1] = both[1, rows, :]


def pick_tiles(place_ref, target_ref, residual_ref, out_ref, rows_ref):
    for zl in range(ZL):
        rows_ref[zl] = jnp.concatenate(
            [residual_ref[zl].astype(f32), residual_ref[ZL + zl].astype(f32)], axis=1
        )

    def step(xc, carry):
        for y in range(Y):
            for zl in range(ZL):
                row = first_row(place_ref, target_ref, zl, y, xc)
                out_ref[xc * Y + y, zl] = rows_ref[zl, pl.ds(row, HITS * QR), :].astype(bf16)
        return carry

    lax.fori_loop(0, XC, step, 0)


def back_project(radon_ref, picked_ref, volume_ref, out_ref):
    gradient = jnp.dot(
        radon_ref[...],
        picked_ref[...].reshape(NEAR * ZL * HITS * QR, 2 * NZ),
        preferred_element_type=f32,
    )
    for part in range(2):
        rows = pl.ds(part, TILE, stride=2)
        out_ref[rows, :] = volume_ref[rows, :] - volume_step * gradient[:, part * NZ : (part + 1) * NZ]


def updates(
    place_ref, own_ref, one_ref, two_ref, three_ref, theirs_ref, object_ref, dual_ref, object_out, dual_out
):
    zh = place_ref[0]
    y = place_ref[1]
    for back, ref in enumerate((own_ref, one_ref, two_ref, three_ref)):
        source = lax.rem(y + Y - back, Y)
        for other in range(ZH):
            part = lax.rem(zh + other, ZH)
            for tile in range(2):
                piece = slice(tile * QR, (tile + 1) * QR)
                projection = theirs_ref[back, 0, piece, :] if other else ref[0, 0, piece, :]
                inter = theirs_ref[back, 1, piece, :] if other else ref[0, 1, piece, :]
                rows = pl.ds((tile * RAYS + source * QR) * 2 + part, QR, stride=2)
                field = object_ref[rows, :]
                dual = dual_ref[rows, :]
                object_next = field - object_step * (inter + dual + penalty * (field - projection))
                object_out[rows, :] = object_next
                dual_out[rows, :] = dual + penalty * (object_next - projection)


def split(value):
    high = value.astype(bf16)
    return high, (value - high.astype(f32)).astype(bf16)


def from_left(high_table, low_table, value):
    high, low = split(value)
    return (
        jnp.dot(high_table, high, preferred_element_type=f32)
        + jnp.dot(high_table, low, preferred_element_type=f32)
        + jnp.dot(low_table, high, preferred_element_type=f32)
    )


def from_right(value, high_table, low_table):
    high, low = split(value)
    return (
        jnp.dot(high, high_table, preferred_element_type=f32)
        + jnp.dot(low, high_table, preferred_element_type=f32)
        + jnp.dot(high, low_table, preferred_element_type=f32)
    )


FIELD_ROWS = 4 * 64
DRIFT_ROWS = 4 * QR
SENT_ROWS = FIELD_ROWS + DRIFT_ROWS + QR


def pack(place_ref, object_ref, theirs_ref, dual_ref, target_ref, own_ref, one_ref, two_ref, three_ref, drift):
    y = place_ref[1]
    drift[...] = object_ref[...] + dual_ref[...]
    for ahead, ref in enumerate((own_ref, one_ref, two_ref, three_ref)):
        ref[0:128, :] = object_ref[...]
        ref[128:256, :] = theirs_ref[...]
        ref[FIELD_ROWS + DRIFT_ROWS :, :] = target_ref[...]
        for part in range(2):
            for tile in range(2):
                start = (tile * RAYS + lax.rem(y + ahead, Y) * QR) * 2 + part
                base = FIELD_ROWS + (part * 2 + tile) * QR
                ref[base : base + QR, :] = drift[pl.ds(start, QR, stride=2), :]


def frame_gradients(
    place_ref, starts_ref, own_field, one_field, two_field, three_field, probe_ref, measured_ref,
    ah_ref, al_ref, bh_ref, bl_ref, own_ref, sent_one, sent_two, sent_three, mine_ref, theirs_ref,
    field_re, field_im, total_re, total_im,
):
    zh = place_ref[0]
    y = place_ref[1]
    for back, field_ref in enumerate((own_field, one_field, two_field, three_field)):
        source = lax.rem(y + Y - back, Y)
        for other in range(ZH):
            owner = lax.rem(zh + other, ZH) * Y + source
            rows = pl.ds(pl.multiple_of(owner * 64, 64), 64)
            field_re[rows, :] = field_ref[pl.ds(other * 128, 64, stride=2), :]
            field_im[rows, :] = field_ref[pl.ds(other * 128 + 1, 64, stride=2), :]
        rows = pl.ds(pl.multiple_of(source * 2 * QR, 2 * QR), 2 * QR)
        mine_ref[rows, :] = field_ref[pl.ds(pl.multiple_of(FIELD_ROWS + zh * 2 * QR, 2 * QR), 2 * QR), :]
        theirs_ref[rows, :] = field_ref[pl.ds(pl.multiple_of(FIELD_ROWS + (1 - zh) * 2 * QR, 2 * QR), 2 * QR), :]
    total_re[...] = jnp.zeros(total_re.shape, f32)
    total_im[...] = jnp.zeros(total_im.shape, f32)
    probe_re = probe_ref[0]
    probe_im = probe_ref[1]
    ah, al, bh, bl = ah_ref[...], al_ref[...], bh_ref[...], bl_ref[...]
    for pair in range(FR_DEV // 2):
        waves = []
        for frame in (2 * pair, 2 * pair + 1):
            rows = pl.ds(starts_ref[0, frame], PROBE)
            object_re = field_re[rows, :]
            object_im = field_im[rows, :]
            waves.append(
                jnp.concatenate(
                    [
                        probe_re * object_re - probe_im * object_im,
                        probe_re * object_im + probe_im * object_re,
                    ],
                    axis=0,
                )
            )
        lefts = from_left(ah, al, jnp.concatenate(waves, axis=1))
        sides = jnp.concatenate(
            [
                jnp.concatenate([lefts[:PROBE, i * NZ : (i + 1) * NZ], lefts[PROBE:, i * NZ : (i + 1) * NZ]], axis=1)
                for i in range(2)
            ],
            axis=0,
        )
        far = from_right(sides, bh, bl)
        far_re = far[:, :NZ]
        far_im = far[:, NZ:]
        modulus = jnp.sqrt(far_re * far_re + far_im * far_im)
        intensity = measured_ref[2 * pair : 2 * pair + 2].reshape(2 * PROBE, NZ)
        shrink = 1.0 - jnp.sqrt(intensity) / jnp.maximum(modulus, 1.0)
        diff = jnp.concatenate([far_re * shrink, far_im * shrink], axis=1)
        half = from_right(diff, ah, al)
        stacked = jnp.concatenate(
            [
                jnp.concatenate([half[i * PROBE : (i + 1) * PROBE, :NZ], half[i * PROBE : (i + 1) * PROBE, NZ:]], axis=0)
                for i in range(2)
            ],
            axis=1,
        )
        backs = from_left(bh, bl, stacked)
        for i in range(2):
            back_re = backs[:PROBE, i * NZ : (i + 1) * NZ]
            back_im = backs[PROBE:, i * NZ : (i + 1) * NZ]
            rows = pl.ds(starts_ref[0, 2 * pair + i], PROBE)
            total_re[rows, :] += probe_re * back_re + probe_im * back_im
            total_im[rows, :] += probe_re * back_im - probe_im * back_re
    for ahead in range(Y):
        owner = lax.rem(y + ahead, Y)
        for tile in range(0, NR, 2):
            low = pl.ds(pl.multiple_of(tile * RAYS + owner * QR, QR), QR)
            high = pl.ds(pl.multiple_of((tile + 1) * RAYS + owner * QR, QR), QR)
            rows = slice(tile * QR, (tile + 2) * QR)
            for part, total in enumerate((total_re, total_im)):
                piece = jnp.concatenate([total[low, :], total[high, :]], axis=0)
                if ahead == 0:
                    own_ref[part, rows, :] = piece
                else:
                    (sent_one, sent_two, sent_three)[ahead - 1][part, rows, :] = piece.astype(bf16)


def shifted(value, axis, length, step):
    return lax.ppermute(value, axis, [(i, (i + step) % length) for i in range(length)])


def across(value):
    return shifted(value, "zh", ZH, 1)


def round_y(pieces):
    return [pieces[0]] + [shifted(pieces[k], "y", Y, k) for k in range(1, Y)]


def body(measured, positions, probe_field, object_field, dual_field, volume, radon_tiles, tile_range):
    zh = lax.axis_index("zh")
    zl = lax.axis_index("zl")
    y = lax.axis_index("y")
    place = jnp.stack([zh, y, zl]).astype(jnp.int32)
    ah, al, bh, bl = dft_blocks()
    radon = radon_tiles.reshape(ZL * XC, HITS, RAYS, TILE)
    volume_rows = volume.reshape(2 * TILE, NZ)
    object_rows = object_field.reshape(128, NZ)
    dual_rows = dual_field.reshape(128, NZ)

    with jax.named_scope("ray_sums"):
        sums = call(ray_sums, shape(NEAR, ZL, HITS * QR, 2 * NZ, dtype=bf16), 0, 2, flops=2 * 2048 * 256 * 256)(
            radon, volume_rows
        )
        near_sums = lax.all_to_all(sums, CROSS, 0, 0, tiled=True)

    with jax.named_scope("fields"):
        own_targets = jnp.zeros((QR, NZ), f32).at[0, : ZL * XC].set(tile_range.reshape(ZL * XC).astype(f32))
        packed = call(
            pack, (shape(SENT_ROWS, NZ),) * Y, 1, 4, scratch=[pltpu.VMEM((128, NZ), f32)], flops=1_000_000
        )(place, object_rows, across(object_rows), dual_rows, own_targets)
        fields = round_y(packed)

    with jax.named_scope("targets"):
        tables = jnp.stack([field[FIELD_ROWS + DRIFT_ROWS, : ZL * XC] for field in fields])
        tables = tables.reshape(Y, ZL, XC).astype(jnp.int32)
        ahead = [lax.dynamic_index_in_dim(tables, (zl + k) % ZL, 1, keepdims=False) for k in range(ZL)]
        targets = jnp.stack([ahead[0]] + [shifted(ahead[k], "zl", ZL, k) for k in range(1, ZL)])
        targets = targets.reshape(ZL, Y * XC)

    with jax.named_scope("frames"):
        *inter_parts, drift_mine, drift_sent = call(
            frame_gradients,
            (shape(2, 128, NZ),) + (shape(2, 128, NZ, dtype=bf16),) * 3 + (shape(64, NZ),) * 2,
            2,
            10,
            scratch=[pltpu.VMEM((NDET, NZ), f32)] * 4,
            flops=1_600_000_000,
        )(place, positions, *fields, probe_field, measured[0], ah, al, bh, bl)
        inter_sum = sum(piece.astype(f32) for piece in round_y(inter_parts))
        inter_mine = lax.dynamic_index_in_dim(inter_sum, zh, 0, keepdims=False)
        inter_sent = lax.dynamic_index_in_dim(inter_sum, 1 - zh, 0, keepdims=False)
        inter = inter_mine + across(inter_sent)
        drift_theirs = across(drift_sent)

    with jax.named_scope("near_sum"):
        dense = call(
            add_tiles,
            shape(DEEP, 128, NZ, dtype=bf16),
            2,
            1,
            scratch=[pltpu.VMEM((ZL, 128, 2 * NZ), f32)],
            flops=1_000_000,
        )(place, targets, near_sums)
        far_sums = lax.all_to_all(dense, ALONG, 0, 0, tiled=True)

    with jax.named_scope("residual"):
        residual, *kept = call(
            residual_part,
            (shape(128, NZ, dtype=bf16),) + (shape(ZH, 2, 2 * QR, NZ),) * Y,
            1,
            4,
            scratch=[pltpu.VMEM((2, 128, NZ), f32)],
            flops=1_000_000,
        )(place, far_sums, inter, drift_mine, drift_theirs)
        kept = round_y(kept)
        copies = jnp.broadcast_to(residual, (DEEP, 128, NZ))
        residuals = lax.all_to_all(copies, ALONG, 0, 0, tiled=True)

    with jax.named_scope("pick"):
        picked = call(
            pick_tiles,
            shape(NEAR, ZL, HITS * QR, 2 * NZ, dtype=bf16),
            2,
            1,
            scratch=[pltpu.VMEM((ZL, 128, 2 * NZ), f32)],
            flops=1_000_000,
        )(place, targets, residuals)
        picked, kept = lax.optimization_barrier((picked, kept))
        returned = lax.all_to_all(picked, CROSS, 0, 0, tiled=True)

    with jax.named_scope("updates"):
        theirs = across(jnp.stack([piece[1] for piece in kept]))
        object_next, dual_next = call(updates, (shape(128, NZ), shape(128, NZ)), 1, 7, flops=1_000_000)(
            place, *kept, theirs, object_rows, dual_rows
        )

    with jax.named_scope("back_project"):
        ordered = radon.reshape(ZL, XC, HITS, Y, QR, TILE).transpose(5, 1, 3, 0, 2, 4).reshape(TILE, -1)
        volume_next = call(back_project, shape(2 * TILE, NZ), 0, 3, flops=2 * 2048 * 256 * 256)(
            ordered, returned, volume_rows
        )
    return (
        object_next.reshape(object_field.shape),
        dual_next.reshape(dual_field.shape),
        volume_next.reshape(volume.shape),
    )


def solution(mesh):
    fine = Mesh(mesh.devices.reshape(ZL, X, C, ZH, Y), ("zl", "x", "c", "zh", "y"))
    ang = ("zl", "x", "c")
    strip = ("zh", "y")
    return jax.shard_map(
        body,
        mesh=fine,
        in_specs=(
            P(ang, strip, None, None),
            P(ang, strip),
            P(),
            P(ang, strip, None, None),
            P(ang, strip, None, None),
            P(ang + strip, None, None),
            P(ang + strip, None, None, None, None),
            P(ang, None, strip, None),
        ),
        out_specs=(
            P(ang, strip, None, None),
            P(ang, strip, None, None),
            P(ang + strip, None, None),
        ),
        check_vma=False,
    )
```

```python
import math

import jax
import jax.numpy as jnp
import numpy as np
from jax import lax
from jax.experimental import pallas as pl
from jax.experimental.pallas import tpu as pltpu
from jax.sharding import Mesh
from jax.sharding import PartitionSpec as P

PROBE = 128
NZ = 128
NDET = 512
RAYS = 32
TILE = 256
HITS = 2
NR = 16

ZL, X, C, ZH, Y = 4, 4, 2, 2, 4
XC = X * C
CROSS = ("x", "c", "y")
ALONG = ("zh", "zl")
NEAR = XC * Y
DEEP = ZH * ZL
QR = RAYS // Y
FR_DEV = 8

penalty = 1.0
object_step = 0.1
volume_step = 1.0
keep = 1.0 - object_step
share = object_step / keep
f32 = jnp.float32
bf16 = jnp.bfloat16

VM = pl.BlockSpec(memory_space=pltpu.VMEM)
SM = pl.BlockSpec(memory_space=pltpu.SMEM)


def call(kernel, outs, n_smem, n_vmem, scratch=(), flops=0, moved=1 << 20, limit=48 << 20):
    many = isinstance(outs, tuple)
    return pl.pallas_call(
        kernel,
        out_shape=outs,
        in_specs=[SM] * n_smem + [VM] * n_vmem,
        out_specs=tuple(VM for _ in outs) if many else VM,
        scratch_shapes=list(scratch),
        compiler_params=pltpu.CompilerParams(vmem_limit_bytes=limit),
        cost_estimate=pl.CostEstimate(flops=flops, bytes_accessed=moved, transcendentals=0),
        name=kernel.__name__,
    )


def shape(*dims, dtype=f32):
    return jax.ShapeDtypeStruct(dims, dtype)


def dft_blocks():
    k = np.arange(PROBE)
    angles = (k[:, None] * k[None, :] % PROBE) * (2.0 * math.pi / PROBE)
    cosine = np.cos(angles) / math.sqrt(PROBE)
    sine = np.sin(angles) / math.sqrt(PROBE)
    left = np.block([[cosine, sine], [-sine, cosine]]).astype(np.float32)
    high = left.astype(jnp.bfloat16)
    low = (left - high.astype(np.float32)).astype(jnp.bfloat16)
    return jnp.asarray(high), jnp.asarray(low), jnp.asarray(high.T.copy()), jnp.asarray(low.T.copy())


def ray_sums(radon_ref, volume_ref, out_ref):
    volume_half = jnp.concatenate(
        [volume_ref[pl.ds(0, TILE, stride=2), :], volume_ref[pl.ds(1, TILE, stride=2), :]], axis=1
    ).astype(bf16)
    for zl in range(ZL):
        for xc in range(XC):
            rows = radon_ref[zl * XC + xc].reshape(HITS * RAYS, TILE)
            sums = jnp.dot(rows, volume_half, preferred_element_type=f32)
            for y in range(Y):
                low = sums[y * QR : (y + 1) * QR]
                high = sums[RAYS + y * QR : RAYS + (y + 1) * QR]
                out_ref[xc * Y + y, zl] = jnp.concatenate([low, high], axis=0).astype(bf16)


def first_rows(place_ref, target_ref):
    back_y = [lax.rem(place_ref[1] + Y - y, Y) for y in range(Y)]
    back_zl = [lax.rem(place_ref[2] + ZL - zl, ZL) * XC for zl in range(ZL)]

    def row(zl, y, xc):
        return pl.multiple_of(target_ref[back_y[y], back_zl[zl] + xc] * QR, QR)

    return row


def add_tiles(place_ref, target_ref, sums_ref, own_ref, one_ref, two_ref, three_ref, out_ref, inter_ref, total):
    row = first_rows(place_ref, target_ref)
    total[...] = jnp.zeros(total.shape, f32)
    for part in range(2):
        inter = (own_ref[part] + one_ref[part].astype(f32)) + (two_ref[part].astype(f32) + three_ref[part].astype(f32))
        inter_ref[part] = inter
        total[place_ref[2], :, part * NZ : (part + 1) * NZ] = inter * share
    for xc in range(XC):
        for y in range(Y):
            for zl in range(ZL):
                total[zl, pl.ds(row(zl, y, xc), HITS * QR), :] += sums_ref[xc * Y + y, zl].astype(f32)
    for zh in range(ZH):
        for zl in range(ZL):
            out_ref[zh * ZL + zl] = total[zl, :, zh * NZ : (zh + 1) * NZ].astype(bf16)


def residual_part(
    place_ref, sums_ref, inter_ref, mine_ref, theirs_ref, residual_ref, own_ref, one_ref, two_ref, three_ref, joint
):
    zh = place_ref[0]
    y = place_ref[1]
    total = sums_ref[0].astype(f32)
    for source in range(1, DEEP):
        total = total + sums_ref[source].astype(f32)
    joint[...] = total
    first = zh == 0
    drift = jnp.concatenate(
        [
            jnp.where(first, mine_ref[...], theirs_ref[...]),
            jnp.where(first, theirs_ref[...], mine_ref[...]),
        ],
        axis=0,
    )
    residual = (keep * (total - drift)).astype(bf16)
    for copy in range(DEEP):
        residual_ref[copy] = residual
    for ahead, ref in enumerate((own_ref, one_ref, two_ref, three_ref)):
        for other in range(ZH):
            owner = lax.rem(zh + other, ZH) * Y + lax.rem(y + ahead, Y)
            rows = pl.ds(pl.multiple_of(owner * 2 * QR, 2 * QR), 2 * QR)
            ref[other, 0] = joint[rows, :]
            for part in range(2):
                ref[other, 1 + part] = inter_ref[part, rows, :]


def pick_tiles(place_ref, target_ref, residual_ref, out_ref, rows_ref):
    for zl in range(ZL):
        rows_ref[zl] = jnp.concatenate(
            [residual_ref[zl].astype(f32), residual_ref[ZL + zl].astype(f32)], axis=1
        )

    row = first_rows(place_ref, target_ref)
    for xc in range(XC):
        for y in range(Y):
            for zl in range(ZL):
                out_ref[xc * Y + y, zl] = rows_ref[zl, pl.ds(row(zl, y, xc), HITS * QR), :].astype(bf16)


def back_project(radon_ref, picked_ref, volume_ref, out_ref):
    gradient = jnp.dot(
        radon_ref[...],
        picked_ref[...].reshape(NEAR * ZL * HITS * QR, 2 * NZ),
        preferred_element_type=f32,
    )
    for part in range(2):
        rows = pl.ds(part, TILE, stride=2)
        out_ref[rows, :] = volume_ref[rows, :] - volume_step * gradient[:, part * NZ : (part + 1) * NZ]


def updates(
    place_ref, own_ref, one_ref, two_ref, three_ref, theirs_ref, object_ref, dual_ref, object_out, dual_out
):
    zh = place_ref[0]
    y = place_ref[1]
    for back, ref in enumerate((own_ref, one_ref, two_ref, three_ref)):
        source = lax.rem(y + Y - back, Y)
        for other in range(ZH):
            part = lax.rem(zh + other, ZH)
            for tile in range(2):
                piece = slice(tile * QR, (tile + 1) * QR)
                inter = ref[0, 1 + part, piece, :] + theirs_ref[back, 1 + part, piece, :]
                joint = theirs_ref[back, 0, piece, :] if other else ref[0, 0, piece, :]
                projection = joint - share * inter
                rows = pl.ds((tile * RAYS + source * QR) * 2 + part, QR, stride=2)
                field = object_ref[rows, :]
                dual = dual_ref[rows, :]
                object_next = field - object_step * (inter + dual + penalty * (field - projection))
                object_out[rows, :] = object_next
                dual_out[rows, :] = dual + penalty * (object_next - projection)


def split(value):
    high = value.astype(bf16)
    return high, (value - high.astype(f32)).astype(bf16)


def from_left(high_table, low_table, value):
    high, low = split(value)
    return (
        jnp.dot(high_table, high, preferred_element_type=f32)
        + jnp.dot(high_table, low, preferred_element_type=f32)
        + jnp.dot(low_table, high, preferred_element_type=f32)
    )


def from_right(value, high_table, low_table):
    high, low = split(value)
    return (
        jnp.dot(high, high_table, preferred_element_type=f32)
        + jnp.dot(low, high_table, preferred_element_type=f32)
        + jnp.dot(high, low_table, preferred_element_type=f32)
    )


FIELD_ROWS = 4 * 64
DRIFT_ROWS = 4 * QR
SENT_ROWS = FIELD_ROWS + DRIFT_ROWS + QR


def pack(place_ref, object_ref, theirs_ref, dual_ref, target_ref, own_ref, one_ref, two_ref, three_ref, drift):
    y = place_ref[1]
    drift[...] = object_ref[...] + dual_ref[...]
    for ahead, ref in enumerate((own_ref, one_ref, two_ref, three_ref)):
        ref[0:128, :] = object_ref[...]
        ref[128:256, :] = theirs_ref[...]
        ref[FIELD_ROWS + DRIFT_ROWS :, :] = target_ref[...]
        for part in range(2):
            for tile in range(2):
                start = (tile * RAYS + lax.rem(y + ahead, Y) * QR) * 2 + part
                base = FIELD_ROWS + (part * 2 + tile) * QR
                ref[base : base + QR, :] = drift[pl.ds(start, QR, stride=2), :]


def frame_gradients(
    place_ref, starts_ref, own_field, one_field, two_field, three_field, probe_ref, measured_ref,
    ah_ref, al_ref, bh_ref, bl_ref, own_ref, sent_one, sent_two, sent_three, mine_ref, theirs_ref,
    field_re, field_im, total_re, total_im,
):
    zh = place_ref[0]
    y = place_ref[1]
    for back, field_ref in enumerate((own_field, one_field, two_field, three_field)):
        source = lax.rem(y + Y - back, Y)
        for other in range(ZH):
            owner = lax.rem(zh + other, ZH) * Y + source
            rows = pl.ds(pl.multiple_of(owner * 64, 64), 64)
            field_re[rows, :] = field_ref[pl.ds(other * 128, 64, stride=2), :]
            field_im[rows, :] = field_ref[pl.ds(other * 128 + 1, 64, stride=2), :]
        rows = pl.ds(pl.multiple_of(source * 2 * QR, 2 * QR), 2 * QR)
        mine_ref[rows, :] = field_ref[pl.ds(pl.multiple_of(FIELD_ROWS + zh * 2 * QR, 2 * QR), 2 * QR), :]
        theirs_ref[rows, :] = field_ref[pl.ds(pl.multiple_of(FIELD_ROWS + (1 - zh) * 2 * QR, 2 * QR), 2 * QR), :]
    total_re[...] = jnp.zeros(total_re.shape, f32)
    total_im[...] = jnp.zeros(total_im.shape, f32)
    probe_re = probe_ref[0]
    probe_im = probe_ref[1]
    ah, al, bh, bl = ah_ref[...], al_ref[...], bh_ref[...], bl_ref[...]
    for pair in range(FR_DEV // 2):
        waves = []
        for frame in (2 * pair, 2 * pair + 1):
            rows = pl.ds(starts_ref[0, frame], PROBE)
            object_re = field_re[rows, :]
            object_im = field_im[rows, :]
            waves.append(
                jnp.concatenate(
                    [
                        probe_re * object_re - probe_im * object_im,
                        probe_re * object_im + probe_im * object_re,
                    ],
                    axis=0,
                )
            )
        lefts = from_left(ah, al, jnp.concatenate(waves, axis=1))
        sides = jnp.concatenate(
            [
                jnp.concatenate([lefts[:PROBE, i * NZ : (i + 1) * NZ], lefts[PROBE:, i * NZ : (i + 1) * NZ]], axis=1)
                for i in range(2)
            ],
            axis=0,
        )
        far = from_right(sides, bh, bl)
        far_re = far[:, :NZ]
        far_im = far[:, NZ:]
        modulus = jnp.sqrt(far_re * far_re + far_im * far_im)
        intensity = measured_ref[2 * pair : 2 * pair + 2].reshape(2 * PROBE, NZ)
        shrink = 1.0 - jnp.sqrt(intensity) / jnp.maximum(modulus, 1.0)
        diff = jnp.concatenate([far_re * shrink, far_im * shrink], axis=1)
        half = from_right(diff, ah, al)
        stacked = jnp.concatenate(
            [
                jnp.concatenate([half[i * PROBE : (i + 1) * PROBE, :NZ], half[i * PROBE : (i + 1) * PROBE, NZ:]], axis=0)
                for i in range(2)
            ],
            axis=1,
        )
        backs = from_left(bh, bl, stacked)
        for i in range(2):
            back_re = backs[:PROBE, i * NZ : (i + 1) * NZ]
            back_im = backs[PROBE:, i * NZ : (i + 1) * NZ]
            rows = pl.ds(starts_ref[0, 2 * pair + i], PROBE)
            total_re[rows, :] += probe_re * back_re + probe_im * back_im
            total_im[rows, :] += probe_re * back_im - probe_im * back_re
    for ahead in range(Y):
        owner = lax.rem(y + ahead, Y)
        for tile in range(0, NR, 2):
            low = pl.ds(pl.multiple_of(tile * RAYS + owner * QR, QR), QR)
            high = pl.ds(pl.multiple_of((tile + 1) * RAYS + owner * QR, QR), QR)
            rows = slice(tile * QR, (tile + 2) * QR)
            for part, total in enumerate((total_re, total_im)):
                piece = jnp.concatenate([total[low, :], total[high, :]], axis=0)
                if ahead == 0:
                    own_ref[part, rows, :] = piece
                else:
                    (sent_one, sent_two, sent_three)[ahead - 1][part, rows, :] = piece.astype(bf16)


def shifted(value, axis, length, step):
    return lax.ppermute(value, axis, [(i, (i + step) % length) for i in range(length)])


def across(value):
    return shifted(value, "zh", ZH, 1)


def round_y(pieces):
    return [pieces[0]] + [shifted(pieces[k], "y", Y, k) for k in range(1, Y)]


def body(measured, positions, probe_field, object_field, dual_field, volume, radon_tiles, tile_range):
    zh = lax.axis_index("zh")
    zl = lax.axis_index("zl")
    y = lax.axis_index("y")
    place = jnp.stack([zh, y, zl]).astype(jnp.int32)
    ah, al, bh, bl = dft_blocks()
    radon = radon_tiles.reshape(ZL * XC, HITS, RAYS, TILE)
    volume_rows = volume.reshape(2 * TILE, NZ)
    object_rows = object_field.reshape(128, NZ)
    dual_rows = dual_field.reshape(128, NZ)

    with jax.named_scope("targets"):
        own_targets = tile_range.reshape(ZL, XC)
        ahead = [lax.dynamic_index_in_dim(own_targets, (zl + k) % ZL, 0, keepdims=False) for k in range(ZL)]
        targets = jnp.stack([ahead[0]] + [shifted(ahead[k], "zl", ZL, k) for k in range(1, ZL)])
        target_rows = jnp.zeros((QR, NZ), f32).at[0, : ZL * XC].set(targets.reshape(ZL * XC).astype(f32))

    with jax.named_scope("fields"):
        object_theirs = across(object_rows)

    with jax.named_scope("ray_sums"):
        radon_first, target_rows = lax.optimization_barrier((radon, target_rows))
        sums = call(ray_sums, shape(NEAR, ZL, HITS * QR, 2 * NZ, dtype=bf16), 0, 2, flops=2 * 2048 * 256 * 256)(
            radon_first, volume_rows
        )

    with jax.named_scope("fields"):
        packed = call(
            pack, (shape(SENT_ROWS, NZ),) * Y, 1, 4, scratch=[pltpu.VMEM((128, NZ), f32)], flops=1_000_000
        )(place, object_rows, object_theirs, dual_rows, target_rows)
        sums, packed = lax.optimization_barrier((sums, packed))
        fields = round_y(packed)

    with jax.named_scope("ray_sums"):
        near_sums = lax.all_to_all(sums, CROSS, 0, 0, tiled=True)

    with jax.named_scope("targets"):
        tables = jnp.stack([field[FIELD_ROWS + DRIFT_ROWS, : ZL * XC] for field in fields]).astype(jnp.int32)

    with jax.named_scope("frames"):
        *inter_parts, drift_mine, drift_sent = call(
            frame_gradients,
            (shape(2, 128, NZ),) + (shape(2, 128, NZ, dtype=bf16),) * 3 + (shape(64, NZ),) * 2,
            2,
            10,
            scratch=[pltpu.VMEM((NDET, NZ), f32)] * 4,
            flops=1_600_000_000,
        )(place, positions, *fields, probe_field, measured[0], ah, al, bh, bl)
        inter_parts = round_y(inter_parts)
        drift_theirs = across(drift_sent)

    with jax.named_scope("near_sum"):
        dense, inter = call(
            add_tiles,
            (shape(DEEP, 128, NZ, dtype=bf16), shape(2, 128, NZ)),
            2,
            5,
            scratch=[pltpu.VMEM((ZL, 128, 2 * NZ), f32)],
            flops=1_000_000,
        )(place, tables, near_sums, *inter_parts)
        dense, drift_theirs = lax.optimization_barrier((dense, drift_theirs))
        far_sums = lax.all_to_all(dense, ALONG, 0, 0, tiled=True)

    with jax.named_scope("residual"):
        copies, *kept = call(
            residual_part,
            (shape(DEEP, 128, NZ, dtype=bf16),) + (shape(ZH, 3, 2 * QR, NZ),) * Y,
            1,
            4,
            scratch=[pltpu.VMEM((128, NZ), f32)],
            flops=1_000_000,
        )(place, far_sums, inter, drift_mine, drift_theirs)
        kept = round_y(kept)
        residuals = lax.all_to_all(copies, ALONG, 0, 0, tiled=True)

    with jax.named_scope("pick"):
        picked = call(
            pick_tiles,
            shape(NEAR, ZL, HITS * QR, 2 * NZ, dtype=bf16),
            2,
            1,
            scratch=[pltpu.VMEM((ZL, 128, 2 * NZ), f32)],
            flops=1_000_000,
        )(place, tables, residuals)
        picked, kept = lax.optimization_barrier((picked, kept))
        returned = lax.all_to_all(picked, CROSS, 0, 0, tiled=True)

    with jax.named_scope("updates"):
        theirs = across(jnp.stack([piece[1] for piece in kept]))
        object_next, dual_next = call(updates, (shape(128, NZ), shape(128, NZ)), 1, 7, flops=1_000_000)(
            place, *kept, theirs, object_rows, dual_rows
        )

    with jax.named_scope("back_project"):
        ordered = radon.reshape(ZL, XC, HITS, Y, QR, TILE).transpose(5, 1, 3, 0, 2, 4).reshape(TILE, -1)
        volume_next = call(back_project, shape(2 * TILE, NZ), 0, 3, flops=2 * 2048 * 256 * 256)(
            ordered, returned, volume_rows
        )
    return (
        object_next.reshape(object_field.shape),
        dual_next.reshape(dual_field.shape),
        volume_next.reshape(volume.shape),
    )


def solution(mesh):
    fine = Mesh(mesh.devices.reshape(ZL, X, C, ZH, Y), ("zl", "x", "c", "zh", "y"))
    ang = ("zl", "x", "c")
    strip = ("zh", "y")
    return jax.shard_map(
        body,
        mesh=fine,
        in_specs=(
            P(ang, strip, None, None),
            P(ang, strip),
            P(),
            P(ang, strip, None, None),
            P(ang, strip, None, None),
            P(ang + strip, None, None),
            P(ang + strip, None, None, None, None),
            P(ang, None, strip, None),
        ),
        out_specs=(
            P(ang, strip, None, None),
            P(ang, strip, None, None),
            P(ang + strip, None, None),
        ),
        check_vma=False,
    )
```

```python
import math

import jax
import jax.numpy as jnp
import numpy as np
from jax import lax
from jax.experimental import pallas as pl
from jax.experimental.pallas import tpu as pltpu
from jax.sharding import Mesh
from jax.sharding import PartitionSpec as P

PROBE = 128
NZ = 128
NDET = 512
RAYS = 32
TILE = 256
HITS = 2
NR = 16

ZL, X, C, ZH, Y = 4, 4, 2, 2, 4
XC = X * C
CROSS = ("x", "c", "y")
ALONG = ("zh", "zl")
NEAR = XC * Y
DEEP = ZH * ZL
QR = RAYS // Y
FR_DEV = 8

penalty = 1.0
object_step = 0.1
volume_step = 1.0
keep = 1.0 - object_step
share = object_step / keep
f32 = jnp.float32
bf16 = jnp.bfloat16

VM = pl.BlockSpec(memory_space=pltpu.VMEM)
SM = pl.BlockSpec(memory_space=pltpu.SMEM)


def call(kernel, outs, n_smem, n_vmem, scratch=(), flops=0, moved=1 << 20, limit=48 << 20):
    many = isinstance(outs, tuple)
    return pl.pallas_call(
        kernel,
        out_shape=outs,
        in_specs=[SM] * n_smem + [VM] * n_vmem,
        out_specs=tuple(VM for _ in outs) if many else VM,
        scratch_shapes=list(scratch),
        compiler_params=pltpu.CompilerParams(vmem_limit_bytes=limit),
        cost_estimate=pl.CostEstimate(flops=flops, bytes_accessed=moved, transcendentals=0),
        name=kernel.__name__,
    )


def shape(*dims, dtype=f32):
    return jax.ShapeDtypeStruct(dims, dtype)


def dft_blocks():
    k = np.arange(PROBE)
    angles = (k[:, None] * k[None, :] % PROBE) * (2.0 * math.pi / PROBE)
    cosine = np.cos(angles) / math.sqrt(PROBE)
    sine = np.sin(angles) / math.sqrt(PROBE)
    left = np.block([[cosine, sine], [-sine, cosine]]).astype(np.float32)
    high = left.astype(jnp.bfloat16)
    low = (left - high.astype(np.float32)).astype(jnp.bfloat16)
    return jnp.asarray(high), jnp.asarray(low), jnp.asarray(high.T.copy()), jnp.asarray(low.T.copy())


def ray_sums(radon_ref, volume_ref, out_ref):
    volume_half = jnp.concatenate(
        [volume_ref[pl.ds(0, TILE, stride=2), :], volume_ref[pl.ds(1, TILE, stride=2), :]], axis=1
    ).astype(bf16)
    for zl in range(ZL):
        for xc in range(XC):
            rows = radon_ref[zl * XC + xc].reshape(HITS * RAYS, TILE)
            sums = jnp.dot(rows, volume_half, preferred_element_type=f32)
            for y in range(Y):
                low = sums[y * QR : (y + 1) * QR]
                high = sums[RAYS + y * QR : RAYS + (y + 1) * QR]
                out_ref[xc * Y + y, zl] = jnp.concatenate([low, high], axis=0).astype(bf16)


def first_rows(place_ref, target_ref):
    back_y = [lax.rem(place_ref[1] + Y - y, Y) * XC for y in range(Y)]
    back_zl = [lax.rem(place_ref[2] + ZL - zl, ZL) for zl in range(ZL)]

    def row(zl, y, xc):
        return pl.multiple_of(target_ref[back_zl[zl], back_y[y] + xc] * QR, QR)

    return row


def add_tiles(place_ref, target_ref, sums_ref, own_ref, one_ref, two_ref, three_ref, out_ref, inter_ref, total):
    row = first_rows(place_ref, target_ref)
    total[...] = jnp.zeros(total.shape, f32)
    for part in range(2):
        inter = (own_ref[part] + one_ref[part].astype(f32)) + (two_ref[part].astype(f32) + three_ref[part].astype(f32))
        inter_ref[part] = inter
        total[place_ref[2], :, part * NZ : (part + 1) * NZ] = inter * share
    for xc in range(XC):
        for y in range(Y):
            for zl in range(ZL):
                total[zl, pl.ds(row(zl, y, xc), HITS * QR), :] += sums_ref[xc * Y + y, zl].astype(f32)
    for zh in range(ZH):
        for zl in range(ZL):
            out_ref[zh * ZL + zl] = total[zl, :, zh * NZ : (zh + 1) * NZ].astype(bf16)


def residual_part(
    place_ref, sums_ref, inter_ref, mine_ref, theirs_ref, residual_ref, own_ref, one_ref, two_ref, three_ref, joint
):
    zh = place_ref[0]
    y = place_ref[1]
    total = sums_ref[0].astype(f32)
    for source in range(1, DEEP):
        total = total + sums_ref[source].astype(f32)
    joint[...] = total
    first = zh == 0
    drift = jnp.concatenate(
        [
            jnp.where(first, mine_ref[...], theirs_ref[...]),
            jnp.where(first, theirs_ref[...], mine_ref[...]),
        ],
        axis=0,
    )
    residual = (keep * (total - drift)).astype(bf16)
    for copy in range(DEEP):
        residual_ref[copy] = residual
    for ahead, ref in enumerate((own_ref, one_ref, two_ref, three_ref)):
        for other in range(ZH):
            owner = lax.rem(zh + other, ZH) * Y + lax.rem(y + ahead, Y)
            rows = pl.ds(pl.multiple_of(owner * 2 * QR, 2 * QR), 2 * QR)
            ref[other, 0] = joint[rows, :]
            for part in range(2):
                ref[other, 1 + part] = inter_ref[part, rows, :]


def pick_tiles(place_ref, target_ref, residual_ref, out_ref, rows_ref):
    for zl in range(ZL):
        rows_ref[zl] = jnp.concatenate(
            [residual_ref[zl].astype(f32), residual_ref[ZL + zl].astype(f32)], axis=1
        )

    row = first_rows(place_ref, target_ref)
    for xc in range(XC):
        for y in range(Y):
            for zl in range(ZL):
                out_ref[xc * Y + y, zl] = rows_ref[zl, pl.ds(row(zl, y, xc), HITS * QR), :].astype(bf16)


def back_project(radon_ref, picked_ref, volume_ref, out_ref):
    gradient = jnp.dot(
        radon_ref[...],
        picked_ref[...].reshape(NEAR * ZL * HITS * QR, 2 * NZ),
        preferred_element_type=f32,
    )
    for part in range(2):
        rows = pl.ds(part, TILE, stride=2)
        out_ref[rows, :] = volume_ref[rows, :] - volume_step * gradient[:, part * NZ : (part + 1) * NZ]


def updates(
    place_ref, own_ref, one_ref, two_ref, three_ref, theirs_ref, object_ref, dual_ref, object_out, dual_out
):
    zh = place_ref[0]
    y = place_ref[1]
    for back, ref in enumerate((own_ref, one_ref, two_ref, three_ref)):
        source = lax.rem(y + Y - back, Y)
        for other in range(ZH):
            part = lax.rem(zh + other, ZH)
            for tile in range(2):
                piece = slice(tile * QR, (tile + 1) * QR)
                inter = ref[0, 1 + part, piece, :] + theirs_ref[back, 1 + part, piece, :]
                joint = theirs_ref[back, 0, piece, :] if other else ref[0, 0, piece, :]
                projection = joint - share * inter
                rows = pl.ds((tile * RAYS + source * QR) * 2 + part, QR, stride=2)
                field = object_ref[rows, :]
                dual = dual_ref[rows, :]
                object_next = field - object_step * (inter + dual + penalty * (field - projection))
                object_out[rows, :] = object_next
                dual_out[rows, :] = dual + penalty * (object_next - projection)


def split(value):
    high = value.astype(bf16)
    return high, (value - high.astype(f32)).astype(bf16)


def from_left(high_table, low_table, value):
    high, low = split(value)
    return (
        jnp.dot(high_table, high, preferred_element_type=f32)
        + jnp.dot(high_table, low, preferred_element_type=f32)
        + jnp.dot(low_table, high, preferred_element_type=f32)
    )


def from_right(value, high_table, low_table):
    high, low = split(value)
    return (
        jnp.dot(high, high_table, preferred_element_type=f32)
        + jnp.dot(low, high_table, preferred_element_type=f32)
        + jnp.dot(high, low_table, preferred_element_type=f32)
    )


FIELD_ROWS = 4 * 64
DRIFT_ROWS = 4 * QR
SENT_ROWS = FIELD_ROWS + DRIFT_ROWS + QR


def pack(place_ref, object_ref, theirs_ref, dual_ref, target_ref, own_ref, one_ref, two_ref, three_ref, drift):
    y = place_ref[1]
    targets = target_ref[...].astype(f32)
    drift[...] = object_ref[...] + dual_ref[...]
    for ahead, ref in enumerate((own_ref, one_ref, two_ref, three_ref)):
        ref[0:128, :] = object_ref[...]
        ref[128:256, :] = theirs_ref[...]
        ref[FIELD_ROWS + DRIFT_ROWS :, :] = jnp.zeros((QR, NZ), f32)
        ref[FIELD_ROWS + DRIFT_ROWS : FIELD_ROWS + DRIFT_ROWS + 1, : ZL * XC] = targets
        for part in range(2):
            for tile in range(2):
                start = (tile * RAYS + lax.rem(y + ahead, Y) * QR) * 2 + part
                base = FIELD_ROWS + (part * 2 + tile) * QR
                ref[base : base + QR, :] = drift[pl.ds(start, QR, stride=2), :]


def frame_gradients(
    place_ref, starts_ref, own_field, one_field, two_field, three_field, probe_ref, measured_ref,
    ah_ref, al_ref, bh_ref, bl_ref, own_ref, sent_one, sent_two, sent_three, mine_ref, theirs_ref,
    field_re, field_im, total_re, total_im,
):
    zh = place_ref[0]
    y = place_ref[1]
    for back, field_ref in enumerate((own_field, one_field, two_field, three_field)):
        source = lax.rem(y + Y - back, Y)
        for other in range(ZH):
            owner = lax.rem(zh + other, ZH) * Y + source
            rows = pl.ds(pl.multiple_of(owner * 64, 64), 64)
            field_re[rows, :] = field_ref[pl.ds(other * 128, 64, stride=2), :]
            field_im[rows, :] = field_ref[pl.ds(other * 128 + 1, 64, stride=2), :]
        rows = pl.ds(pl.multiple_of(source * 2 * QR, 2 * QR), 2 * QR)
        mine_ref[rows, :] = field_ref[pl.ds(pl.multiple_of(FIELD_ROWS + zh * 2 * QR, 2 * QR), 2 * QR), :]
        theirs_ref[rows, :] = field_ref[pl.ds(pl.multiple_of(FIELD_ROWS + (1 - zh) * 2 * QR, 2 * QR), 2 * QR), :]
    total_re[...] = jnp.zeros(total_re.shape, f32)
    total_im[...] = jnp.zeros(total_im.shape, f32)
    probe_re = probe_ref[0]
    probe_im = probe_ref[1]
    ah, al, bh, bl = ah_ref[...], al_ref[...], bh_ref[...], bl_ref[...]
    for pair in range(FR_DEV // 2):
        waves = []
        for frame in (2 * pair, 2 * pair + 1):
            rows = pl.ds(starts_ref[0, frame], PROBE)
            object_re = field_re[rows, :]
            object_im = field_im[rows, :]
            waves.append(
                jnp.concatenate(
                    [
                        probe_re * object_re - probe_im * object_im,
                        probe_re * object_im + probe_im * object_re,
                    ],
                    axis=0,
                )
            )
        lefts = from_left(ah, al, jnp.concatenate(waves, axis=1))
        sides = jnp.concatenate(
            [
                jnp.concatenate([lefts[:PROBE, i * NZ : (i + 1) * NZ], lefts[PROBE:, i * NZ : (i + 1) * NZ]], axis=1)
                for i in range(2)
            ],
            axis=0,
        )
        far = from_right(sides, bh, bl)
        far_re = far[:, :NZ]
        far_im = far[:, NZ:]
        modulus = jnp.sqrt(far_re * far_re + far_im * far_im)
        intensity = measured_ref[2 * pair : 2 * pair + 2].reshape(2 * PROBE, NZ)
        shrink = 1.0 - jnp.sqrt(intensity) / jnp.maximum(modulus, 1.0)
        diff = jnp.concatenate([far_re * shrink, far_im * shrink], axis=1)
        half = from_right(diff, ah, al)
        stacked = jnp.concatenate(
            [
                jnp.concatenate([half[i * PROBE : (i + 1) * PROBE, :NZ], half[i * PROBE : (i + 1) * PROBE, NZ:]], axis=0)
                for i in range(2)
            ],
            axis=1,
        )
        backs = from_left(bh, bl, stacked)
        for i in range(2):
            back_re = backs[:PROBE, i * NZ : (i + 1) * NZ]
            back_im = backs[PROBE:, i * NZ : (i + 1) * NZ]
            rows = pl.ds(starts_ref[0, 2 * pair + i], PROBE)
            total_re[rows, :] += probe_re * back_re + probe_im * back_im
            total_im[rows, :] += probe_re * back_im - probe_im * back_re
    for ahead in range(Y):
        owner = lax.rem(y + ahead, Y)
        for tile in range(0, NR, 2):
            low = pl.ds(pl.multiple_of(tile * RAYS + owner * QR, QR), QR)
            high = pl.ds(pl.multiple_of((tile + 1) * RAYS + owner * QR, QR), QR)
            rows = slice(tile * QR, (tile + 2) * QR)
            for part, total in enumerate((total_re, total_im)):
                piece = jnp.concatenate([total[low, :], total[high, :]], axis=0)
                if ahead == 0:
                    own_ref[part, rows, :] = piece
                else:
                    (sent_one, sent_two, sent_three)[ahead - 1][part, rows, :] = piece.astype(bf16)


def shifted(value, axis, length, step):
    return lax.ppermute(value, axis, [(i, (i + step) % length) for i in range(length)])


def across(value):
    return shifted(value, "zh", ZH, 1)


def round_y(pieces):
    return [pieces[0]] + [shifted(pieces[k], "y", Y, k) for k in range(1, Y)]


def body(measured, positions, probe_field, object_field, dual_field, volume, radon_tiles, tile_range):
    zh = lax.axis_index("zh")
    zl = lax.axis_index("zl")
    y = lax.axis_index("y")
    place = jnp.stack([zh, y, zl]).astype(jnp.int32)
    ah, al, bh, bl = dft_blocks()
    radon = radon_tiles.reshape(ZL * XC, HITS, RAYS, TILE)
    volume_rows = volume.reshape(2 * TILE, NZ)
    object_rows = object_field.reshape(128, NZ)
    dual_rows = dual_field.reshape(128, NZ)

    with jax.named_scope("fields"):
        packed = call(
            pack, (shape(SENT_ROWS, NZ),) * Y, 1, 4, scratch=[pltpu.VMEM((128, NZ), f32)], flops=1_000_000
        )(place, object_rows, across(object_rows), dual_rows, tile_range.reshape(1, ZL * XC))
        fields = round_y(packed)

    with jax.named_scope("ray_sums"):
        sums = call(ray_sums, shape(NEAR, ZL, HITS * QR, 2 * NZ, dtype=bf16), 0, 2, flops=2 * 2048 * 256 * 256)(
            radon, volume_rows
        )
        sums, fields = lax.optimization_barrier((sums, fields))
        near_sums = lax.all_to_all(sums, CROSS, 0, 0, tiled=True)

    with jax.named_scope("frames"):
        *inter_parts, drift_mine, drift_sent = call(
            frame_gradients,
            (shape(2, 128, NZ),) + (shape(2, 128, NZ, dtype=bf16),) * 3 + (shape(64, NZ),) * 2,
            2,
            10,
            scratch=[pltpu.VMEM((NDET, NZ), f32)] * 4,
            flops=1_600_000_000,
        )(place, positions, *fields, probe_field, measured[0], ah, al, bh, bl)
        inter_parts = round_y(inter_parts)

    with jax.named_scope("targets"):
        tables = jnp.stack([field[FIELD_ROWS + DRIFT_ROWS, : ZL * XC] for field in fields])
        tables, inter_parts[1] = lax.optimization_barrier((tables, inter_parts[1]))
        tables = tables.astype(jnp.int32).reshape(Y, ZL, XC)
        ahead = [lax.dynamic_index_in_dim(tables, (zl + k) % ZL, 1, keepdims=False) for k in range(ZL)]
        tables = jnp.stack([ahead[0]] + [shifted(ahead[k], "zl", ZL, k) for k in range(1, ZL)])
        tables = tables.reshape(ZL, Y * XC)
        drift_theirs = across(drift_sent)

    with jax.named_scope("near_sum"):
        dense, inter = call(
            add_tiles,
            (shape(DEEP, 128, NZ, dtype=bf16), shape(2, 128, NZ)),
            2,
            5,
            scratch=[pltpu.VMEM((ZL, 128, 2 * NZ), f32)],
            flops=1_000_000,
        )(place, tables, near_sums, *inter_parts)
        dense, drift_theirs = lax.optimization_barrier((dense, drift_theirs))
        far_sums = lax.all_to_all(dense, ALONG, 0, 0, tiled=True)

    with jax.named_scope("residual"):
        copies, *kept = call(
            residual_part,
            (shape(DEEP, 128, NZ, dtype=bf16),) + (shape(ZH, 3, 2 * QR, NZ),) * Y,
            1,
            4,
            scratch=[pltpu.VMEM((128, NZ), f32)],
            flops=1_000_000,
        )(place, far_sums, inter, drift_mine, drift_theirs)
        kept = round_y(kept)
        residuals = lax.all_to_all(copies, ALONG, 0, 0, tiled=True)

    with jax.named_scope("pick"):
        picked = call(
            pick_tiles,
            shape(NEAR, ZL, HITS * QR, 2 * NZ, dtype=bf16),
            2,
            1,
            scratch=[pltpu.VMEM((ZL, 128, 2 * NZ), f32)],
            flops=1_000_000,
        )(place, tables, residuals)
        picked, kept = lax.optimization_barrier((picked, kept))
        returned = lax.all_to_all(picked, CROSS, 0, 0, tiled=True)

    with jax.named_scope("updates"):
        theirs = across(jnp.stack([piece[1] for piece in kept]))
        object_next, dual_next = call(updates, (shape(128, NZ), shape(128, NZ)), 1, 7, flops=1_000_000)(
            place, *kept, theirs, object_rows, dual_rows
        )

    with jax.named_scope("back_project"):
        ordered = radon.reshape(ZL, XC, HITS, Y, QR, TILE).transpose(5, 1, 3, 0, 2, 4).reshape(TILE, -1)
        volume_next = call(back_project, shape(2 * TILE, NZ), 0, 3, flops=2 * 2048 * 256 * 256)(
            ordered, returned, volume_rows
        )
    return (
        object_next.reshape(object_field.shape),
        dual_next.reshape(dual_field.shape),
        volume_next.reshape(volume.shape),
    )


def solution(mesh):
    fine = Mesh(mesh.devices.reshape(ZL, X, C, ZH, Y), ("zl", "x", "c", "zh", "y"))
    ang = ("zl", "x", "c")
    strip = ("zh", "y")
    return jax.shard_map(
        body,
        mesh=fine,
        in_specs=(
            P(ang, strip, None, None),
            P(ang, strip),
            P(),
            P(ang, strip, None, None),
            P(ang, strip, None, None),
            P(ang + strip, None, None),
            P(ang + strip, None, None, None, None),
            P(ang, None, strip, None),
        ),
        out_specs=(
            P(ang, strip, None, None),
            P(ang, strip, None, None),
            P(ang + strip, None, None),
        ),
        check_vma=False,
    )
```

```python
import math

import jax
import jax.numpy as jnp
import numpy as np
from jax import lax
from jax.experimental import pallas as pl
from jax.experimental.pallas import tpu as pltpu
from jax.sharding import Mesh
from jax.sharding import PartitionSpec as P

PROBE = 128
NZ = 128
NDET = 512
RAYS = 32
TILE = 256
HITS = 2
NR = 16

ZL, X, C, ZH, Y = 4, 4, 2, 2, 4
XC = X * C
CROSS = ("x", "c", "y")
ALONG = ("zh", "zl")
NEAR = XC * Y
DEEP = ZH * ZL
QR = RAYS // Y
FR_DEV = 8

penalty = 1.0
object_step = 0.1
volume_step = 1.0
keep = 1.0 - object_step
share = object_step / keep
f32 = jnp.float32
bf16 = jnp.bfloat16

VM = pl.BlockSpec(memory_space=pltpu.VMEM)
SM = pl.BlockSpec(memory_space=pltpu.SMEM)


def call(kernel, outs, n_smem, n_vmem, scratch=(), flops=0, moved=1 << 20, limit=48 << 20):
    many = isinstance(outs, tuple)
    return pl.pallas_call(
        kernel,
        out_shape=outs,
        in_specs=[SM] * n_smem + [VM] * n_vmem,
        out_specs=tuple(VM for _ in outs) if many else VM,
        scratch_shapes=list(scratch),
        compiler_params=pltpu.CompilerParams(vmem_limit_bytes=limit),
        cost_estimate=pl.CostEstimate(flops=flops, bytes_accessed=moved, transcendentals=0),
        name=kernel.__name__,
    )


def shape(*dims, dtype=f32):
    return jax.ShapeDtypeStruct(dims, dtype)


def dft_blocks():
    k = np.arange(PROBE)
    angles = (k[:, None] * k[None, :] % PROBE) * (2.0 * math.pi / PROBE)
    cosine = np.cos(angles) / math.sqrt(PROBE)
    sine = np.sin(angles) / math.sqrt(PROBE)
    left = np.block([[cosine, sine], [-sine, cosine]]).astype(np.float32)
    high = left.astype(jnp.bfloat16)
    low = (left - high.astype(np.float32)).astype(jnp.bfloat16)
    return jnp.asarray(high), jnp.asarray(low), jnp.asarray(high.T.copy()), jnp.asarray(low.T.copy())


def ray_sums(radon_ref, volume_ref, out_ref):
    volume_half = jnp.concatenate(
        [volume_ref[pl.ds(0, TILE, stride=2), :], volume_ref[pl.ds(1, TILE, stride=2), :]], axis=1
    ).astype(bf16)
    for zl in range(ZL):
        for xc in range(XC):
            rows = radon_ref[zl * XC + xc].reshape(HITS * RAYS, TILE)
            sums = jnp.dot(rows, volume_half, preferred_element_type=f32)
            for y in range(Y):
                low = sums[y * QR : (y + 1) * QR]
                high = sums[RAYS + y * QR : RAYS + (y + 1) * QR]
                out_ref[xc * Y + y, zl] = jnp.concatenate([low, high], axis=0).astype(bf16)


def first_rows(place_ref, target_ref):
    back_y = [lax.rem(place_ref[1] + Y - y, Y) * XC for y in range(Y)]
    back_zl = [lax.rem(place_ref[2] + ZL - zl, ZL) for zl in range(ZL)]

    def row(zl, y, xc):
        return pl.multiple_of(target_ref[back_zl[zl], back_y[y] + xc] * QR, QR)

    return row


def add_tiles(place_ref, target_ref, sums_ref, own_ref, one_ref, two_ref, three_ref, out_ref, inter_ref, total):
    row = first_rows(place_ref, target_ref)
    total[...] = jnp.zeros(total.shape, f32)
    for part in range(2):
        inter = (own_ref[part] + one_ref[part].astype(f32)) + (two_ref[part].astype(f32) + three_ref[part].astype(f32))
        inter_ref[part] = inter
        total[place_ref[2], :, part * NZ : (part + 1) * NZ] = inter * share
    for xc in range(XC):
        for y in range(Y):
            for zl in range(ZL):
                total[zl, pl.ds(row(zl, y, xc), HITS * QR), :] += sums_ref[xc * Y + y, zl].astype(f32)
    for zh in range(ZH):
        for zl in range(ZL):
            out_ref[zh * ZL + zl] = total[zl, :, zh * NZ : (zh + 1) * NZ].astype(bf16)


def residual_part(
    place_ref, sums_ref, inter_ref, mine_ref, theirs_ref, residual_ref, own_ref, one_ref, two_ref, three_ref,
    joint, drift,
):
    zh = place_ref[0]
    y = place_ref[1]
    total = sums_ref[0].astype(f32)
    for source in range(1, DEEP):
        total = total + sums_ref[source].astype(f32)
    joint[...] = total
    for other, ref in enumerate((mine_ref, theirs_ref)):
        for back in range(Y):
            owner = lax.rem(zh + other, ZH) * Y + lax.rem(y + Y - back, Y)
            drift[pl.ds(pl.multiple_of(owner * 2 * QR, 2 * QR), 2 * QR), :] = ref[back]
    residual = (keep * (total - drift[...])).astype(bf16)
    for copy in range(DEEP):
        residual_ref[copy] = residual
    for ahead, ref in enumerate((own_ref, one_ref, two_ref, three_ref)):
        for other in range(ZH):
            owner = lax.rem(zh + other, ZH) * Y + lax.rem(y + ahead, Y)
            rows = pl.ds(pl.multiple_of(owner * 2 * QR, 2 * QR), 2 * QR)
            ref[other, 0] = joint[rows, :]
            for part in range(2):
                ref[other, 1 + part] = inter_ref[part, rows, :]


def pick_tiles(place_ref, target_ref, residual_ref, out_ref, rows_ref):
    for zl in range(ZL):
        rows_ref[zl] = jnp.concatenate(
            [residual_ref[zl].astype(f32), residual_ref[ZL + zl].astype(f32)], axis=1
        )

    row = first_rows(place_ref, target_ref)
    for xc in range(XC):
        for y in range(Y):
            for zl in range(ZL):
                out_ref[xc * Y + y, zl] = rows_ref[zl, pl.ds(row(zl, y, xc), HITS * QR), :].astype(bf16)


def back_project(radon_ref, picked_ref, volume_ref, out_ref):
    gradient = jnp.dot(
        radon_ref[...],
        picked_ref[...].reshape(NEAR * ZL * HITS * QR, 2 * NZ),
        preferred_element_type=f32,
    )
    for part in range(2):
        rows = pl.ds(part, TILE, stride=2)
        out_ref[rows, :] = volume_ref[rows, :] - volume_step * gradient[:, part * NZ : (part + 1) * NZ]


def updates(
    place_ref, own_ref, one_ref, two_ref, three_ref, theirs_ref, object_ref, dual_ref, object_out, dual_out
):
    zh = place_ref[0]
    y = place_ref[1]
    for back, ref in enumerate((own_ref, one_ref, two_ref, three_ref)):
        source = lax.rem(y + Y - back, Y)
        for other in range(ZH):
            part = lax.rem(zh + other, ZH)
            for tile in range(2):
                piece = slice(tile * QR, (tile + 1) * QR)
                inter = ref[0, 1 + part, piece, :] + theirs_ref[back, 1 + part, piece, :]
                joint = theirs_ref[back, 0, piece, :] if other else ref[0, 0, piece, :]
                projection = joint - share * inter
                rows = pl.ds((tile * RAYS + source * QR) * 2 + part, QR, stride=2)
                field = object_ref[rows, :]
                dual = dual_ref[rows, :]
                object_next = field - object_step * (inter + dual + penalty * (field - projection))
                object_out[rows, :] = object_next
                dual_out[rows, :] = dual + penalty * (object_next - projection)


def split(value):
    high = value.astype(bf16)
    return high, (value - high.astype(f32)).astype(bf16)


def from_left(high_table, low_table, value):
    high, low = split(value)
    return (
        jnp.dot(high_table, high, preferred_element_type=f32)
        + jnp.dot(high_table, low, preferred_element_type=f32)
        + jnp.dot(low_table, high, preferred_element_type=f32)
    )


def from_right(value, high_table, low_table):
    high, low = split(value)
    return (
        jnp.dot(high, high_table, preferred_element_type=f32)
        + jnp.dot(low, high_table, preferred_element_type=f32)
        + jnp.dot(high, low_table, preferred_element_type=f32)
    )


FIELD_ROWS = 128
DRIFT_ROWS = 4 * QR
SENT_ROWS = FIELD_ROWS + DRIFT_ROWS + QR


def pack(place_ref, object_ref, dual_ref, target_ref, own_ref, one_ref, two_ref, three_ref, drift):
    y = place_ref[1]
    targets = target_ref[...].astype(f32)
    drift[...] = object_ref[...] + dual_ref[...]
    for ahead, ref in enumerate((own_ref, one_ref, two_ref, three_ref)):
        ref[0:FIELD_ROWS, :] = object_ref[...]
        ref[FIELD_ROWS + DRIFT_ROWS :, :] = jnp.zeros((QR, NZ), f32)
        ref[FIELD_ROWS + DRIFT_ROWS : FIELD_ROWS + DRIFT_ROWS + 1, : ZL * XC] = targets
        for part in range(2):
            for tile in range(2):
                start = (tile * RAYS + lax.rem(y + ahead, Y) * QR) * 2 + part
                base = FIELD_ROWS + (part * 2 + tile) * QR
                ref[base : base + QR, :] = drift[pl.ds(start, QR, stride=2), :]


def frame_gradients(
    place_ref, starts_ref, field_0, field_1, field_2, field_3, field_4, field_5, field_6, field_7,
    probe_ref, measured_ref, ah_ref, al_ref, bh_ref, bl_ref, own_ref, sent_one, sent_two, sent_three,
    field_re, field_im, total_re, total_im,
):
    zh = place_ref[0]
    y = place_ref[1]
    fields = (field_0, field_1, field_2, field_3, field_4, field_5, field_6, field_7)
    for place, field_ref in enumerate(fields):
        owner = lax.rem(zh + place // Y, ZH) * Y + lax.rem(y + Y - place % Y, Y)
        rows = pl.ds(pl.multiple_of(owner * 64, 64), 64)
        field_re[rows, :] = field_ref[pl.ds(0, 64, stride=2), :]
        field_im[rows, :] = field_ref[pl.ds(1, 64, stride=2), :]
    total_re[...] = jnp.zeros(total_re.shape, f32)
    total_im[...] = jnp.zeros(total_im.shape, f32)
    probe_re = probe_ref[0]
    probe_im = probe_ref[1]
    ah, al, bh, bl = ah_ref[...], al_ref[...], bh_ref[...], bl_ref[...]
    for pair in range(FR_DEV // 2):
        waves = []
        for frame in (2 * pair, 2 * pair + 1):
            rows = pl.ds(starts_ref[0, frame], PROBE)
            object_re = field_re[rows, :]
            object_im = field_im[rows, :]
            waves.append(
                jnp.concatenate(
                    [
                        probe_re * object_re - probe_im * object_im,
                        probe_re * object_im + probe_im * object_re,
                    ],
                    axis=0,
                )
            )
        lefts = from_left(ah, al, jnp.concatenate(waves, axis=1))
        sides = jnp.concatenate(
            [
                jnp.concatenate([lefts[:PROBE, i * NZ : (i + 1) * NZ], lefts[PROBE:, i * NZ : (i + 1) * NZ]], axis=1)
                for i in range(2)
            ],
            axis=0,
        )
        far = from_right(sides, bh, bl)
        far_re = far[:, :NZ]
        far_im = far[:, NZ:]
        modulus = jnp.sqrt(far_re * far_re + far_im * far_im)
        intensity = measured_ref[2 * pair : 2 * pair + 2].reshape(2 * PROBE, NZ)
        shrink = 1.0 - jnp.sqrt(intensity) / jnp.maximum(modulus, 1.0)
        diff = jnp.concatenate([far_re * shrink, far_im * shrink], axis=1)
        half = from_right(diff, ah, al)
        stacked = jnp.concatenate(
            [
                jnp.concatenate([half[i * PROBE : (i + 1) * PROBE, :NZ], half[i * PROBE : (i + 1) * PROBE, NZ:]], axis=0)
                for i in range(2)
            ],
            axis=1,
        )
        backs = from_left(bh, bl, stacked)
        for i in range(2):
            back_re = backs[:PROBE, i * NZ : (i + 1) * NZ]
            back_im = backs[PROBE:, i * NZ : (i + 1) * NZ]
            rows = pl.ds(starts_ref[0, 2 * pair + i], PROBE)
            total_re[rows, :] += probe_re * back_re + probe_im * back_im
            total_im[rows, :] += probe_re * back_im - probe_im * back_re
    for ahead in range(Y):
        owner = lax.rem(y + ahead, Y)
        for tile in range(0, NR, 2):
            low = pl.ds(pl.multiple_of(tile * RAYS + owner * QR, QR), QR)
            high = pl.ds(pl.multiple_of((tile + 1) * RAYS + owner * QR, QR), QR)
            rows = slice(tile * QR, (tile + 2) * QR)
            for part, total in enumerate((total_re, total_im)):
                piece = jnp.concatenate([total[low, :], total[high, :]], axis=0)
                if ahead == 0:
                    own_ref[part, rows, :] = piece
                else:
                    (sent_one, sent_two, sent_three)[ahead - 1][part, rows, :] = piece.astype(bf16)


def shifted(value, axis, length, step):
    return lax.ppermute(value, axis, [(i, (i + step) % length) for i in range(length)])


def across(value):
    return shifted(value, "zh", ZH, 1)


def round_y(pieces):
    return [pieces[0]] + [shifted(pieces[k], "y", Y, k) for k in range(1, Y)]


def body(measured, positions, probe_field, object_field, dual_field, volume, radon_tiles, tile_range):
    zh = lax.axis_index("zh")
    zl = lax.axis_index("zl")
    y = lax.axis_index("y")
    place = jnp.stack([zh, y, zl]).astype(jnp.int32)
    ah, al, bh, bl = dft_blocks()
    radon = radon_tiles.reshape(ZL * XC, HITS, RAYS, TILE)
    volume_rows = volume.reshape(2 * TILE, NZ)
    object_rows = object_field.reshape(128, NZ)
    dual_rows = dual_field.reshape(128, NZ)

    with jax.named_scope("ray_sums"):
        object_theirs = across(object_rows)
        sums = call(ray_sums, shape(NEAR, ZL, HITS * QR, 2 * NZ, dtype=bf16), 0, 2, flops=2 * 2048 * 256 * 256)(
            radon, volume_rows
        )

    with jax.named_scope("fields"):
        packed = call(
            pack, (shape(SENT_ROWS, NZ),) * Y, 1, 3, scratch=[pltpu.VMEM((128, NZ), f32)], flops=1_000_000
        )(place, object_rows, dual_rows, tile_range.reshape(1, ZL * XC))
        fields = round_y(packed)
        far_fields = round_y([object_theirs] * Y)

    with jax.named_scope("ray_sums"):
        near_sums = lax.all_to_all(sums, CROSS, 0, 0, tiled=True)

    with jax.named_scope("targets"):
        tables = jnp.stack([field[FIELD_ROWS + DRIFT_ROWS, : ZL * XC] for field in fields])
        tables = tables.astype(jnp.int32).reshape(Y, ZL, XC)
        ahead = [lax.dynamic_index_in_dim(tables, (zl + k) % ZL, 1, keepdims=False) for k in range(ZL)]
        tables = jnp.stack([ahead[0]] + [shifted(ahead[k], "zl", ZL, k) for k in range(1, ZL)])
        tables = tables.reshape(ZL, Y * XC)
        drifts = jnp.stack([field[FIELD_ROWS : FIELD_ROWS + DRIFT_ROWS] for field in fields])
        drifts = drifts.reshape(Y, 2, 2 * QR, NZ)
        drift_mine = lax.dynamic_index_in_dim(drifts, zh, 1, keepdims=False)
        drift_theirs = across(lax.dynamic_index_in_dim(drifts, 1 - zh, 1, keepdims=False))
        far_fields, tables, drift_theirs = lax.optimization_barrier((far_fields, tables, drift_theirs))

    with jax.named_scope("frames"):
        inter_parts = call(
            frame_gradients,
            (shape(2, 128, NZ),) + (shape(2, 128, NZ, dtype=bf16),) * 3,
            2,
            14,
            scratch=[pltpu.VMEM((NDET, NZ), f32)] * 4,
            flops=1_600_000_000,
        )(place, positions, *fields, *far_fields, probe_field, measured[0], ah, al, bh, bl)
        inter_parts = round_y(inter_parts)

    with jax.named_scope("near_sum"):
        dense, inter = call(
            add_tiles,
            (shape(DEEP, 128, NZ, dtype=bf16), shape(2, 128, NZ)),
            2,
            5,
            scratch=[pltpu.VMEM((ZL, 128, 2 * NZ), f32)],
            flops=1_000_000,
        )(place, tables, near_sums, *inter_parts)
        far_sums = lax.all_to_all(dense, ALONG, 0, 0, tiled=True)

    with jax.named_scope("residual"):
        copies, *kept = call(
            residual_part,
            (shape(DEEP, 128, NZ, dtype=bf16),) + (shape(ZH, 3, 2 * QR, NZ),) * Y,
            1,
            4,
            scratch=[pltpu.VMEM((128, NZ), f32)] * 2,
            flops=1_000_000,
        )(place, far_sums, inter, drift_mine, drift_theirs)
        kept = round_y(kept)
        residuals = lax.all_to_all(copies, ALONG, 0, 0, tiled=True)

    with jax.named_scope("pick"):
        picked = call(
            pick_tiles,
            shape(NEAR, ZL, HITS * QR, 2 * NZ, dtype=bf16),
            2,
            1,
            scratch=[pltpu.VMEM((ZL, 128, 2 * NZ), f32)],
            flops=1_000_000,
        )(place, tables, residuals)
        picked, kept = lax.optimization_barrier((picked, kept))
        returned = lax.all_to_all(picked, CROSS, 0, 0, tiled=True)

    with jax.named_scope("updates"):
        theirs = across(jnp.stack([piece[1] for piece in kept]))
        object_next, dual_next = call(updates, (shape(128, NZ), shape(128, NZ)), 1, 7, flops=1_000_000)(
            place, *kept, theirs, object_rows, dual_rows
        )

    with jax.named_scope("back_project"):
        ordered = radon.reshape(ZL, XC, HITS, Y, QR, TILE).transpose(5, 1, 3, 0, 2, 4).reshape(TILE, -1)
        volume_next = call(back_project, shape(2 * TILE, NZ), 0, 3, flops=2 * 2048 * 256 * 256)(
            ordered, returned, volume_rows
        )
    return (
        object_next.reshape(object_field.shape),
        dual_next.reshape(dual_field.shape),
        volume_next.reshape(volume.shape),
    )


def solution(mesh):
    fine = Mesh(mesh.devices.reshape(ZL, X, C, ZH, Y), ("zl", "x", "c", "zh", "y"))
    ang = ("zl", "x", "c")
    strip = ("zh", "y")
    return jax.shard_map(
        body,
        mesh=fine,
        in_specs=(
            P(ang, strip, None, None),
            P(ang, strip),
            P(),
            P(ang, strip, None, None),
            P(ang, strip, None, None),
            P(ang + strip, None, None),
            P(ang + strip, None, None, None, None),
            P(ang, None, strip, None),
        ),
        out_specs=(
            P(ang, strip, None, None),
            P(ang, strip, None, None),
            P(ang + strip, None, None),
        ),
        check_vma=False,
    )
```

```python
import math

import jax
import jax.numpy as jnp
import numpy as np
from jax import lax
from jax.experimental import pallas as pl
from jax.experimental.pallas import tpu as pltpu
from jax.sharding import Mesh
from jax.sharding import PartitionSpec as P

PROBE = 128
NZ = 128
NDET = 512
RAYS = 32
TILE = 256
HITS = 2
NR = 16

ZL, X, C, ZH, Y = 4, 4, 2, 2, 4
XC = X * C
CROSS = ("x", "c", "y")
ALONG = ("zh", "zl")
NEAR = XC * Y
DEEP = ZH * ZL
QR = RAYS // Y
FR_DEV = 8
FRAMES_COST = 20_000_000_000

penalty = 1.0
object_step = 0.1
volume_step = 1.0
keep = 1.0 - object_step
share = object_step / keep
f32 = jnp.float32
bf16 = jnp.bfloat16

VM = pl.BlockSpec(memory_space=pltpu.VMEM)
SM = pl.BlockSpec(memory_space=pltpu.SMEM)
FAR = pl.BlockSpec(memory_space=pltpu.HBM)


def call(kernel, outs, n_smem, n_vmem, scratch=(), flops=0, moved=1 << 20, limit=48 << 20, n_far=0):
    many = isinstance(outs, tuple)
    return pl.pallas_call(
        kernel,
        out_shape=outs,
        in_specs=[SM] * n_smem + [FAR] * n_far + [VM] * n_vmem,
        out_specs=tuple(VM for _ in outs) if many else VM,
        scratch_shapes=list(scratch),
        compiler_params=pltpu.CompilerParams(vmem_limit_bytes=limit),
        cost_estimate=pl.CostEstimate(flops=flops, bytes_accessed=moved, transcendentals=0),
        name=kernel.__name__,
    )


def shape(*dims, dtype=f32):
    return jax.ShapeDtypeStruct(dims, dtype)


def dft_blocks():
    k = np.arange(PROBE)
    angles = (k[:, None] * k[None, :] % PROBE) * (2.0 * math.pi / PROBE)
    cosine = np.cos(angles) / math.sqrt(PROBE)
    sine = np.sin(angles) / math.sqrt(PROBE)
    left = np.block([[cosine, sine], [-sine, cosine]]).astype(np.float32)
    high = left.astype(jnp.bfloat16)
    low = (left - high.astype(np.float32)).astype(jnp.bfloat16)
    return jnp.asarray(high), jnp.asarray(low), jnp.asarray(high.T.copy()), jnp.asarray(low.T.copy())


def ray_sums(radon_far, volume_far, out_ref, radon_ref, volume_ref, sems):
    copies = [pltpu.make_async_copy(volume_far, volume_ref, sems.at[ZL])]
    for zl in range(ZL):
        angles = pl.ds(zl * XC, XC)
        copies.append(pltpu.make_async_copy(radon_far.at[angles], radon_ref.at[angles], sems.at[zl]))
    for copy in copies:
        copy.start()
    copies[0].wait()
    volume_half = jnp.concatenate(
        [volume_ref[pl.ds(0, TILE, stride=2), :], volume_ref[pl.ds(1, TILE, stride=2), :]], axis=1
    ).astype(bf16)
    for zl in range(ZL):
        copies[1 + zl].wait()
        for xc in range(XC):
            rows = radon_ref[zl * XC + xc].reshape(HITS * RAYS, TILE)
            sums = jnp.dot(rows, volume_half, preferred_element_type=f32)
            for y in range(Y):
                low = sums[y * QR : (y + 1) * QR]
                high = sums[RAYS + y * QR : RAYS + (y + 1) * QR]
                out_ref[xc * Y + y, zl] = jnp.concatenate([low, high], axis=0).astype(bf16)


def first_rows(place_ref, target_ref):
    zl_here = place_ref[2]
    back_y = [lax.rem(place_ref[1] + Y - y, Y) * ZL for y in range(Y)]
    back_zl = [lax.rem(zl_here + ZL - zl, ZL) for zl in range(ZL)]

    def row(zl, y, xc):
        return pl.multiple_of(target_ref[back_y[y] + back_zl[zl], zl_here * XC + xc] * QR, QR)

    return row


def add_tiles(
    place_ref, target_ref, sums_ref, inter_0, inter_1, inter_2, inter_3, field_0, field_1, field_2, field_3,
    out_ref, inter_ref, total,
):
    zh = place_ref[0]
    y_here = place_ref[1]
    zl_here = place_ref[2]
    row = first_rows(place_ref, target_ref)
    total[...] = jnp.zeros(total.shape, f32)
    for part in range(2):
        inter = (inter_0[part] + inter_1[part].astype(f32)) + (inter_2[part].astype(f32) + inter_3[part].astype(f32))
        inter_ref[part] = inter
        total[zl_here, :, part * NZ : (part + 1) * NZ] = inter * share
    for back, field_ref in enumerate((field_0, field_1, field_2, field_3)):
        owner = zh * Y + lax.rem(y_here + Y - back, Y)
        rows = pl.ds(pl.multiple_of(owner * 2 * QR, 2 * QR), 2 * QR)
        base = FIELD_ROWS
        total[zl_here, rows, :] -= jnp.concatenate(
            [field_ref[base : base + 2 * QR, :], field_ref[base + 2 * QR : base + 4 * QR, :]], axis=1
        )
    for xc in range(XC):
        for y in range(Y):
            for zl in range(ZL):
                total[zl, pl.ds(row(zl, y, xc), HITS * QR), :] += sums_ref[xc * Y + y, zl].astype(f32)
    for zh in range(ZH):
        for zl in range(ZL):
            out_ref[zh * ZL + zl] = total[zl, :, zh * NZ : (zh + 1) * NZ].astype(bf16)


def residual_part(place_ref, sums_ref, inter_ref, residual_ref, own_ref, one_ref, two_ref, three_ref, joint):
    zh = place_ref[0]
    y = place_ref[1]
    total = sums_ref[0].astype(f32)
    for source in range(1, DEEP):
        total = total + sums_ref[source].astype(f32)
    joint[...] = total
    residual = (keep * total).astype(bf16)
    for copy in range(DEEP):
        residual_ref[copy] = residual
    for ahead, ref in enumerate((own_ref, one_ref, two_ref, three_ref)):
        for other in range(ZH):
            owner = lax.rem(zh + other, ZH) * Y + lax.rem(y + ahead, Y)
            rows = pl.ds(pl.multiple_of(owner * 2 * QR, 2 * QR), 2 * QR)
            ref[other, 0] = joint[rows, :]
            for part in range(2):
                ref[other, 1 + part] = inter_ref[part, rows, :]


def pick_tiles(place_ref, target_ref, residual_ref, out_ref, rows_ref):
    for zl in range(ZL):
        rows_ref[zl] = jnp.concatenate(
            [residual_ref[zl].astype(f32), residual_ref[ZL + zl].astype(f32)], axis=1
        )

    row = first_rows(place_ref, target_ref)
    for xc in range(XC):
        for y in range(Y):
            for zl in range(ZL):
                out_ref[xc * Y + y, zl] = rows_ref[zl, pl.ds(row(zl, y, xc), HITS * QR), :].astype(bf16)


def back_project(radon_ref, picked_ref, volume_ref, out_ref):
    gradient = jnp.dot(
        radon_ref[...],
        picked_ref[...].reshape(NEAR * ZL * HITS * QR, 2 * NZ),
        preferred_element_type=f32,
    )
    for part in range(2):
        rows = pl.ds(part, TILE, stride=2)
        out_ref[rows, :] = volume_ref[rows, :] - volume_step * gradient[:, part * NZ : (part + 1) * NZ]


def updates(
    place_ref, own_ref, one_ref, two_ref, three_ref, theirs_ref, object_ref, dual_ref, object_out, dual_out
):
    zh = place_ref[0]
    y = place_ref[1]
    for back, ref in enumerate((own_ref, one_ref, two_ref, three_ref)):
        source = lax.rem(y + Y - back, Y)
        for other in range(ZH):
            part = lax.rem(zh + other, ZH)
            for tile in range(2):
                piece = slice(tile * QR, (tile + 1) * QR)
                inter = ref[0, 1 + part, piece, :] + theirs_ref[back, 1 + part, piece, :]
                joint = theirs_ref[back, 0, piece, :] if other else ref[0, 0, piece, :]
                rows = pl.ds((tile * RAYS + source * QR) * 2 + part, QR, stride=2)
                field = object_ref[rows, :]
                dual = dual_ref[rows, :]
                projection = joint + (field + dual) - share * inter
                object_next = field - object_step * (inter + dual + penalty * (field - projection))
                object_out[rows, :] = object_next
                dual_out[rows, :] = dual + penalty * (object_next - projection)


def split(value):
    high = value.astype(bf16)
    return high, (value - high.astype(f32)).astype(bf16)


def from_left(high_table, low_table, value):
    high, low = split(value)
    return (
        jnp.dot(high_table, high, preferred_element_type=f32)
        + jnp.dot(high_table, low, preferred_element_type=f32)
        + jnp.dot(low_table, high, preferred_element_type=f32)
    )


def from_right(value, high_table, low_table):
    high, low = split(value)
    return (
        jnp.dot(high, high_table, preferred_element_type=f32)
        + jnp.dot(low, high_table, preferred_element_type=f32)
        + jnp.dot(high, low_table, preferred_element_type=f32)
    )


FIELD_ROWS = 128
SENT_ROWS = FIELD_ROWS + 4 * QR


def pack(place_ref, object_far, dual_far, own_ref, one_ref, two_ref, three_ref, field, both, sems):
    y = place_ref[1]
    copies = [pltpu.make_async_copy(object_far, field, sems.at[0]), pltpu.make_async_copy(dual_far, both, sems.at[1])]
    for copy in copies:
        copy.start()
    for copy in copies:
        copy.wait()
    both[...] += field[...]
    for ahead, ref in enumerate((own_ref, one_ref, two_ref, three_ref)):
        ref[0:FIELD_ROWS, :] = field[...]
        for part in range(2):
            for tile in range(2):
                start = (tile * RAYS + lax.rem(y + ahead, Y) * QR) * 2 + part
                base = FIELD_ROWS + (part * 2 + tile) * QR
                ref[base : base + QR, :] = both[pl.ds(start, QR, stride=2), :]


def pack_far(theirs_ref, own_ref, one_ref, two_ref, three_ref, out_ref):
    out_ref[0:FIELD_ROWS, :] = theirs_ref[...]
    out_ref[FIELD_ROWS:, :] = jnp.zeros((QR, NZ), f32)
    for back, ref in enumerate((own_ref, one_ref, two_ref, three_ref)):
        out_ref[FIELD_ROWS + back : FIELD_ROWS + back + 1, : ZL * XC] = ref[...].astype(f32)


def frame_gradients(
    place_ref, starts_ref, field_0, field_1, field_2, field_3, field_4, field_5, field_6, field_7,
    probe_ref, measured_ref, ah_ref, al_ref, bh_ref, bl_ref, own_ref, sent_one, sent_two, sent_three,
    field_re, field_im, total_re, total_im,
):
    zh = place_ref[0]
    y = place_ref[1]
    fields = (field_0, field_1, field_2, field_3, field_4, field_5, field_6, field_7)
    for place, field_ref in enumerate(fields):
        owner = lax.rem(zh + place // Y, ZH) * Y + lax.rem(y + Y - place % Y, Y)
        rows = pl.ds(pl.multiple_of(owner * 64, 64), 64)
        field_re[rows, :] = field_ref[pl.ds(0, 64, stride=2), :]
        field_im[rows, :] = field_ref[pl.ds(1, 64, stride=2), :]
    total_re[...] = jnp.zeros(total_re.shape, f32)
    total_im[...] = jnp.zeros(total_im.shape, f32)
    probe_re = probe_ref[0]
    probe_im = probe_ref[1]
    ah, al, bh, bl = ah_ref[...], al_ref[...], bh_ref[...], bl_ref[...]
    for pair in range(FR_DEV // 2):
        waves = []
        for frame in (2 * pair, 2 * pair + 1):
            rows = pl.ds(starts_ref[0, frame], PROBE)
            object_re = field_re[rows, :]
            object_im = field_im[rows, :]
            waves.append(
                jnp.concatenate(
                    [
                        probe_re * object_re - probe_im * object_im,
                        probe_re * object_im + probe_im * object_re,
                    ],
                    axis=0,
                )
            )
        lefts = from_left(ah, al, jnp.concatenate(waves, axis=1))
        sides = jnp.concatenate(
            [
                jnp.concatenate([lefts[:PROBE, i * NZ : (i + 1) * NZ], lefts[PROBE:, i * NZ : (i + 1) * NZ]], axis=1)
                for i in range(2)
            ],
            axis=0,
        )
        far = from_right(sides, bh, bl)
        far_re = far[:, :NZ]
        far_im = far[:, NZ:]
        modulus = jnp.sqrt(far_re * far_re + far_im * far_im)
        intensity = measured_ref[2 * pair : 2 * pair + 2].reshape(2 * PROBE, NZ)
        shrink = 1.0 - jnp.sqrt(intensity) / jnp.maximum(modulus, 1.0)
        diff = jnp.concatenate([far_re * shrink, far_im * shrink], axis=1)
        half = from_right(diff, ah, al)
        stacked = jnp.concatenate(
            [
                jnp.concatenate([half[i * PROBE : (i + 1) * PROBE, :NZ], half[i * PROBE : (i + 1) * PROBE, NZ:]], axis=0)
                for i in range(2)
            ],
            axis=1,
        )
        backs = from_left(bh, bl, stacked)
        for i in range(2):
            back_re = backs[:PROBE, i * NZ : (i + 1) * NZ]
            back_im = backs[PROBE:, i * NZ : (i + 1) * NZ]
            rows = pl.ds(starts_ref[0, 2 * pair + i], PROBE)
            total_re[rows, :] += probe_re * back_re + probe_im * back_im
            total_im[rows, :] += probe_re * back_im - probe_im * back_re
    for ahead in range(Y):
        owner = lax.rem(y + ahead, Y)
        for tile in range(0, NR, 2):
            low = pl.ds(pl.multiple_of(tile * RAYS + owner * QR, QR), QR)
            high = pl.ds(pl.multiple_of((tile + 1) * RAYS + owner * QR, QR), QR)
            rows = slice(tile * QR, (tile + 2) * QR)
            for part, total in enumerate((total_re, total_im)):
                piece = jnp.concatenate([total[low, :], total[high, :]], axis=0)
                if ahead == 0:
                    own_ref[part, rows, :] = piece
                else:
                    (sent_one, sent_two, sent_three)[ahead - 1][part, rows, :] = piece.astype(bf16)


def shifted(value, axis, length, step):
    return lax.ppermute(value, axis, [(i, (i + step) % length) for i in range(length)])


def across(value):
    return shifted(value, "zh", ZH, 1)


def round_y(pieces):
    return [pieces[0]] + [shifted(pieces[k], "y", Y, k) for k in range(1, Y)]


def body(measured, positions, probe_field, object_field, dual_field, volume, radon_tiles, tile_range):
    zh = lax.axis_index("zh")
    zl = lax.axis_index("zl")
    y = lax.axis_index("y")
    place = jnp.stack([zh, y, zl]).astype(jnp.int32)
    ah, al, bh, bl = dft_blocks()
    radon = radon_tiles.reshape(ZL * XC, HITS, RAYS, TILE)
    volume_rows = volume.reshape(2 * TILE, NZ)
    object_rows = object_field.reshape(128, NZ)
    dual_rows = dual_field.reshape(128, NZ)

    with jax.named_scope("fields"):
        object_theirs = across(object_rows)
        own_targets = tile_range.reshape(1, ZL * XC)
        targets = [own_targets] + [shifted(own_targets, "zl", ZL, k) for k in range(1, ZL)]
        targets, radon = lax.optimization_barrier((targets, radon))

    with jax.named_scope("ray_sums"):
        sums = call(
            ray_sums,
            shape(NEAR, ZL, HITS * QR, 2 * NZ, dtype=bf16),
            0,
            0,
            n_far=2,
            scratch=[pltpu.VMEM(radon.shape, bf16), pltpu.VMEM((2 * TILE, NZ), f32), pltpu.SemaphoreType.DMA((ZL + 1,))],
            flops=2 * 2048 * 256 * 256,
        )(radon, volume_rows)

    with jax.named_scope("fields"):
        packed = call(
            pack,
            (shape(SENT_ROWS, NZ),) * Y,
            1,
            0,
            n_far=2,
            scratch=[pltpu.VMEM((128, NZ), f32)] * 2 + [pltpu.SemaphoreType.DMA((2,))],
            flops=1_000_000,
        )(place, object_rows, dual_rows)
        fields = round_y(packed)
        object_theirs, sums = lax.optimization_barrier((object_theirs, sums))
        near_sums = lax.all_to_all(sums, CROSS, 0, 0, tiled=True)
        packed_far = call(pack_far, shape(FIELD_ROWS + QR, NZ), 0, 5, flops=1_000_000)(object_theirs, *targets)
        far_fields = round_y([packed_far] * Y)
        tables = jnp.concatenate([field[FIELD_ROWS : FIELD_ROWS + ZL, : ZL * XC] for field in far_fields])
        tables = tables.astype(jnp.int32)

    with jax.named_scope("frames"):
        inter_parts = call(
            frame_gradients,
            (shape(2, 128, NZ),) + (shape(2, 128, NZ, dtype=bf16),) * 3,
            2,
            14,
            scratch=[pltpu.VMEM((NDET, NZ), f32)] * 4,
            flops=FRAMES_COST,
        )(place, positions, *fields, *far_fields, probe_field, measured[0], ah, al, bh, bl)
        inter_parts = round_y(inter_parts)

    with jax.named_scope("near_sum"):
        dense, inter = call(
            add_tiles,
            (shape(DEEP, 128, NZ, dtype=bf16), shape(2, 128, NZ)),
            2,
            9,
            scratch=[pltpu.VMEM((ZL, 128, 2 * NZ), f32)],
            flops=1_000_000,
        )(place, tables, near_sums, *inter_parts, *fields)
        far_sums = lax.all_to_all(dense, ALONG, 0, 0, tiled=True)

    with jax.named_scope("residual"):
        copies, *kept = call(
            residual_part,
            (shape(DEEP, 128, NZ, dtype=bf16),) + (shape(ZH, 3, 2 * QR, NZ),) * Y,
            1,
            2,
            scratch=[pltpu.VMEM((128, NZ), f32)],
            flops=1_000_000,
        )(place, far_sums, inter)
        kept = round_y(kept)
        residuals = lax.all_to_all(copies, ALONG, 0, 0, tiled=True)

    with jax.named_scope("pick"):
        picked = call(
            pick_tiles,
            shape(NEAR, ZL, HITS * QR, 2 * NZ, dtype=bf16),
            2,
            1,
            scratch=[pltpu.VMEM((ZL, 128, 2 * NZ), f32)],
            flops=1_000_000,
        )(place, tables, residuals)
        picked, kept = lax.optimization_barrier((picked, kept))
        returned = lax.all_to_all(picked, CROSS, 0, 0, tiled=True)

    with jax.named_scope("updates"):
        theirs = across(jnp.stack([piece[1] for piece in kept]))
        object_next, dual_next = call(updates, (shape(128, NZ), shape(128, NZ)), 1, 7, flops=1_000_000)(
            place, *kept, theirs, object_rows, dual_rows
        )

    with jax.named_scope("back_project"):
        ordered = radon.reshape(ZL, XC, HITS, Y, QR, TILE).transpose(5, 1, 3, 0, 2, 4).reshape(TILE, -1)
        volume_next = call(back_project, shape(2 * TILE, NZ), 0, 3, flops=2 * 2048 * 256 * 256)(
            ordered, returned, volume_rows
        )
    return (
        object_next.reshape(object_field.shape),
        dual_next.reshape(dual_field.shape),
        volume_next.reshape(volume.shape),
    )


def solution(mesh):
    fine = Mesh(mesh.devices.reshape(ZL, X, C, ZH, Y), ("zl", "x", "c", "zh", "y"))
    ang = ("zl", "x", "c")
    strip = ("zh", "y")
    return jax.shard_map(
        body,
        mesh=fine,
        in_specs=(
            P(ang, strip, None, None),
            P(ang, strip),
            P(),
            P(ang, strip, None, None),
            P(ang, strip, None, None),
            P(ang + strip, None, None),
            P(ang + strip, None, None, None, None),
            P(ang, None, strip, None),
        ),
        out_specs=(
            P(ang, strip, None, None),
            P(ang, strip, None, None),
            P(ang + strip, None, None),
        ),
        check_vma=False,
    )
```

```python
import math

import jax
import jax.numpy as jnp
import numpy as np
from jax import lax
from jax.experimental import pallas as pl
from jax.experimental.pallas import tpu as pltpu
from jax.sharding import Mesh
from jax.sharding import PartitionSpec as P

PROBE = 128
NZ = 128
NDET = 512
RAYS = 32
TILE = 256
HITS = 2
NR = 16

ZL, X, C, ZH, Y = 4, 4, 2, 2, 4
XC = X * C
CROSS = ("x", "c", "y")
ALONG = ("zh", "zl")
NEAR = XC * Y
DEEP = ZH * ZL
QR = RAYS // Y
FR_DEV = 8
FRAMES_COST = 6_000_000_000
SUMS_LIMIT = 62 << 20

penalty = 1.0
object_step = 0.1
volume_step = 1.0
keep = 1.0 - object_step
share = object_step / keep
f32 = jnp.float32
bf16 = jnp.bfloat16

VM = pl.BlockSpec(memory_space=pltpu.VMEM)
SM = pl.BlockSpec(memory_space=pltpu.SMEM)
FAR = pl.BlockSpec(memory_space=pltpu.HBM)


def call(kernel, outs, n_smem, n_vmem, scratch=(), flops=0, moved=1 << 20, limit=48 << 20, n_far=0):
    many = isinstance(outs, tuple)
    return pl.pallas_call(
        kernel,
        out_shape=outs,
        in_specs=[SM] * n_smem + [FAR] * n_far + [VM] * n_vmem,
        out_specs=tuple(VM for _ in outs) if many else VM,
        scratch_shapes=list(scratch),
        compiler_params=pltpu.CompilerParams(vmem_limit_bytes=limit),
        cost_estimate=pl.CostEstimate(flops=flops, bytes_accessed=moved, transcendentals=0),
        name=kernel.__name__,
    )


def shape(*dims, dtype=f32):
    return jax.ShapeDtypeStruct(dims, dtype)


def dft_blocks():
    k = np.arange(PROBE)
    angles = (k[:, None] * k[None, :] % PROBE) * (2.0 * math.pi / PROBE)
    cosine = np.cos(angles) / math.sqrt(PROBE)
    sine = np.sin(angles) / math.sqrt(PROBE)
    left = np.block([[cosine, sine], [-sine, cosine]]).astype(np.float32)
    high = left.astype(jnp.bfloat16)
    low = (left - high.astype(np.float32)).astype(jnp.bfloat16)
    return jnp.asarray(high), jnp.asarray(low), jnp.asarray(high.T.copy()), jnp.asarray(low.T.copy())


def ray_sums(radon_far, volume_far, out_ref, radon_ref, volume_ref, sems):
    copies = [pltpu.make_async_copy(volume_far, volume_ref, sems.at[ZL])]
    for zl in range(ZL):
        angles = pl.ds(zl * XC, XC)
        copies.append(pltpu.make_async_copy(radon_far.at[angles], radon_ref.at[angles], sems.at[zl]))
    for copy in copies:
        copy.start()
    copies[0].wait()
    volume_half = jnp.concatenate(
        [volume_ref[pl.ds(0, TILE, stride=2), :], volume_ref[pl.ds(1, TILE, stride=2), :]], axis=1
    ).astype(bf16)
    for zl in range(ZL):
        copies[1 + zl].wait()
        for xc in range(XC):
            rows = radon_ref[zl * XC + xc].reshape(HITS * RAYS, TILE)
            sums = jnp.dot(rows, volume_half, preferred_element_type=f32)
            for y in range(Y):
                low = sums[y * QR : (y + 1) * QR]
                high = sums[RAYS + y * QR : RAYS + (y + 1) * QR]
                out_ref[xc * Y + y, zl] = jnp.concatenate([low, high], axis=0).astype(bf16)


def first_rows(place_ref, target_ref):
    zl_here = place_ref[2]
    back_y = [lax.rem(place_ref[1] + Y - y, Y) for y in range(Y)]
    back_zl = [lax.rem(zl_here + ZL - zl, ZL) * Y for zl in range(ZL)]

    def row(zl, y, xc):
        return pl.multiple_of(target_ref[back_y[y] + back_zl[zl], zl_here * XC + xc] * QR, QR)

    return row


def add_tiles(
    place_ref, target_ref, sums_ref, inter_0, inter_1, inter_2, inter_3, field_0, field_1, field_2, field_3,
    out_ref, inter_ref, total,
):
    zh = place_ref[0]
    y_here = place_ref[1]
    zl_here = place_ref[2]
    row = first_rows(place_ref, target_ref)
    total[...] = jnp.zeros(total.shape, f32)
    for part in range(2):
        inter = (inter_0[part] + inter_1[part].astype(f32)) + (inter_2[part].astype(f32) + inter_3[part].astype(f32))
        inter_ref[part] = inter
        total[zl_here, :, part * NZ : (part + 1) * NZ] = inter * share
    for back, field_ref in enumerate((field_0, field_1, field_2, field_3)):
        owner = zh * Y + lax.rem(y_here + Y - back, Y)
        rows = pl.ds(pl.multiple_of(owner * 2 * QR, 2 * QR), 2 * QR)
        base = FIELD_ROWS
        total[zl_here, rows, :] -= jnp.concatenate(
            [field_ref[base : base + 2 * QR, :], field_ref[base + 2 * QR : base + 4 * QR, :]], axis=1
        )
    for xc in range(XC):
        for y in range(Y):
            for zl in range(ZL):
                total[zl, pl.ds(row(zl, y, xc), HITS * QR), :] += sums_ref[xc * Y + y, zl].astype(f32)
    for zh in range(ZH):
        for zl in range(ZL):
            out_ref[zh * ZL + zl] = total[zl, :, zh * NZ : (zh + 1) * NZ].astype(bf16)


def residual_part(place_ref, sums_ref, inter_ref, residual_ref, own_ref, one_ref, two_ref, three_ref, joint):
    zh = place_ref[0]
    y = place_ref[1]
    total = sums_ref[0].astype(f32)
    for source in range(1, DEEP):
        total = total + sums_ref[source].astype(f32)
    joint[...] = total
    residual = (keep * total).astype(bf16)
    for copy in range(DEEP):
        residual_ref[copy] = residual
    for ahead, ref in enumerate((own_ref, one_ref, two_ref, three_ref)):
        for other in range(ZH):
            owner = lax.rem(zh + other, ZH) * Y + lax.rem(y + ahead, Y)
            rows = pl.ds(pl.multiple_of(owner * 2 * QR, 2 * QR), 2 * QR)
            ref[other, 0] = joint[rows, :]
            for part in range(2):
                ref[other, 1 + part] = inter_ref[part, rows, :]


def pick_tiles(place_ref, target_ref, residual_ref, out_ref, rows_ref):
    for zl in range(ZL):
        rows_ref[zl] = jnp.concatenate(
            [residual_ref[zl].astype(f32), residual_ref[ZL + zl].astype(f32)], axis=1
        )

    row = first_rows(place_ref, target_ref)
    for xc in range(XC):
        for y in range(Y):
            for zl in range(ZL):
                out_ref[xc * Y + y, zl] = rows_ref[zl, pl.ds(row(zl, y, xc), HITS * QR), :].astype(bf16)


def back_project(radon_ref, picked_ref, volume_ref, out_ref):
    gradient = jnp.dot(
        radon_ref[...],
        picked_ref[...].reshape(NEAR * ZL * HITS * QR, 2 * NZ),
        preferred_element_type=f32,
    )
    for part in range(2):
        rows = pl.ds(part, TILE, stride=2)
        out_ref[rows, :] = volume_ref[rows, :] - volume_step * gradient[:, part * NZ : (part + 1) * NZ]


def updates(
    place_ref, own_ref, one_ref, two_ref, three_ref, theirs_ref, object_ref, dual_ref, object_out, dual_out
):
    zh = place_ref[0]
    y = place_ref[1]
    for back, ref in enumerate((own_ref, one_ref, two_ref, three_ref)):
        source = lax.rem(y + Y - back, Y)
        for other in range(ZH):
            part = lax.rem(zh + other, ZH)
            for tile in range(2):
                piece = slice(tile * QR, (tile + 1) * QR)
                inter = ref[0, 1 + part, piece, :] + theirs_ref[back, 1 + part, piece, :]
                joint = theirs_ref[back, 0, piece, :] if other else ref[0, 0, piece, :]
                rows = pl.ds((tile * RAYS + source * QR) * 2 + part, QR, stride=2)
                field = object_ref[rows, :]
                dual = dual_ref[rows, :]
                projection = joint + (field + dual) - share * inter
                object_next = field - object_step * (inter + dual + penalty * (field - projection))
                object_out[rows, :] = object_next
                dual_out[rows, :] = dual + penalty * (object_next - projection)


def split(value):
    high = value.astype(bf16)
    return high, (value - high.astype(f32)).astype(bf16)


def from_left(high_table, low_table, value):
    high, low = split(value)
    return (
        jnp.dot(high_table, high, preferred_element_type=f32)
        + jnp.dot(high_table, low, preferred_element_type=f32)
        + jnp.dot(low_table, high, preferred_element_type=f32)
    )


def from_right(value, high_table, low_table):
    high, low = split(value)
    return (
        jnp.dot(high, high_table, preferred_element_type=f32)
        + jnp.dot(low, high_table, preferred_element_type=f32)
        + jnp.dot(high, low_table, preferred_element_type=f32)
    )


FIELD_ROWS = 2 * 128
DRIFT_ROWS = 4 * QR
SENT_ROWS = FIELD_ROWS + DRIFT_ROWS + QR


def pack(place_ref, object_ref, theirs_ref, dual_ref, target_ref, own_ref, one_ref, two_ref, three_ref, both):
    y = place_ref[1]
    targets = target_ref[...].astype(f32)
    both[...] = object_ref[...] + dual_ref[...]
    for ahead, ref in enumerate((own_ref, one_ref, two_ref, three_ref)):
        ref[0:128, :] = object_ref[...]
        ref[128:256, :] = theirs_ref[...]
        ref[FIELD_ROWS + DRIFT_ROWS :, :] = jnp.zeros((QR, NZ), f32)
        ref[FIELD_ROWS + DRIFT_ROWS : FIELD_ROWS + DRIFT_ROWS + 1, : ZL * XC] = targets
        for part in range(2):
            for tile in range(2):
                start = (tile * RAYS + lax.rem(y + ahead, Y) * QR) * 2 + part
                base = FIELD_ROWS + (part * 2 + tile) * QR
                ref[base : base + QR, :] = both[pl.ds(start, QR, stride=2), :]


def frame_gradients(
    place_ref, starts_ref, field_0, field_1, field_2, field_3, probe_ref,
    measured_ref, ah_ref, al_ref, bh_ref, bl_ref, own_ref, sent_one, sent_two, sent_three,
    field_re, field_im, total_re, total_im,
):
    zh = place_ref[0]
    y = place_ref[1]
    for back, field_ref in enumerate((field_0, field_1, field_2, field_3)):
        for other in range(ZH):
            owner = lax.rem(zh + other, ZH) * Y + lax.rem(y + Y - back, Y)
            rows = pl.ds(pl.multiple_of(owner * 64, 64), 64)
            field_re[rows, :] = field_ref[pl.ds(other * 128, 64, stride=2), :]
            field_im[rows, :] = field_ref[pl.ds(other * 128 + 1, 64, stride=2), :]
    total_re[...] = jnp.zeros(total_re.shape, f32)
    total_im[...] = jnp.zeros(total_im.shape, f32)
    probe_re = probe_ref[0]
    probe_im = probe_ref[1]
    ah, al, bh, bl = ah_ref[...], al_ref[...], bh_ref[...], bl_ref[...]
    for pair in range(FR_DEV // 2):
        waves = []
        for frame in (2 * pair, 2 * pair + 1):
            rows = pl.ds(starts_ref[0, frame], PROBE)
            object_re = field_re[rows, :]
            object_im = field_im[rows, :]
            waves.append(
                jnp.concatenate(
                    [
                        probe_re * object_re - probe_im * object_im,
                        probe_re * object_im + probe_im * object_re,
                    ],
                    axis=0,
                )
            )
        lefts = from_left(ah, al, jnp.concatenate(waves, axis=1))
        sides = jnp.concatenate(
            [
                jnp.concatenate([lefts[:PROBE, i * NZ : (i + 1) * NZ], lefts[PROBE:, i * NZ : (i + 1) * NZ]], axis=1)
                for i in range(2)
            ],
            axis=0,
        )
        far = from_right(sides, bh, bl)
        far_re = far[:, :NZ]
        far_im = far[:, NZ:]
        modulus = jnp.sqrt(far_re * far_re + far_im * far_im)
        intensity = measured_ref[2 * pair : 2 * pair + 2].reshape(2 * PROBE, NZ)
        shrink = 1.0 - jnp.sqrt(intensity) / jnp.maximum(modulus, 1.0)
        diff = jnp.concatenate([far_re * shrink, far_im * shrink], axis=1)
        half = from_right(diff, ah, al)
        stacked = jnp.concatenate(
            [
                jnp.concatenate([half[i * PROBE : (i + 1) * PROBE, :NZ], half[i * PROBE : (i + 1) * PROBE, NZ:]], axis=0)
                for i in range(2)
            ],
            axis=1,
        )
        backs = from_left(bh, bl, stacked)
        for i in range(2):
            back_re = backs[:PROBE, i * NZ : (i + 1) * NZ]
            back_im = backs[PROBE:, i * NZ : (i + 1) * NZ]
            rows = pl.ds(starts_ref[0, 2 * pair + i], PROBE)
            total_re[rows, :] += probe_re * back_re + probe_im * back_im
            total_im[rows, :] += probe_re * back_im - probe_im * back_re
    for ahead in range(Y):
        owner = lax.rem(y + ahead, Y)
        for tile in range(0, NR, 2):
            low = pl.ds(pl.multiple_of(tile * RAYS + owner * QR, QR), QR)
            high = pl.ds(pl.multiple_of((tile + 1) * RAYS + owner * QR, QR), QR)
            rows = slice(tile * QR, (tile + 2) * QR)
            for part, total in enumerate((total_re, total_im)):
                piece = jnp.concatenate([total[low, :], total[high, :]], axis=0)
                if ahead == 0:
                    own_ref[part, rows, :] = piece
                else:
                    (sent_one, sent_two, sent_three)[ahead - 1][part, rows, :] = piece.astype(bf16)


def shifted(value, axis, length, step):
    return lax.ppermute(value, axis, [(i, (i + step) % length) for i in range(length)])


def across(value):
    return shifted(value, "zh", ZH, 1)


def round_y(pieces):
    return [pieces[0]] + [shifted(pieces[k], "y", Y, k) for k in range(1, Y)]


def body(measured, positions, probe_field, object_field, dual_field, volume, radon_tiles, tile_range):
    zh = lax.axis_index("zh")
    zl = lax.axis_index("zl")
    y = lax.axis_index("y")
    place = jnp.stack([zh, y, zl]).astype(jnp.int32)
    ah, al, bh, bl = dft_blocks()
    radon = radon_tiles.reshape(ZL * XC, HITS, RAYS, TILE)
    volume_rows = volume.reshape(2 * TILE, NZ)
    object_rows = object_field.reshape(128, NZ)
    dual_rows = dual_field.reshape(128, NZ)

    with jax.named_scope("ray_sums"):
        object_theirs = across(object_rows)
        sums = call(
            ray_sums,
            shape(NEAR, ZL, HITS * QR, 2 * NZ, dtype=bf16),
            0,
            0,
            n_far=2,
            scratch=[pltpu.VMEM(radon.shape, bf16), pltpu.VMEM((2 * TILE, NZ), f32), pltpu.SemaphoreType.DMA((ZL + 1,))],
            flops=2 * 2048 * 256 * 256,
            limit=SUMS_LIMIT,
        )(radon, volume_rows)
        near_sums = lax.all_to_all(sums, CROSS, 0, 0, tiled=True)

    with jax.named_scope("fields"):
        object_theirs, sums = lax.optimization_barrier((object_theirs, sums))
        packed = call(
            pack, (shape(SENT_ROWS, NZ),) * Y, 1, 4, scratch=[pltpu.VMEM((128, NZ), f32)], flops=1_000_000
        )(place, object_rows, object_theirs, dual_rows, tile_range.reshape(1, ZL * XC))
        fields = round_y(packed)

    with jax.named_scope("frames"):
        inter_parts = call(
            frame_gradients,
            (shape(2, 128, NZ),) + (shape(2, 128, NZ, dtype=bf16),) * 3,
            2,
            10,
            scratch=[pltpu.VMEM((NDET, NZ), f32)] * 4,
            flops=FRAMES_COST,
        )(place, positions, *fields, probe_field, measured[0], ah, al, bh, bl)

    with jax.named_scope("targets"):
        tables = jnp.concatenate([field[FIELD_ROWS + DRIFT_ROWS :][:1, : ZL * XC] for field in fields])
        tables, inter_parts = lax.optimization_barrier((tables.astype(jnp.int32), inter_parts))
        tables = jnp.concatenate([tables] + [shifted(tables, "zl", ZL, k) for k in range(1, ZL)])

    with jax.named_scope("frames"):
        inter_parts = round_y(inter_parts)

    with jax.named_scope("near_sum"):
        dense, inter = call(
            add_tiles,
            (shape(DEEP, 128, NZ, dtype=bf16), shape(2, 128, NZ)),
            2,
            9,
            scratch=[pltpu.VMEM((ZL, 128, 2 * NZ), f32)],
            flops=1_000_000,
        )(place, tables, near_sums, *inter_parts, *fields)
        far_sums = lax.all_to_all(dense, ALONG, 0, 0, tiled=True)

    with jax.named_scope("residual"):
        copies, *kept = call(
            residual_part,
            (shape(DEEP, 128, NZ, dtype=bf16),) + (shape(ZH, 3, 2 * QR, NZ),) * Y,
            1,
            2,
            scratch=[pltpu.VMEM((128, NZ), f32)],
            flops=1_000_000,
        )(place, far_sums, inter)
        kept = round_y(kept)
        residuals = lax.all_to_all(copies, ALONG, 0, 0, tiled=True)

    with jax.named_scope("pick"):
        picked = call(
            pick_tiles,
            shape(NEAR, ZL, HITS * QR, 2 * NZ, dtype=bf16),
            2,
            1,
            scratch=[pltpu.VMEM((ZL, 128, 2 * NZ), f32)],
            flops=1_000_000,
        )(place, tables, residuals)
        picked, kept = lax.optimization_barrier((picked, kept))
        returned = lax.all_to_all(picked, CROSS, 0, 0, tiled=True)

    with jax.named_scope("updates"):
        theirs = across(jnp.stack([piece[1] for piece in kept]))
        object_next, dual_next = call(updates, (shape(128, NZ), shape(128, NZ)), 1, 7, flops=1_000_000)(
            place, *kept, theirs, object_rows, dual_rows
        )

    with jax.named_scope("back_project"):
        ordered = radon.reshape(ZL, XC, HITS, Y, QR, TILE).transpose(5, 1, 3, 0, 2, 4).reshape(TILE, -1)
        volume_next = call(back_project, shape(2 * TILE, NZ), 0, 3, flops=2 * 2048 * 256 * 256)(
            ordered, returned, volume_rows
        )
    return (
        object_next.reshape(object_field.shape),
        dual_next.reshape(dual_field.shape),
        volume_next.reshape(volume.shape),
    )


def solution(mesh):
    fine = Mesh(mesh.devices.reshape(ZL, X, C, ZH, Y), ("zl", "x", "c", "zh", "y"))
    ang = ("zl", "x", "c")
    strip = ("zh", "y")
    return jax.shard_map(
        body,
        mesh=fine,
        in_specs=(
            P(ang, strip, None, None),
            P(ang, strip),
            P(),
            P(ang, strip, None, None),
            P(ang, strip, None, None),
            P(ang + strip, None, None),
            P(ang + strip, None, None, None, None),
            P(ang, None, strip, None),
        ),
        out_specs=(
            P(ang, strip, None, None),
            P(ang, strip, None, None),
            P(ang + strip, None, None),
        ),
        check_vma=False,
    )
```

```python
import math

import jax
import jax.numpy as jnp
import numpy as np
from jax import lax
from jax.experimental import pallas as pl
from jax.experimental.pallas import tpu as pltpu
from jax.sharding import Mesh
from jax.sharding import PartitionSpec as P

PROBE = 128
NZ = 128
NDET = 512
RAYS = 32
TILE = 256
HITS = 2
NR = 16

ZL, X, C, ZH, Y = 4, 4, 2, 2, 4
XC = X * C
CROSS = ("x", "c", "y")
ALONG = ("zh", "zl")
NEAR = XC * Y
DEEP = ZH * ZL
QR = RAYS // Y
FR_DEV = 8
FRAMES_COST = 20_000_000_000
SUMS_LIMIT = 62 << 20

penalty = 1.0
object_step = 0.1
volume_step = 1.0
keep = 1.0 - object_step
share = object_step / keep
f32 = jnp.float32
bf16 = jnp.bfloat16

VM = pl.BlockSpec(memory_space=pltpu.VMEM)
SM = pl.BlockSpec(memory_space=pltpu.SMEM)
FAR = pl.BlockSpec(memory_space=pltpu.HBM)


def call(kernel, outs, n_smem, n_vmem, scratch=(), flops=0, moved=1 << 20, limit=48 << 20, n_far=0):
    many = isinstance(outs, tuple)
    return pl.pallas_call(
        kernel,
        out_shape=outs,
        in_specs=[SM] * n_smem + [FAR] * n_far + [VM] * n_vmem,
        out_specs=tuple(VM for _ in outs) if many else VM,
        scratch_shapes=list(scratch),
        compiler_params=pltpu.CompilerParams(vmem_limit_bytes=limit),
        cost_estimate=pl.CostEstimate(flops=flops, bytes_accessed=moved, transcendentals=0),
        name=kernel.__name__,
    )


def shape(*dims, dtype=f32):
    return jax.ShapeDtypeStruct(dims, dtype)


def dft_blocks():
    k = np.arange(PROBE)
    angles = (k[:, None] * k[None, :] % PROBE) * (2.0 * math.pi / PROBE)
    cosine = np.cos(angles) / math.sqrt(PROBE)
    sine = np.sin(angles) / math.sqrt(PROBE)
    left = np.block([[cosine, sine], [-sine, cosine]]).astype(np.float32)
    high = left.astype(jnp.bfloat16)
    low = (left - high.astype(np.float32)).astype(jnp.bfloat16)
    return jnp.asarray(high), jnp.asarray(low), jnp.asarray(high.T.copy()), jnp.asarray(low.T.copy())


def ray_sums(radon_far, volume_far, out_ref, radon_ref, volume_ref, sems):
    copies = [pltpu.make_async_copy(volume_far, volume_ref, sems.at[ZL])]
    for zl in range(ZL):
        angles = pl.ds(zl * XC, XC)
        copies.append(pltpu.make_async_copy(radon_far.at[angles], radon_ref.at[angles], sems.at[zl]))
    for copy in copies:
        copy.start()
    copies[0].wait()
    volume_half = jnp.concatenate(
        [volume_ref[pl.ds(0, TILE, stride=2), :], volume_ref[pl.ds(1, TILE, stride=2), :]], axis=1
    ).astype(bf16)
    for zl in range(ZL):
        copies[1 + zl].wait()
        for xc in range(XC):
            rows = radon_ref[zl * XC + xc].reshape(HITS * RAYS, TILE)
            sums = jnp.dot(rows, volume_half, preferred_element_type=f32)
            for y in range(Y):
                low = sums[y * QR : (y + 1) * QR]
                high = sums[RAYS + y * QR : RAYS + (y + 1) * QR]
                out_ref[xc * Y + y, zl] = jnp.concatenate([low, high], axis=0).astype(bf16)


def first_rows(place_ref, target_ref):
    zl_here = place_ref[2]
    back_y = [lax.rem(place_ref[1] + Y - y, Y) for y in range(Y)]
    back_zl = [lax.rem(zl_here + ZL - zl, ZL) * Y for zl in range(ZL)]

    def row(zl, y, xc):
        return pl.multiple_of(target_ref[back_y[y] + back_zl[zl], zl_here * XC + xc] * QR, QR)

    return row


def add_tiles(
    place_ref, target_ref, sums_ref, inter_0, inter_1, inter_2, inter_3, field_0, field_1, field_2, field_3,
    out_ref, inter_ref, total,
):
    zh = place_ref[0]
    y_here = place_ref[1]
    zl_here = place_ref[2]
    row = first_rows(place_ref, target_ref)
    total[...] = jnp.zeros(total.shape, f32)
    for part in range(2):
        inter = (inter_0[part] + inter_1[part].astype(f32)) + (inter_2[part].astype(f32) + inter_3[part].astype(f32))
        inter_ref[part] = inter
        total[zl_here, :, part * NZ : (part + 1) * NZ] = inter * share
    for back, field_ref in enumerate((field_0, field_1, field_2, field_3)):
        owner = zh * Y + lax.rem(y_here + Y - back, Y)
        rows = pl.ds(pl.multiple_of(owner * 2 * QR, 2 * QR), 2 * QR)
        base = FIELD_ROWS
        total[zl_here, rows, :] -= jnp.concatenate(
            [field_ref[base : base + 2 * QR, :], field_ref[base + 2 * QR : base + 4 * QR, :]], axis=1
        )
    for xc in range(XC):
        for y in range(Y):
            for zl in range(ZL):
                total[zl, pl.ds(row(zl, y, xc), HITS * QR), :] += sums_ref[xc * Y + y, zl].astype(f32)
    for zh in range(ZH):
        for zl in range(ZL):
            out_ref[zh * ZL + zl] = total[zl, :, zh * NZ : (zh + 1) * NZ].astype(bf16)


def residual_part(place_ref, sums_ref, inter_ref, residual_ref, own_ref, one_ref, two_ref, three_ref, joint):
    zh = place_ref[0]
    y = place_ref[1]
    total = sums_ref[0].astype(f32)
    for source in range(1, DEEP):
        total = total + sums_ref[source].astype(f32)
    joint[...] = total
    residual = (keep * total).astype(bf16)
    for copy in range(DEEP):
        residual_ref[copy] = residual
    for ahead, ref in enumerate((own_ref, one_ref, two_ref, three_ref)):
        for other in range(ZH):
            owner = lax.rem(zh + other, ZH) * Y + lax.rem(y + ahead, Y)
            rows = pl.ds(pl.multiple_of(owner * 2 * QR, 2 * QR), 2 * QR)
            ref[other, 0] = joint[rows, :]
            for part in range(2):
                ref[other, 1 + part] = inter_ref[part, rows, :]


def pick_tiles(place_ref, target_ref, residual_ref, out_ref, rows_ref):
    for zl in range(ZL):
        rows_ref[zl] = jnp.concatenate(
            [residual_ref[zl].astype(f32), residual_ref[ZL + zl].astype(f32)], axis=1
        )

    row = first_rows(place_ref, target_ref)
    for xc in range(XC):
        for y in range(Y):
            for zl in range(ZL):
                out_ref[xc * Y + y, zl] = rows_ref[zl, pl.ds(row(zl, y, xc), HITS * QR), :].astype(bf16)


def back_project(radon_ref, picked_ref, volume_ref, out_ref):
    gradient = jnp.dot(
        radon_ref[...],
        picked_ref[...].reshape(NEAR * ZL * HITS * QR, 2 * NZ),
        preferred_element_type=f32,
    )
    for part in range(2):
        rows = pl.ds(part, TILE, stride=2)
        out_ref[rows, :] = volume_ref[rows, :] - volume_step * gradient[:, part * NZ : (part + 1) * NZ]


def updates(
    place_ref, own_ref, one_ref, two_ref, three_ref, theirs_ref, object_ref, dual_ref, object_out, dual_out
):
    zh = place_ref[0]
    y = place_ref[1]
    for back, ref in enumerate((own_ref, one_ref, two_ref, three_ref)):
        source = lax.rem(y + Y - back, Y)
        for other in range(ZH):
            part = lax.rem(zh + other, ZH)
            for tile in range(2):
                piece = slice(tile * QR, (tile + 1) * QR)
                inter = ref[0, 1 + part, piece, :] + theirs_ref[back, 1 + part, piece, :]
                joint = theirs_ref[back, 0, piece, :] if other else ref[0, 0, piece, :]
                rows = pl.ds((tile * RAYS + source * QR) * 2 + part, QR, stride=2)
                field = object_ref[rows, :]
                dual = dual_ref[rows, :]
                projection = joint + (field + dual) - share * inter
                object_next = field - object_step * (inter + dual + penalty * (field - projection))
                object_out[rows, :] = object_next
                dual_out[rows, :] = dual + penalty * (object_next - projection)


def split(value):
    high = value.astype(bf16)
    return high, (value - high.astype(f32)).astype(bf16)


def from_left(high_table, low_table, value):
    high, low = split(value)
    return (
        jnp.dot(high_table, high, preferred_element_type=f32)
        + jnp.dot(high_table, low, preferred_element_type=f32)
        + jnp.dot(low_table, high, preferred_element_type=f32)
    )


def from_right(value, high_table, low_table):
    high, low = split(value)
    return (
        jnp.dot(high, high_table, preferred_element_type=f32)
        + jnp.dot(low, high_table, preferred_element_type=f32)
        + jnp.dot(high, low_table, preferred_element_type=f32)
    )


FIELD_ROWS = 2 * 128
DRIFT_ROWS = 4 * QR
SENT_ROWS = FIELD_ROWS + DRIFT_ROWS + QR


def pack(place_ref, object_ref, theirs_ref, dual_ref, target_ref, own_ref, one_ref, two_ref, three_ref, both):
    y = place_ref[1]
    targets = target_ref[...].astype(f32)
    both[...] = object_ref[...] + dual_ref[...]
    for ahead, ref in enumerate((own_ref, one_ref, two_ref, three_ref)):
        ref[0:128, :] = object_ref[...]
        ref[128:256, :] = theirs_ref[...]
        ref[FIELD_ROWS + DRIFT_ROWS :, :] = jnp.zeros((QR, NZ), f32)
        ref[FIELD_ROWS + DRIFT_ROWS : FIELD_ROWS + DRIFT_ROWS + 1, : ZL * XC] = targets
        for part in range(2):
            for tile in range(2):
                start = (tile * RAYS + lax.rem(y + ahead, Y) * QR) * 2 + part
                base = FIELD_ROWS + (part * 2 + tile) * QR
                ref[base : base + QR, :] = both[pl.ds(start, QR, stride=2), :]


def frame_gradients(
    place_ref, starts_ref, field_0, field_1, field_2, field_3, probe_ref,
    measured_ref, ah_ref, al_ref, bh_ref, bl_ref, own_ref, sent_one, sent_two, sent_three,
    field_re, field_im, total_re, total_im,
):
    zh = place_ref[0]
    y = place_ref[1]
    for back, field_ref in enumerate((field_0, field_1, field_2, field_3)):
        for other in range(ZH):
            owner = lax.rem(zh + other, ZH) * Y + lax.rem(y + Y - back, Y)
            rows = pl.ds(pl.multiple_of(owner * 64, 64), 64)
            field_re[rows, :] = field_ref[pl.ds(other * 128, 64, stride=2), :]
            field_im[rows, :] = field_ref[pl.ds(other * 128 + 1, 64, stride=2), :]
    total_re[...] = jnp.zeros(total_re.shape, f32)
    total_im[...] = jnp.zeros(total_im.shape, f32)
    probe_re = probe_ref[0]
    probe_im = probe_ref[1]
    ah, al, bh, bl = ah_ref[...], al_ref[...], bh_ref[...], bl_ref[...]
    for pair in range(FR_DEV // 2):
        waves = []
        for frame in (2 * pair, 2 * pair + 1):
            rows = pl.ds(starts_ref[0, frame], PROBE)
            object_re = field_re[rows, :]
            object_im = field_im[rows, :]
            waves.append(
                jnp.concatenate(
                    [
                        probe_re * object_re - probe_im * object_im,
                        probe_re * object_im + probe_im * object_re,
                    ],
                    axis=0,
                )
            )
        lefts = from_left(ah, al, jnp.concatenate(waves, axis=1))
        sides = jnp.concatenate(
            [
                jnp.concatenate([lefts[:PROBE, i * NZ : (i + 1) * NZ], lefts[PROBE:, i * NZ : (i + 1) * NZ]], axis=1)
                for i in range(2)
            ],
            axis=0,
        )
        far = from_right(sides, bh, bl)
        far_re = far[:, :NZ]
        far_im = far[:, NZ:]
        modulus = jnp.sqrt(far_re * far_re + far_im * far_im)
        intensity = measured_ref[2 * pair : 2 * pair + 2].reshape(2 * PROBE, NZ)
        shrink = 1.0 - jnp.sqrt(intensity) / jnp.maximum(modulus, 1.0)
        diff = jnp.concatenate([far_re * shrink, far_im * shrink], axis=1)
        half = from_right(diff, ah, al)
        stacked = jnp.concatenate(
            [
                jnp.concatenate([half[i * PROBE : (i + 1) * PROBE, :NZ], half[i * PROBE : (i + 1) * PROBE, NZ:]], axis=0)
                for i in range(2)
            ],
            axis=1,
        )
        backs = from_left(bh, bl, stacked)
        for i in range(2):
            back_re = backs[:PROBE, i * NZ : (i + 1) * NZ]
            back_im = backs[PROBE:, i * NZ : (i + 1) * NZ]
            rows = pl.ds(starts_ref[0, 2 * pair + i], PROBE)
            total_re[rows, :] += probe_re * back_re + probe_im * back_im
            total_im[rows, :] += probe_re * back_im - probe_im * back_re
    for ahead in range(Y):
        owner = lax.rem(y + ahead, Y)
        for tile in range(0, NR, 2):
            low = pl.ds(pl.multiple_of(tile * RAYS + owner * QR, QR), QR)
            high = pl.ds(pl.multiple_of((tile + 1) * RAYS + owner * QR, QR), QR)
            rows = slice(tile * QR, (tile + 2) * QR)
            for part, total in enumerate((total_re, total_im)):
                piece = jnp.concatenate([total[low, :], total[high, :]], axis=0)
                if ahead == 0:
                    own_ref[part, rows, :] = piece
                else:
                    (sent_one, sent_two, sent_three)[ahead - 1][part, rows, :] = piece.astype(bf16)


def shifted(value, axis, length, step):
    return lax.ppermute(value, axis, [(i, (i + step) % length) for i in range(length)])


def across(value):
    return shifted(value, "zh", ZH, 1)


def round_y(pieces):
    return [pieces[0]] + [shifted(pieces[k], "y", Y, k) for k in range(1, Y)]


def body(measured, positions, probe_field, object_field, dual_field, volume, radon_tiles, tile_range):
    zh = lax.axis_index("zh")
    zl = lax.axis_index("zl")
    y = lax.axis_index("y")
    place = jnp.stack([zh, y, zl]).astype(jnp.int32)
    ah, al, bh, bl = dft_blocks()
    radon = radon_tiles.reshape(ZL * XC, HITS, RAYS, TILE)
    volume_rows = volume.reshape(2 * TILE, NZ)
    object_rows = object_field.reshape(128, NZ)
    dual_rows = dual_field.reshape(128, NZ)

    with jax.named_scope("ray_sums"):
        object_theirs = across(object_rows)
        sums = call(
            ray_sums,
            shape(NEAR, ZL, HITS * QR, 2 * NZ, dtype=bf16),
            0,
            0,
            n_far=2,
            scratch=[pltpu.VMEM(radon.shape, bf16), pltpu.VMEM((2 * TILE, NZ), f32), pltpu.SemaphoreType.DMA((ZL + 1,))],
            flops=2 * 2048 * 256 * 256,
            limit=SUMS_LIMIT,
        )(radon, volume_rows)
        near_sums = lax.all_to_all(sums, CROSS, 0, 0, tiled=True)

    with jax.named_scope("fields"):
        object_theirs, sums = lax.optimization_barrier((object_theirs, sums))
        packed = call(
            pack, (shape(SENT_ROWS, NZ),) * Y, 1, 4, scratch=[pltpu.VMEM((128, NZ), f32)], flops=1_000_000
        )(place, object_rows, object_theirs, dual_rows, tile_range.reshape(1, ZL * XC))
        fields = round_y(packed)

    with jax.named_scope("frames"):
        inter_parts = call(
            frame_gradients,
            (shape(2, 128, NZ),) + (shape(2, 128, NZ, dtype=bf16),) * 3,
            2,
            10,
            scratch=[pltpu.VMEM((NDET, NZ), f32)] * 4,
            flops=FRAMES_COST,
        )(place, positions, *fields, probe_field, measured[0], ah, al, bh, bl)

    with jax.named_scope("targets"):
        tables = jnp.concatenate([field[FIELD_ROWS + DRIFT_ROWS :][:1, : ZL * XC] for field in fields])
        tables, inter_parts = lax.optimization_barrier((tables.astype(jnp.int32), inter_parts))
        tables = jnp.concatenate([tables] + [shifted(tables, "zl", ZL, k) for k in range(1, ZL)])

    with jax.named_scope("frames"):
        inter_parts = round_y(inter_parts)

    with jax.named_scope("near_sum"):
        dense, inter = call(
            add_tiles,
            (shape(DEEP, 128, NZ, dtype=bf16), shape(2, 128, NZ)),
            2,
            9,
            scratch=[pltpu.VMEM((ZL, 128, 2 * NZ), f32)],
            flops=1_000_000,
        )(place, tables, near_sums, *inter_parts, *fields)
        far_sums = lax.all_to_all(dense, ALONG, 0, 0, tiled=True)

    with jax.named_scope("residual"):
        copies, *kept = call(
            residual_part,
            (shape(DEEP, 128, NZ, dtype=bf16),) + (shape(ZH, 3, 2 * QR, NZ),) * Y,
            1,
            2,
            scratch=[pltpu.VMEM((128, NZ), f32)],
            flops=1_000_000,
        )(place, far_sums, inter)
        kept = round_y(kept)
        residuals = lax.all_to_all(copies, ALONG, 0, 0, tiled=True)

    with jax.named_scope("pick"):
        picked = call(
            pick_tiles,
            shape(NEAR, ZL, HITS * QR, 2 * NZ, dtype=bf16),
            2,
            1,
            scratch=[pltpu.VMEM((ZL, 128, 2 * NZ), f32)],
            flops=1_000_000,
        )(place, tables, residuals)
        picked, kept = lax.optimization_barrier((picked, kept))
        returned = lax.all_to_all(picked, CROSS, 0, 0, tiled=True)

    with jax.named_scope("updates"):
        theirs = across(jnp.stack([piece[1] for piece in kept]))
        object_next, dual_next = call(updates, (shape(128, NZ), shape(128, NZ)), 1, 7, flops=1_000_000)(
            place, *kept, theirs, object_rows, dual_rows
        )

    with jax.named_scope("back_project"):
        ordered = radon.reshape(ZL, XC, HITS, Y, QR, TILE).transpose(5, 1, 3, 0, 2, 4).reshape(TILE, -1)
        volume_next = call(back_project, shape(2 * TILE, NZ), 0, 3, flops=2 * 2048 * 256 * 256)(
            ordered, returned, volume_rows
        )
    return (
        object_next.reshape(object_field.shape),
        dual_next.reshape(dual_field.shape),
        volume_next.reshape(volume.shape),
    )


def solution(mesh):
    fine = Mesh(mesh.devices.reshape(ZL, X, C, ZH, Y), ("zl", "x", "c", "zh", "y"))
    ang = ("zl", "x", "c")
    strip = ("zh", "y")
    return jax.shard_map(
        body,
        mesh=fine,
        in_specs=(
            P(ang, strip, None, None),
            P(ang, strip),
            P(),
            P(ang, strip, None, None),
            P(ang, strip, None, None),
            P(ang + strip, None, None),
            P(ang + strip, None, None, None, None),
            P(ang, None, strip, None),
        ),
        out_specs=(
            P(ang, strip, None, None),
            P(ang, strip, None, None),
            P(ang + strip, None, None),
        ),
        check_vma=False,
    )
```

```python
import math

import jax
import jax.numpy as jnp
import numpy as np
from jax import lax
from jax.experimental import pallas as pl
from jax.experimental.pallas import tpu as pltpu
from jax.sharding import Mesh
from jax.sharding import PartitionSpec as P

PROBE = 128
NZ = 128
NDET = 512
RAYS = 32
TILE = 256
HITS = 2
NR = 16

ZL, X, C, ZH, Y = 4, 4, 2, 2, 4
XC = X * C
CROSS = ("x", "c", "y")
ALONG = ("zh", "zl")
NEAR = XC * Y
DEEP = ZH * ZL
QR = RAYS // Y
FR_DEV = 8
FRAMES_COST = 20_000_000_000
SUMS_LIMIT = 62 << 20

penalty = 1.0
object_step = 0.1
volume_step = 1.0
keep = 1.0 - object_step
share = object_step / keep
f32 = jnp.float32
bf16 = jnp.bfloat16

VM = pl.BlockSpec(memory_space=pltpu.VMEM)
SM = pl.BlockSpec(memory_space=pltpu.SMEM)
FAR = pl.BlockSpec(memory_space=pltpu.HBM)


def call(kernel, outs, n_smem, n_vmem, scratch=(), flops=0, moved=1 << 20, limit=48 << 20, n_far=0):
    many = isinstance(outs, tuple)
    return pl.pallas_call(
        kernel,
        out_shape=outs,
        in_specs=[SM] * n_smem + [FAR] * n_far + [VM] * n_vmem,
        out_specs=tuple(VM for _ in outs) if many else VM,
        scratch_shapes=list(scratch),
        compiler_params=pltpu.CompilerParams(vmem_limit_bytes=limit),
        cost_estimate=pl.CostEstimate(flops=flops, bytes_accessed=moved, transcendentals=0),
        name=kernel.__name__,
    )


def shape(*dims, dtype=f32):
    return jax.ShapeDtypeStruct(dims, dtype)


def dft_blocks():
    k = np.arange(PROBE)
    angles = (k[:, None] * k[None, :] % PROBE) * (2.0 * math.pi / PROBE)
    cosine = np.cos(angles) / math.sqrt(PROBE)
    sine = np.sin(angles) / math.sqrt(PROBE)
    left = np.block([[cosine, sine], [-sine, cosine]]).astype(np.float32)
    high = left.astype(jnp.bfloat16)
    low = (left - high.astype(np.float32)).astype(jnp.bfloat16)
    return jnp.asarray(high), jnp.asarray(low), jnp.asarray(high.T.copy()), jnp.asarray(low.T.copy())


def ray_sums(radon_far, volume_far, out_ref, radon_ref, volume_ref, sems):
    copies = [pltpu.make_async_copy(volume_far, volume_ref, sems.at[ZL])]
    for zl in range(ZL):
        angles = pl.ds(zl * XC, XC)
        copies.append(pltpu.make_async_copy(radon_far.at[angles], radon_ref.at[angles], sems.at[zl]))
    for copy in copies:
        copy.start()
    copies[0].wait()
    volume_half = jnp.concatenate(
        [volume_ref[pl.ds(0, TILE, stride=2), :], volume_ref[pl.ds(1, TILE, stride=2), :]], axis=1
    ).astype(bf16)
    for zl in range(ZL):
        copies[1 + zl].wait()
        for xc in range(XC):
            rows = radon_ref[zl * XC + xc].reshape(HITS * RAYS, TILE)
            sums = jnp.dot(rows, volume_half, preferred_element_type=f32)
            for y in range(Y):
                low = sums[y * QR : (y + 1) * QR]
                high = sums[RAYS + y * QR : RAYS + (y + 1) * QR]
                out_ref[xc * Y + y, zl] = jnp.concatenate([low, high], axis=0).astype(bf16)


def first_rows(place_ref, target_ref):
    zl_here = place_ref[2]
    back_y = [lax.rem(place_ref[1] + Y - y, Y) * ZL for y in range(Y)]
    back_zl = [lax.rem(zl_here + ZL - zl, ZL) for zl in range(ZL)]

    def row(zl, y, xc):
        return pl.multiple_of(target_ref[back_y[y] + back_zl[zl], zl_here * XC + xc] * QR, QR)

    return row


def add_tiles(
    place_ref, target_ref, sums_ref, inter_0, inter_1, inter_2, inter_3, field_0, field_1, field_2, field_3,
    out_ref, inter_ref, total,
):
    zh = place_ref[0]
    y_here = place_ref[1]
    zl_here = place_ref[2]
    row = first_rows(place_ref, target_ref)
    total[...] = jnp.zeros(total.shape, f32)
    for part in range(2):
        inter = (inter_0[part] + inter_1[part].astype(f32)) + (inter_2[part].astype(f32) + inter_3[part].astype(f32))
        inter_ref[part] = inter
        total[zl_here, :, part * NZ : (part + 1) * NZ] = inter * share
    for back, field_ref in enumerate((field_0, field_1, field_2, field_3)):
        owner = zh * Y + lax.rem(y_here + Y - back, Y)
        rows = pl.ds(pl.multiple_of(owner * 2 * QR, 2 * QR), 2 * QR)
        base = FIELD_ROWS
        total[zl_here, rows, :] -= jnp.concatenate(
            [field_ref[base : base + 2 * QR, :], field_ref[base + 2 * QR : base + 4 * QR, :]], axis=1
        )
    for xc in range(XC):
        for y in range(Y):
            for zl in range(ZL):
                total[zl, pl.ds(row(zl, y, xc), HITS * QR), :] += sums_ref[xc * Y + y, zl].astype(f32)
    for zh in range(ZH):
        for zl in range(ZL):
            out_ref[zh * ZL + zl] = total[zl, :, zh * NZ : (zh + 1) * NZ].astype(bf16)


def residual_part(sums_ref, residual_ref, joint_ref):
    total = sums_ref[0].astype(f32)
    for source in range(1, DEEP):
        total = total + sums_ref[source].astype(f32)
    joint_ref[...] = total
    residual = (keep * total).astype(bf16)
    for copy in range(DEEP):
        residual_ref[copy] = residual


def share_out(place_ref, joint_ref, inter_ref, own_ref, one_ref, two_ref, three_ref):
    zh = place_ref[0]
    y = place_ref[1]
    for ahead, ref in enumerate((own_ref, one_ref, two_ref, three_ref)):
        for other in range(ZH):
            owner = lax.rem(zh + other, ZH) * Y + lax.rem(y + ahead, Y)
            rows = pl.ds(pl.multiple_of(owner * 2 * QR, 2 * QR), 2 * QR)
            ref[other, 0] = joint_ref[rows, :]
            for part in range(2):
                ref[other, 1 + part] = inter_ref[part, rows, :]


def pick_tiles(place_ref, target_ref, residual_ref, out_ref, rows_ref):
    for zl in range(ZL):
        rows_ref[zl] = jnp.concatenate(
            [residual_ref[zl].astype(f32), residual_ref[ZL + zl].astype(f32)], axis=1
        )

    row = first_rows(place_ref, target_ref)
    for xc in range(XC):
        for y in range(Y):
            for zl in range(ZL):
                out_ref[xc * Y + y, zl] = rows_ref[zl, pl.ds(row(zl, y, xc), HITS * QR), :].astype(bf16)


def back_project(radon_ref, picked_ref, volume_ref, out_ref):
    gradient = jnp.dot(
        radon_ref[...],
        picked_ref[...].reshape(NEAR * ZL * HITS * QR, 2 * NZ),
        preferred_element_type=f32,
    )
    for part in range(2):
        rows = pl.ds(part, TILE, stride=2)
        out_ref[rows, :] = volume_ref[rows, :] - volume_step * gradient[:, part * NZ : (part + 1) * NZ]


def updates(
    place_ref, own_ref, one_ref, two_ref, three_ref, theirs_ref, object_ref, dual_ref, object_out, dual_out
):
    zh = place_ref[0]
    y = place_ref[1]
    for back, ref in enumerate((own_ref, one_ref, two_ref, three_ref)):
        source = lax.rem(y + Y - back, Y)
        for other in range(ZH):
            part = lax.rem(zh + other, ZH)
            for tile in range(2):
                piece = slice(tile * QR, (tile + 1) * QR)
                inter = ref[0, 1 + part, piece, :] + theirs_ref[back, 1 + part, piece, :]
                joint = theirs_ref[back, 0, piece, :] if other else ref[0, 0, piece, :]
                rows = pl.ds((tile * RAYS + source * QR) * 2 + part, QR, stride=2)
                field = object_ref[rows, :]
                dual = dual_ref[rows, :]
                projection = joint + (field + dual) - share * inter
                object_next = field - object_step * (inter + dual + penalty * (field - projection))
                object_out[rows, :] = object_next
                dual_out[rows, :] = dual + penalty * (object_next - projection)


def split(value):
    high = value.astype(bf16)
    return high, (value - high.astype(f32)).astype(bf16)


def from_left(high_table, low_table, value):
    high, low = split(value)
    return (
        jnp.dot(high_table, high, preferred_element_type=f32)
        + jnp.dot(high_table, low, preferred_element_type=f32)
        + jnp.dot(low_table, high, preferred_element_type=f32)
    )


def from_right(value, high_table, low_table):
    high, low = split(value)
    return (
        jnp.dot(high, high_table, preferred_element_type=f32)
        + jnp.dot(low, high_table, preferred_element_type=f32)
        + jnp.dot(high, low_table, preferred_element_type=f32)
    )


FIELD_ROWS = 2 * 128
DRIFT_ROWS = 4 * QR
SENT_ROWS = FIELD_ROWS + DRIFT_ROWS + QR


def pack(place_ref, object_ref, theirs_ref, dual_ref, target_ref, own_ref, one_ref, two_ref, three_ref, both):
    y = place_ref[1]
    both[...] = object_ref[...] + dual_ref[...]
    for ahead, ref in enumerate((own_ref, one_ref, two_ref, three_ref)):
        ref[0:128, :] = object_ref[...]
        ref[128:256, :] = theirs_ref[...]
        ref[FIELD_ROWS + DRIFT_ROWS :, :] = target_ref[...]
        for part in range(2):
            for tile in range(2):
                start = (tile * RAYS + lax.rem(y + ahead, Y) * QR) * 2 + part
                base = FIELD_ROWS + (part * 2 + tile) * QR
                ref[base : base + QR, :] = both[pl.ds(start, QR, stride=2), :]


def frame_gradients(
    place_ref, starts_ref, field_0, field_1, field_2, field_3, probe_ref,
    measured_ref, ah_ref, al_ref, bh_ref, bl_ref, own_ref, sent_one, sent_two, sent_three,
    field_re, field_im, total_re, total_im,
):
    zh = place_ref[0]
    y = place_ref[1]
    for back, field_ref in enumerate((field_0, field_1, field_2, field_3)):
        for other in range(ZH):
            owner = lax.rem(zh + other, ZH) * Y + lax.rem(y + Y - back, Y)
            rows = pl.ds(pl.multiple_of(owner * 64, 64), 64)
            field_re[rows, :] = field_ref[pl.ds(other * 128, 64, stride=2), :]
            field_im[rows, :] = field_ref[pl.ds(other * 128 + 1, 64, stride=2), :]
    total_re[...] = jnp.zeros(total_re.shape, f32)
    total_im[...] = jnp.zeros(total_im.shape, f32)
    probe_re = probe_ref[0]
    probe_im = probe_ref[1]
    ah, al, bh, bl = ah_ref[...], al_ref[...], bh_ref[...], bl_ref[...]
    for pair in range(FR_DEV // 2):
        waves = []
        for frame in (2 * pair, 2 * pair + 1):
            rows = pl.ds(starts_ref[0, frame], PROBE)
            object_re = field_re[rows, :]
            object_im = field_im[rows, :]
            waves.append(
                jnp.concatenate(
                    [
                        probe_re * object_re - probe_im * object_im,
                        probe_re * object_im + probe_im * object_re,
                    ],
                    axis=0,
                )
            )
        lefts = from_left(ah, al, jnp.concatenate(waves, axis=1))
        sides = jnp.concatenate(
            [
                jnp.concatenate([lefts[:PROBE, i * NZ : (i + 1) * NZ], lefts[PROBE:, i * NZ : (i + 1) * NZ]], axis=1)
                for i in range(2)
            ],
            axis=0,
        )
        far = from_right(sides, bh, bl)
        far_re = far[:, :NZ]
        far_im = far[:, NZ:]
        modulus = jnp.sqrt(far_re * far_re + far_im * far_im)
        intensity = measured_ref[2 * pair : 2 * pair + 2].reshape(2 * PROBE, NZ)
        shrink = 1.0 - jnp.sqrt(intensity) / jnp.maximum(modulus, 1.0)
        diff = jnp.concatenate([far_re * shrink, far_im * shrink], axis=1)
        half = from_right(diff, ah, al)
        stacked = jnp.concatenate(
            [
                jnp.concatenate([half[i * PROBE : (i + 1) * PROBE, :NZ], half[i * PROBE : (i + 1) * PROBE, NZ:]], axis=0)
                for i in range(2)
            ],
            axis=1,
        )
        backs = from_left(bh, bl, stacked)
        for i in range(2):
            back_re = backs[:PROBE, i * NZ : (i + 1) * NZ]
            back_im = backs[PROBE:, i * NZ : (i + 1) * NZ]
            rows = pl.ds(starts_ref[0, 2 * pair + i], PROBE)
            total_re[rows, :] += probe_re * back_re + probe_im * back_im
            total_im[rows, :] += probe_re * back_im - probe_im * back_re
    for ahead in range(Y):
        owner = lax.rem(y + ahead, Y)
        for tile in range(0, NR, 2):
            low = pl.ds(pl.multiple_of(tile * RAYS + owner * QR, QR), QR)
            high = pl.ds(pl.multiple_of((tile + 1) * RAYS + owner * QR, QR), QR)
            rows = slice(tile * QR, (tile + 2) * QR)
            for part, total in enumerate((total_re, total_im)):
                piece = jnp.concatenate([total[low, :], total[high, :]], axis=0)
                if ahead == 0:
                    own_ref[part, rows, :] = piece
                else:
                    (sent_one, sent_two, sent_three)[ahead - 1][part, rows, :] = piece.astype(bf16)


def shifted(value, axis, length, step):
    return lax.ppermute(value, axis, [(i, (i + step) % length) for i in range(length)])


def across(value):
    return shifted(value, "zh", ZH, 1)


def round_y(pieces):
    return [pieces[0]] + [shifted(pieces[k], "y", Y, k) for k in range(1, Y)]


def body(measured, positions, probe_field, object_field, dual_field, volume, radon_tiles, tile_range):
    zh = lax.axis_index("zh")
    zl = lax.axis_index("zl")
    y = lax.axis_index("y")
    place = jnp.stack([zh, y, zl]).astype(jnp.int32)
    ah, al, bh, bl = dft_blocks()
    radon = radon_tiles.reshape(ZL * XC, HITS, RAYS, TILE)
    volume_rows = volume.reshape(2 * TILE, NZ)
    object_rows = object_field.reshape(128, NZ)
    dual_rows = dual_field.reshape(128, NZ)

    with jax.named_scope("ray_sums"):
        object_theirs = across(object_rows)
        sums = call(
            ray_sums,
            shape(NEAR, ZL, HITS * QR, 2 * NZ, dtype=bf16),
            0,
            0,
            n_far=2,
            scratch=[pltpu.VMEM(radon.shape, bf16), pltpu.VMEM((2 * TILE, NZ), f32), pltpu.SemaphoreType.DMA((ZL + 1,))],
            flops=2 * 2048 * 256 * 256,
            limit=SUMS_LIMIT,
        )(radon, volume_rows)
        near_sums = lax.all_to_all(sums, CROSS, 0, 0, tiled=True)

    with jax.named_scope("targets"):
        own_targets, sums = lax.optimization_barrier((tile_range.reshape(1, ZL * XC), sums))
        targets = jnp.concatenate([own_targets] + [shifted(own_targets, "zl", ZL, k) for k in range(1, ZL)])
        targets = jnp.pad(targets.astype(f32), ((0, QR - ZL), (0, NZ - ZL * XC)))

    with jax.named_scope("fields"):
        object_theirs, sums, targets = lax.optimization_barrier((object_theirs, sums, targets))
        packed = call(
            pack, (shape(SENT_ROWS, NZ),) * Y, 1, 4, scratch=[pltpu.VMEM((128, NZ), f32)], flops=1_000_000
        )(place, object_rows, object_theirs, dual_rows, targets)
        fields = round_y(packed)

    with jax.named_scope("frames"):
        inter_parts = call(
            frame_gradients,
            (shape(2, 128, NZ),) + (shape(2, 128, NZ, dtype=bf16),) * 3,
            2,
            10,
            scratch=[pltpu.VMEM((NDET, NZ), f32)] * 4,
            flops=FRAMES_COST,
        )(place, positions, *fields, probe_field, measured[0], ah, al, bh, bl)
        inter_parts = round_y(inter_parts)

    with jax.named_scope("targets"):
        base = FIELD_ROWS + DRIFT_ROWS
        tables = jnp.concatenate([field[base : base + ZL, : ZL * XC] for field in fields]).astype(jnp.int32)

    with jax.named_scope("near_sum"):
        dense, inter = call(
            add_tiles,
            (shape(DEEP, 128, NZ, dtype=bf16), shape(2, 128, NZ)),
            2,
            9,
            scratch=[pltpu.VMEM((ZL, 128, 2 * NZ), f32)],
            flops=1_000_000,
        )(place, tables, near_sums, *inter_parts, *fields)
        far_sums = lax.all_to_all(dense, ALONG, 0, 0, tiled=True)

    with jax.named_scope("residual"):
        copies, joint = call(
            residual_part, (shape(DEEP, 128, NZ, dtype=bf16), shape(128, NZ)), 0, 1, flops=1_000_000
        )(far_sums)
        residuals = lax.all_to_all(copies, ALONG, 0, 0, tiled=True)
        kept = call(share_out, (shape(ZH, 3, 2 * QR, NZ),) * Y, 1, 2, flops=1_000_000)(place, joint, inter)
        kept = round_y(kept)

    with jax.named_scope("pick"):
        picked = call(
            pick_tiles,
            shape(NEAR, ZL, HITS * QR, 2 * NZ, dtype=bf16),
            2,
            1,
            scratch=[pltpu.VMEM((ZL, 128, 2 * NZ), f32)],
            flops=1_000_000,
        )(place, tables, residuals)
        picked, kept = lax.optimization_barrier((picked, kept))
        returned = lax.all_to_all(picked, CROSS, 0, 0, tiled=True)

    with jax.named_scope("updates"):
        theirs = across(jnp.stack([piece[1] for piece in kept]))
        object_next, dual_next = call(updates, (shape(128, NZ), shape(128, NZ)), 1, 7, flops=1_000_000)(
            place, *kept, theirs, object_rows, dual_rows
        )

    with jax.named_scope("back_project"):
        ordered = radon.reshape(ZL, XC, HITS, Y, QR, TILE).transpose(5, 1, 3, 0, 2, 4).reshape(TILE, -1)
        volume_next = call(back_project, shape(2 * TILE, NZ), 0, 3, flops=2 * 2048 * 256 * 256)(
            ordered, returned, volume_rows
        )
    return (
        object_next.reshape(object_field.shape),
        dual_next.reshape(dual_field.shape),
        volume_next.reshape(volume.shape),
    )


def solution(mesh):
    fine = Mesh(mesh.devices.reshape(ZL, X, C, ZH, Y), ("zl", "x", "c", "zh", "y"))
    ang = ("zl", "x", "c")
    strip = ("zh", "y")
    return jax.shard_map(
        body,
        mesh=fine,
        in_specs=(
            P(ang, strip, None, None),
            P(ang, strip),
            P(),
            P(ang, strip, None, None),
            P(ang, strip, None, None),
            P(ang + strip, None, None),
            P(ang + strip, None, None, None, None),
            P(ang, None, strip, None),
        ),
        out_specs=(
            P(ang, strip, None, None),
            P(ang, strip, None, None),
            P(ang + strip, None, None),
        ),
        check_vma=False,
    )
```

```python
import math

import jax
import jax.numpy as jnp
import numpy as np
from jax import lax
from jax.experimental import pallas as pl
from jax.experimental.pallas import tpu as pltpu
from jax.sharding import Mesh
from jax.sharding import PartitionSpec as P

PROBE = 128
NZ = 128
NDET = 512
RAYS = 32
TILE = 256
HITS = 2
NR = 16

ZL, X, C, ZH, Y = 4, 4, 2, 2, 4
XC = X * C
CROSS = ("x", "c", "y")
ALONG = ("zh", "zl")
NEAR = XC * Y
DEEP = ZH * ZL
QR = RAYS // Y
FR_DEV = 8
FRAMES_COST = 20_000_000_000
SUMS_LIMIT = 62 << 20

penalty = 1.0
object_step = 0.1
volume_step = 1.0
keep = 1.0 - object_step
share = object_step / keep
f32 = jnp.float32
bf16 = jnp.bfloat16

VM = pl.BlockSpec(memory_space=pltpu.VMEM)
SM = pl.BlockSpec(memory_space=pltpu.SMEM)
FAR = pl.BlockSpec(memory_space=pltpu.HBM)


def call(kernel, outs, n_smem, n_vmem, scratch=(), flops=0, moved=1 << 20, limit=48 << 20, n_far=0):
    many = isinstance(outs, tuple)
    return pl.pallas_call(
        kernel,
        out_shape=outs,
        in_specs=[SM] * n_smem + [FAR] * n_far + [VM] * n_vmem,
        out_specs=tuple(VM for _ in outs) if many else VM,
        scratch_shapes=list(scratch),
        compiler_params=pltpu.CompilerParams(vmem_limit_bytes=limit),
        cost_estimate=pl.CostEstimate(flops=flops, bytes_accessed=moved, transcendentals=0),
        name=kernel.__name__,
    )


def shape(*dims, dtype=f32):
    return jax.ShapeDtypeStruct(dims, dtype)


def dft_blocks():
    k = np.arange(PROBE)
    angles = (k[:, None] * k[None, :] % PROBE) * (2.0 * math.pi / PROBE)
    cosine = np.cos(angles) / math.sqrt(PROBE)
    sine = np.sin(angles) / math.sqrt(PROBE)
    both = np.stack([cosine, sine]).astype(np.float32)
    high = both.astype(jnp.bfloat16)
    low = (both - high.astype(np.float32)).astype(jnp.bfloat16)
    return jnp.asarray(np.concatenate([high, low]))


def ray_sums(radon_far, volume_far, target_far, out_ref, target_out, radon_ref, volume_ref, target_ref, sems):
    targets = pltpu.make_async_copy(target_far, target_ref, sems.at[ZL + 1])
    targets.start()
    copies = [pltpu.make_async_copy(volume_far, volume_ref, sems.at[ZL])]
    for zl in range(ZL):
        angles = pl.ds(zl * XC, XC)
        copies.append(pltpu.make_async_copy(radon_far.at[angles], radon_ref.at[angles], sems.at[zl]))
    for copy in copies:
        copy.start()
    copies[0].wait()
    volume_half = jnp.concatenate(
        [volume_ref[pl.ds(0, TILE, stride=2), :], volume_ref[pl.ds(1, TILE, stride=2), :]], axis=1
    ).astype(bf16)
    for zl in range(ZL):
        copies[1 + zl].wait()
        for xc in range(XC):
            rows = radon_ref[zl * XC + xc].reshape(HITS * RAYS, TILE)
            sums = jnp.dot(rows, volume_half, preferred_element_type=f32)
            for y in range(Y):
                low = sums[y * QR : (y + 1) * QR]
                high = sums[RAYS + y * QR : RAYS + (y + 1) * QR]
                out_ref[xc * Y + y, zl] = jnp.concatenate([low, high], axis=0).astype(bf16)
    targets.wait()
    target_out[...] = jnp.zeros(target_out.shape, f32)
    target_out[0:1, : ZL * XC] = target_ref[...].astype(f32)


def each_tile(place_ref, tables):
    zl_here = place_ref[2]
    for back_zl, table in enumerate(tables):
        zl = lax.rem(zl_here + ZL - back_zl, ZL)
        for back_y in range(Y):
            y = lax.rem(place_ref[1] + Y - back_y, Y)
            for xc in range(XC):
                yield zl, xc * Y + y, pl.multiple_of(table[back_y, zl_here * XC + xc] * QR, QR)


def add_tiles(
    place_ref, table_0, table_1, table_2, table_3, sums_ref, inter_0, inter_1, inter_2, inter_3,
    field_0, field_1, field_2, field_3, out_ref, inter_ref, total,
):
    zh = place_ref[0]
    y_here = place_ref[1]
    zl_here = place_ref[2]
    total[...] = jnp.zeros(total.shape, f32)
    for part in range(2):
        inter = (inter_0[part] + inter_1[part].astype(f32)) + (inter_2[part].astype(f32) + inter_3[part].astype(f32))
        inter_ref[part] = inter
        total[zl_here, :, part * NZ : (part + 1) * NZ] = inter * share
    for back, field_ref in enumerate((field_0, field_1, field_2, field_3)):
        owner = zh * Y + lax.rem(y_here + Y - back, Y)
        rows = pl.ds(pl.multiple_of(owner * 2 * QR, 2 * QR), 2 * QR)
        base = FIELD_ROWS
        total[zl_here, rows, :] -= jnp.concatenate(
            [field_ref[base : base + 2 * QR, :], field_ref[base + 2 * QR : base + 4 * QR, :]], axis=1
        )
    for zl, near, row in each_tile(place_ref, (table_0, table_1, table_2, table_3)):
        total[zl, pl.ds(row, HITS * QR), :] += sums_ref[near, zl].astype(f32)
    for zh in range(ZH):
        for zl in range(ZL):
            out_ref[zh * ZL + zl] = total[zl, :, zh * NZ : (zh + 1) * NZ].astype(bf16)


def residual_part(sums_ref, residual_ref, joint_ref):
    total = sums_ref[0].astype(f32)
    for source in range(1, DEEP):
        total = total + sums_ref[source].astype(f32)
    joint_ref[...] = total
    residual = (keep * total).astype(bf16)
    for copy in range(DEEP):
        residual_ref[copy] = residual


def share_out(place_ref, joint_ref, inter_ref, own_ref, one_ref, two_ref, three_ref):
    zh = place_ref[0]
    y = place_ref[1]
    for ahead, ref in enumerate((own_ref, one_ref, two_ref, three_ref)):
        for other in range(ZH):
            owner = lax.rem(zh + other, ZH) * Y + lax.rem(y + ahead, Y)
            rows = pl.ds(pl.multiple_of(owner * 2 * QR, 2 * QR), 2 * QR)
            ref[other, 0] = joint_ref[rows, :]
            for part in range(2):
                ref[other, 1 + part] = inter_ref[part, rows, :]


def pick_tiles(place_ref, table_0, table_1, table_2, table_3, residual_ref, out_ref, rows_ref):
    for zl in range(ZL):
        rows_ref[zl] = jnp.concatenate(
            [residual_ref[zl].astype(f32), residual_ref[ZL + zl].astype(f32)], axis=1
        )

    for zl, near, row in each_tile(place_ref, (table_0, table_1, table_2, table_3)):
        out_ref[near, zl] = rows_ref[zl, pl.ds(row, HITS * QR), :].astype(bf16)


def back_project(radon_ref, picked_ref, volume_ref, out_ref):
    gradient = jnp.dot(
        radon_ref[...],
        picked_ref[...].reshape(NEAR * ZL * HITS * QR, 2 * NZ),
        preferred_element_type=f32,
    )
    for part in range(2):
        rows = pl.ds(part, TILE, stride=2)
        out_ref[rows, :] = volume_ref[rows, :] - volume_step * gradient[:, part * NZ : (part + 1) * NZ]


def updates(
    place_ref, own_ref, one_ref, two_ref, three_ref, theirs_ref, object_ref, dual_ref, object_out, dual_out
):
    zh = place_ref[0]
    y = place_ref[1]
    for back, ref in enumerate((own_ref, one_ref, two_ref, three_ref)):
        source = lax.rem(y + Y - back, Y)
        for other in range(ZH):
            part = lax.rem(zh + other, ZH)
            for tile in range(2):
                piece = slice(tile * QR, (tile + 1) * QR)
                inter = ref[0, 1 + part, piece, :] + theirs_ref[back, 1 + part, piece, :]
                joint = theirs_ref[back, 0, piece, :] if other else ref[0, 0, piece, :]
                rows = pl.ds((tile * RAYS + source * QR) * 2 + part, QR, stride=2)
                field = object_ref[rows, :]
                dual = dual_ref[rows, :]
                projection = joint + (field + dual) - share * inter
                object_next = field - object_step * (inter + dual + penalty * (field - projection))
                object_out[rows, :] = object_next
                dual_out[rows, :] = dual + penalty * (object_next - projection)


def split(value):
    high = value.astype(bf16)
    return high, (value - high.astype(f32)).astype(bf16)


def complex_blocks(cosine, sine):
    forward = jnp.concatenate(
        [jnp.concatenate([cosine, sine], axis=1), jnp.concatenate([-sine, cosine], axis=1)], axis=0
    )
    backward = jnp.concatenate(
        [jnp.concatenate([cosine, -sine], axis=1), jnp.concatenate([sine, cosine], axis=1)], axis=0
    )
    return forward, backward


def from_left(high_table, low_table, value):
    high, low = split(value)
    return (
        jnp.dot(high_table, high, preferred_element_type=f32)
        + jnp.dot(high_table, low, preferred_element_type=f32)
        + jnp.dot(low_table, high, preferred_element_type=f32)
    )


def from_right(value, high_table, low_table):
    high, low = split(value)
    return (
        jnp.dot(high, high_table, preferred_element_type=f32)
        + jnp.dot(low, high_table, preferred_element_type=f32)
        + jnp.dot(high, low_table, preferred_element_type=f32)
    )


FIELD_ROWS = 2 * 128
DRIFT_ROWS = 4 * QR
SENT_ROWS = FIELD_ROWS + DRIFT_ROWS + QR


def pack(place_ref, object_ref, theirs_ref, dual_ref, target_ref, own_ref, one_ref, two_ref, three_ref, both):
    y = place_ref[1]
    both[...] = object_ref[...] + dual_ref[...]
    for ahead, ref in enumerate((own_ref, one_ref, two_ref, three_ref)):
        ref[0:128, :] = object_ref[...]
        ref[128:256, :] = theirs_ref[...]
        ref[FIELD_ROWS + DRIFT_ROWS :, :] = target_ref[...]
        for part in range(2):
            for tile in range(2):
                start = (tile * RAYS + lax.rem(y + ahead, Y) * QR) * 2 + part
                base = FIELD_ROWS + (part * 2 + tile) * QR
                ref[base : base + QR, :] = both[pl.ds(start, QR, stride=2), :]


def frame_gradients(
    place_ref, field_0, field_1, field_2, field_3, probe_ref, measured_ref, dft_ref, own_ref, sent_one, sent_two, sent_three,
    field_re, field_im, total_re, total_im,
):
    zh = place_ref[0]
    y = place_ref[1]
    for back, field_ref in enumerate((field_0, field_1, field_2, field_3)):
        for other in range(ZH):
            owner = lax.rem(zh + other, ZH) * Y + lax.rem(y + Y - back, Y)
            rows = pl.ds(pl.multiple_of(owner * 64, 64), 64)
            field_re[rows, :] = field_ref[pl.ds(other * 128, 64, stride=2), :]
            field_im[rows, :] = field_ref[pl.ds(other * 128 + 1, 64, stride=2), :]
    total_re[...] = jnp.zeros(total_re.shape, f32)
    total_im[...] = jnp.zeros(total_im.shape, f32)
    probe_re = probe_ref[0]
    probe_im = probe_ref[1]
    ah, bh = complex_blocks(dft_ref[0], dft_ref[1])
    al, bl = complex_blocks(dft_ref[2], dft_ref[3])
    for pair in range(FR_DEV // 2):
        waves = []
        for frame in (2 * pair, 2 * pair + 1):
            rows = pl.ds(place_ref[3 + frame], PROBE)
            object_re = field_re[rows, :]
            object_im = field_im[rows, :]
            waves.append(
                jnp.concatenate(
                    [
                        probe_re * object_re - probe_im * object_im,
                        probe_re * object_im + probe_im * object_re,
                    ],
                    axis=0,
                )
            )
        lefts = from_left(ah, al, jnp.concatenate(waves, axis=1))
        sides = jnp.concatenate(
            [
                jnp.concatenate([lefts[:PROBE, i * NZ : (i + 1) * NZ], lefts[PROBE:, i * NZ : (i + 1) * NZ]], axis=1)
                for i in range(2)
            ],
            axis=0,
        )
        far = from_right(sides, bh, bl)
        far_re = far[:, :NZ]
        far_im = far[:, NZ:]
        modulus = jnp.sqrt(far_re * far_re + far_im * far_im)
        intensity = measured_ref[2 * pair : 2 * pair + 2].reshape(2 * PROBE, NZ)
        shrink = 1.0 - jnp.sqrt(intensity) / jnp.maximum(modulus, 1.0)
        diff = jnp.concatenate([far_re * shrink, far_im * shrink], axis=1)
        half = from_right(diff, ah, al)
        stacked = jnp.concatenate(
            [
                jnp.concatenate([half[i * PROBE : (i + 1) * PROBE, :NZ], half[i * PROBE : (i + 1) * PROBE, NZ:]], axis=0)
                for i in range(2)
            ],
            axis=1,
        )
        backs = from_left(bh, bl, stacked)
        for i in range(2):
            back_re = backs[:PROBE, i * NZ : (i + 1) * NZ]
            back_im = backs[PROBE:, i * NZ : (i + 1) * NZ]
            rows = pl.ds(place_ref[3 + 2 * pair + i], PROBE)
            total_re[rows, :] += probe_re * back_re + probe_im * back_im
            total_im[rows, :] += probe_re * back_im - probe_im * back_re
    for ahead in range(Y):
        owner = lax.rem(y + ahead, Y)
        for tile in range(0, NR, 2):
            low = pl.ds(pl.multiple_of(tile * RAYS + owner * QR, QR), QR)
            high = pl.ds(pl.multiple_of((tile + 1) * RAYS + owner * QR, QR), QR)
            rows = slice(tile * QR, (tile + 2) * QR)
            for part, total in enumerate((total_re, total_im)):
                piece = jnp.concatenate([total[low, :], total[high, :]], axis=0)
                if ahead == 0:
                    own_ref[part, rows, :] = piece
                else:
                    (sent_one, sent_two, sent_three)[ahead - 1][part, rows, :] = piece.astype(bf16)


def shifted(value, axis, length, step):
    return lax.ppermute(value, axis, [(i, (i + step) % length) for i in range(length)])


def across(value):
    return shifted(value, "zh", ZH, 1)


def round_y(pieces):
    return [pieces[0]] + [shifted(pieces[k], "y", Y, k) for k in range(1, Y)]


def body(measured, positions, probe_field, object_field, dual_field, volume, radon_tiles, tile_range):
    zh = lax.axis_index("zh")
    zl = lax.axis_index("zl")
    y = lax.axis_index("y")
    place = jnp.concatenate([jnp.stack([zh, y, zl]).astype(jnp.int32), positions.reshape(FR_DEV)])
    radon = radon_tiles.reshape(ZL * XC, HITS, RAYS, TILE)
    volume_rows = volume.reshape(2 * TILE, NZ)
    object_rows = object_field.reshape(128, NZ)
    dual_rows = dual_field.reshape(128, NZ)

    with jax.named_scope("ray_sums"):
        object_theirs = across(object_rows)
        sums, targets = call(
            ray_sums,
            (shape(NEAR, ZL, HITS * QR, 2 * NZ, dtype=bf16), shape(QR, NZ)),
            0,
            0,
            n_far=3,
            scratch=[
                pltpu.VMEM(radon.shape, bf16),
                pltpu.VMEM((2 * TILE, NZ), f32),
                pltpu.VMEM((1, ZL * XC), jnp.int32),
                pltpu.SemaphoreType.DMA((ZL + 2,)),
            ],
            flops=2 * 2048 * 256 * 256,
            limit=SUMS_LIMIT,
        )(radon, volume_rows, tile_range.reshape(1, ZL * XC))
        near_sums = lax.all_to_all(sums, CROSS, 0, 0, tiled=True)

    with jax.named_scope("fields"):
        object_theirs, sums, targets = lax.optimization_barrier((object_theirs, sums, targets))
        packed = call(
            pack, (shape(SENT_ROWS, NZ),) * Y, 1, 4, scratch=[pltpu.VMEM((128, NZ), f32)], flops=1_000_000
        )(place, object_rows, object_theirs, dual_rows, targets)
        fields = round_y(packed)

    with jax.named_scope("frames"):
        inter_parts = call(
            frame_gradients,
            (shape(2, 128, NZ),) + (shape(2, 128, NZ, dtype=bf16),) * 3,
            1,
            7,
            scratch=[pltpu.VMEM((NDET, NZ), f32)] * 4,
            flops=FRAMES_COST,
        )(place, *fields, probe_field, measured[0], dft_blocks())
        inter_own = inter_parts[0]
        inter_parts = round_y(inter_parts)

    with jax.named_scope("targets"):
        base = FIELD_ROWS + DRIFT_ROWS
        table = jnp.concatenate([field[base : base + 1, : ZL * XC] for field in fields]).astype(jnp.int32)
        table, inter_own = lax.optimization_barrier((table, inter_own))
        tables = [table] + [shifted(table, "zl", ZL, k) for k in range(1, ZL)]

    with jax.named_scope("near_sum"):
        dense, inter = call(
            add_tiles,
            (shape(DEEP, 128, NZ, dtype=bf16), shape(2, 128, NZ)),
            5,
            9,
            scratch=[pltpu.VMEM((ZL, 128, 2 * NZ), f32)],
            flops=1_000_000,
        )(place, *tables, near_sums, *inter_parts, *fields)
        far_sums = lax.all_to_all(dense, ALONG, 0, 0, tiled=True)

    with jax.named_scope("residual"):
        copies, joint = call(
            residual_part, (shape(DEEP, 128, NZ, dtype=bf16), shape(128, NZ)), 0, 1, flops=1_000_000
        )(far_sums)
        residuals = lax.all_to_all(copies, ALONG, 0, 0, tiled=True)
        kept = call(share_out, (shape(ZH, 3, 2 * QR, NZ),) * Y, 1, 2, flops=1_000_000)(place, joint, inter)
        kept = round_y(kept)

    with jax.named_scope("pick"):
        picked = call(
            pick_tiles,
            shape(NEAR, ZL, HITS * QR, 2 * NZ, dtype=bf16),
            5,
            1,
            scratch=[pltpu.VMEM((ZL, 128, 2 * NZ), f32)],
            flops=1_000_000,
        )(place, *tables, residuals)
        picked, kept = lax.optimization_barrier((picked, kept))
        returned = lax.all_to_all(picked, CROSS, 0, 0, tiled=True)

    with jax.named_scope("updates"):
        theirs = across(jnp.stack([piece[1] for piece in kept]))
        object_next, dual_next = call(updates, (shape(128, NZ), shape(128, NZ)), 1, 7, flops=1_000_000)(
            place, *kept, theirs, object_rows, dual_rows
        )

    with jax.named_scope("back_project"):
        ordered = radon.reshape(ZL, XC, HITS, Y, QR, TILE).transpose(5, 1, 3, 0, 2, 4).reshape(TILE, -1)
        volume_next = call(back_project, shape(2 * TILE, NZ), 0, 3, flops=2 * 2048 * 256 * 256)(
            ordered, returned, volume_rows
        )
    return (
        object_next.reshape(object_field.shape),
        dual_next.reshape(dual_field.shape),
        volume_next.reshape(volume.shape),
    )


def solution(mesh):
    fine = Mesh(mesh.devices.reshape(ZL, X, C, ZH, Y), ("zl", "x", "c", "zh", "y"))
    ang = ("zl", "x", "c")
    strip = ("zh", "y")
    return jax.shard_map(
        body,
        mesh=fine,
        in_specs=(
            P(ang, strip, None, None),
            P(ang, strip),
            P(),
            P(ang, strip, None, None),
            P(ang, strip, None, None),
            P(ang + strip, None, None),
            P(ang + strip, None, None, None, None),
            P(ang, None, strip, None),
        ),
        out_specs=(
            P(ang, strip, None, None),
            P(ang, strip, None, None),
            P(ang + strip, None, None),
        ),
        check_vma=False,
    )
```

```python
import math

import jax
import jax.numpy as jnp
import numpy as np
from jax import lax
from jax.experimental import pallas as pl
from jax.experimental.pallas import tpu as pltpu
from jax.sharding import Mesh
from jax.sharding import PartitionSpec as P

PROBE = 128
NZ = 128
NDET = 512
RAYS = 32
TILE = 256
HITS = 2
NR = 16

ZL, X, C, ZH, Y = 4, 4, 2, 2, 4
XC = X * C
CROSS = ("x", "c", "y")
ALONG = ("zh", "zl")
NEAR = XC * Y
DEEP = ZH * ZL
QR = RAYS // Y
FR_DEV = 8
FRAMES_COST = 20_000_000_000
SUMS_LIMIT = 62 << 20

penalty = 1.0
object_step = 0.1
volume_step = 1.0
keep = 1.0 - object_step
share = object_step / keep
f32 = jnp.float32
bf16 = jnp.bfloat16

VM = pl.BlockSpec(memory_space=pltpu.VMEM)
SM = pl.BlockSpec(memory_space=pltpu.SMEM)
FAR = pl.BlockSpec(memory_space=pltpu.HBM)


def call(kernel, outs, n_smem, n_vmem, scratch=(), flops=0, moved=1 << 20, limit=48 << 20, n_far=0):
    many = isinstance(outs, tuple)
    return pl.pallas_call(
        kernel,
        out_shape=outs,
        in_specs=[SM] * n_smem + [FAR] * n_far + [VM] * n_vmem,
        out_specs=tuple(VM for _ in outs) if many else VM,
        scratch_shapes=list(scratch),
        compiler_params=pltpu.CompilerParams(vmem_limit_bytes=limit),
        cost_estimate=pl.CostEstimate(flops=flops, bytes_accessed=moved, transcendentals=0),
        name=kernel.__name__,
    )


def shape(*dims, dtype=f32):
    return jax.ShapeDtypeStruct(dims, dtype)


def dft_blocks():
    k = np.arange(PROBE)
    angles = (k[:, None] * k[None, :] % PROBE) * (2.0 * math.pi / PROBE)
    cosine = np.cos(angles) / math.sqrt(PROBE)
    sine = np.sin(angles) / math.sqrt(PROBE)
    both = np.stack([cosine, sine]).astype(np.float32)
    high = both.astype(jnp.bfloat16)
    low = (both - high.astype(np.float32)).astype(jnp.bfloat16)
    return jnp.asarray(np.concatenate([high, low]))


def ray_sums(radon_far, volume_far, out_ref, radon_ref, volume_ref, sems):
    copies = [pltpu.make_async_copy(volume_far, volume_ref, sems.at[ZL])]
    for zl in range(ZL):
        angles = pl.ds(zl * XC, XC)
        copies.append(pltpu.make_async_copy(radon_far.at[angles], radon_ref.at[angles], sems.at[zl]))
    for copy in copies:
        copy.start()
    copies[0].wait()
    volume_half = jnp.concatenate(
        [volume_ref[pl.ds(0, TILE, stride=2), :], volume_ref[pl.ds(1, TILE, stride=2), :]], axis=1
    ).astype(bf16)
    for zl in range(ZL):
        copies[1 + zl].wait()
        for xc in range(XC):
            rows = radon_ref[zl * XC + xc].reshape(HITS * RAYS, TILE)
            sums = jnp.dot(rows, volume_half, preferred_element_type=f32)
            for y in range(Y):
                low = sums[y * QR : (y + 1) * QR]
                high = sums[RAYS + y * QR : RAYS + (y + 1) * QR]
                out_ref[xc * Y + y, zl] = jnp.concatenate([low, high], axis=0).astype(bf16)


def each_tile(place_ref, table_ref):
    zl_here = place_ref[2]
    for apart in range(ZL):
        zl = jnp.bitwise_xor(zl_here, apart)
        for back_y in range(Y):
            y = lax.rem(place_ref[1] + Y - back_y, Y)
            for xc in range(XC):
                row = table_ref[back_y * ZL + apart, zl_here * XC + xc] * QR
                yield zl, xc * Y + y, pl.multiple_of(row, QR)


def add_tiles(
    place_ref, table_ref, sums_ref, inter_0, inter_1, inter_2, inter_3,
    field_0, field_1, field_2, field_3, out_ref, inter_ref, total,
):
    zh = place_ref[0]
    y_here = place_ref[1]
    zl_here = place_ref[2]
    total[...] = jnp.zeros(total.shape, f32)
    for part in range(2):
        inter = (inter_0[part] + inter_1[part].astype(f32)) + (inter_2[part].astype(f32) + inter_3[part].astype(f32))
        inter_ref[part] = inter
        total[zl_here, :, part * NZ : (part + 1) * NZ] = inter * share
    for back, field_ref in enumerate((field_0, field_1, field_2, field_3)):
        owner = zh * Y + lax.rem(y_here + Y - back, Y)
        rows = pl.ds(pl.multiple_of(owner * 2 * QR, 2 * QR), 2 * QR)
        base = FIELD_ROWS
        total[zl_here, rows, :] -= jnp.concatenate(
            [field_ref[base : base + 2 * QR, :], field_ref[base + 2 * QR : base + 4 * QR, :]], axis=1
        )
    for zl, near, row in each_tile(place_ref, table_ref):
        total[zl, pl.ds(row, HITS * QR), :] += sums_ref[near, zl].astype(f32)
    for zh in range(ZH):
        for zl in range(ZL):
            out_ref[zh * ZL + zl] = total[zl, :, zh * NZ : (zh + 1) * NZ].astype(bf16)


def residual_part(sums_ref, residual_ref, joint_ref):
    total = sums_ref[0].astype(f32)
    for source in range(1, DEEP):
        total = total + sums_ref[source].astype(f32)
    joint_ref[...] = total
    residual = (keep * total).astype(bf16)
    for copy in range(DEEP):
        residual_ref[copy] = residual


def share_out(place_ref, joint_ref, inter_ref, own_ref, one_ref, two_ref, three_ref):
    zh = place_ref[0]
    y = place_ref[1]
    for ahead, ref in enumerate((own_ref, one_ref, two_ref, three_ref)):
        for other in range(ZH):
            owner = lax.rem(zh + other, ZH) * Y + lax.rem(y + ahead, Y)
            rows = pl.ds(pl.multiple_of(owner * 2 * QR, 2 * QR), 2 * QR)
            ref[other, 0] = joint_ref[rows, :]
            for part in range(2):
                ref[other, 1 + part] = inter_ref[part, rows, :]


def pick_tiles(place_ref, table_ref, residual_ref, out_ref, rows_ref):
    for zl in range(ZL):
        rows_ref[zl] = jnp.concatenate(
            [residual_ref[zl].astype(f32), residual_ref[ZL + zl].astype(f32)], axis=1
        )

    for zl, near, row in each_tile(place_ref, table_ref):
        out_ref[near, zl] = rows_ref[zl, pl.ds(row, HITS * QR), :].astype(bf16)


def back_project(radon_ref, picked_ref, volume_ref, out_ref):
    gradient = jnp.dot(
        radon_ref[...],
        picked_ref[...].reshape(NEAR * ZL * HITS * QR, 2 * NZ),
        preferred_element_type=f32,
    )
    for part in range(2):
        rows = pl.ds(part, TILE, stride=2)
        out_ref[rows, :] = volume_ref[rows, :] - volume_step * gradient[:, part * NZ : (part + 1) * NZ]


def updates(
    place_ref, own_ref, one_ref, two_ref, three_ref, theirs_ref, object_ref, dual_ref, object_out, dual_out
):
    zh = place_ref[0]
    y = place_ref[1]
    for back, ref in enumerate((own_ref, one_ref, two_ref, three_ref)):
        source = lax.rem(y + Y - back, Y)
        for other in range(ZH):
            part = lax.rem(zh + other, ZH)
            for tile in range(2):
                piece = slice(tile * QR, (tile + 1) * QR)
                inter = ref[0, 1 + part, piece, :] + theirs_ref[back, 1 + part, piece, :]
                joint = theirs_ref[back, 0, piece, :] if other else ref[0, 0, piece, :]
                rows = pl.ds((tile * RAYS + source * QR) * 2 + part, QR, stride=2)
                field = object_ref[rows, :]
                dual = dual_ref[rows, :]
                projection = joint + (field + dual) - share * inter
                object_next = field - object_step * (inter + dual + penalty * (field - projection))
                object_out[rows, :] = object_next
                dual_out[rows, :] = dual + penalty * (object_next - projection)


def split(value):
    high = value.astype(bf16)
    return high, (value - high.astype(f32)).astype(bf16)


def complex_blocks(cosine, sine):
    forward = jnp.concatenate(
        [jnp.concatenate([cosine, sine], axis=1), jnp.concatenate([-sine, cosine], axis=1)], axis=0
    )
    backward = jnp.concatenate(
        [jnp.concatenate([cosine, -sine], axis=1), jnp.concatenate([sine, cosine], axis=1)], axis=0
    )
    return forward, backward


def from_left(high_table, low_table, value):
    high, low = split(value)
    return (
        jnp.dot(high_table, high, preferred_element_type=f32)
        + jnp.dot(high_table, low, preferred_element_type=f32)
        + jnp.dot(low_table, high, preferred_element_type=f32)
    )


def from_right(value, high_table, low_table):
    high, low = split(value)
    return (
        jnp.dot(high, high_table, preferred_element_type=f32)
        + jnp.dot(low, high_table, preferred_element_type=f32)
        + jnp.dot(high, low_table, preferred_element_type=f32)
    )


FIELD_ROWS = 2 * 128
DRIFT_ROWS = 4 * QR
SENT_ROWS = FIELD_ROWS + DRIFT_ROWS + QR


def pack(
    place_ref, object_ref, theirs_ref, dual_ref, near_ref, far_ref,
    own_ref, one_ref, two_ref, three_ref, both,
):
    y = place_ref[1]
    both[...] = object_ref[...] + dual_ref[...]
    for ahead, ref in enumerate((own_ref, one_ref, two_ref, three_ref)):
        ref[0:128, :] = object_ref[...]
        ref[128:256, :] = theirs_ref[...]
        base = FIELD_ROWS + DRIFT_ROWS
        ref[base:, :] = jnp.zeros((QR, NZ), f32)
        ref[base : base + 2, : ZL * XC] = near_ref[...].astype(f32)
        ref[base + 2 : base + 4, : ZL * XC] = far_ref[...].astype(f32)
        for part in range(2):
            for tile in range(2):
                start = (tile * RAYS + lax.rem(y + ahead, Y) * QR) * 2 + part
                base = FIELD_ROWS + (part * 2 + tile) * QR
                ref[base : base + QR, :] = both[pl.ds(start, QR, stride=2), :]


def frame_gradients(
    place_ref, field_0, field_1, field_2, field_3, probe_ref, measured_ref, dft_ref, own_ref, sent_one, sent_two, sent_three,
    field_re, field_im, total_re, total_im,
):
    zh = place_ref[0]
    y = place_ref[1]
    for back, field_ref in enumerate((field_0, field_1, field_2, field_3)):
        for other in range(ZH):
            owner = lax.rem(zh + other, ZH) * Y + lax.rem(y + Y - back, Y)
            rows = pl.ds(pl.multiple_of(owner * 64, 64), 64)
            field_re[rows, :] = field_ref[pl.ds(other * 128, 64, stride=2), :]
            field_im[rows, :] = field_ref[pl.ds(other * 128 + 1, 64, stride=2), :]
    total_re[...] = jnp.zeros(total_re.shape, f32)
    total_im[...] = jnp.zeros(total_im.shape, f32)
    probe_re = probe_ref[0]
    probe_im = probe_ref[1]
    ah, bh = complex_blocks(dft_ref[0], dft_ref[1])
    al, bl = complex_blocks(dft_ref[2], dft_ref[3])
    for pair in range(FR_DEV // 2):
        waves = []
        for frame in (2 * pair, 2 * pair + 1):
            rows = pl.ds(place_ref[3 + frame], PROBE)
            object_re = field_re[rows, :]
            object_im = field_im[rows, :]
            waves.append(
                jnp.concatenate(
                    [
                        probe_re * object_re - probe_im * object_im,
                        probe_re * object_im + probe_im * object_re,
                    ],
                    axis=0,
                )
            )
        lefts = from_left(ah, al, jnp.concatenate(waves, axis=1))
        sides = jnp.concatenate(
            [
                jnp.concatenate([lefts[:PROBE, i * NZ : (i + 1) * NZ], lefts[PROBE:, i * NZ : (i + 1) * NZ]], axis=1)
                for i in range(2)
            ],
            axis=0,
        )
        far = from_right(sides, bh, bl)
        far_re = far[:, :NZ]
        far_im = far[:, NZ:]
        modulus = jnp.sqrt(far_re * far_re + far_im * far_im)
        intensity = measured_ref[2 * pair : 2 * pair + 2].reshape(2 * PROBE, NZ)
        shrink = 1.0 - jnp.sqrt(intensity) / jnp.maximum(modulus, 1.0)
        diff = jnp.concatenate([far_re * shrink, far_im * shrink], axis=1)
        half = from_right(diff, ah, al)
        stacked = jnp.concatenate(
            [
                jnp.concatenate([half[i * PROBE : (i + 1) * PROBE, :NZ], half[i * PROBE : (i + 1) * PROBE, NZ:]], axis=0)
                for i in range(2)
            ],
            axis=1,
        )
        backs = from_left(bh, bl, stacked)
        for i in range(2):
            back_re = backs[:PROBE, i * NZ : (i + 1) * NZ]
            back_im = backs[PROBE:, i * NZ : (i + 1) * NZ]
            rows = pl.ds(place_ref[3 + 2 * pair + i], PROBE)
            total_re[rows, :] += probe_re * back_re + probe_im * back_im
            total_im[rows, :] += probe_re * back_im - probe_im * back_re
    for ahead in range(Y):
        owner = lax.rem(y + ahead, Y)
        for tile in range(0, NR, 2):
            low = pl.ds(pl.multiple_of(tile * RAYS + owner * QR, QR), QR)
            high = pl.ds(pl.multiple_of((tile + 1) * RAYS + owner * QR, QR), QR)
            rows = slice(tile * QR, (tile + 2) * QR)
            for part, total in enumerate((total_re, total_im)):
                piece = jnp.concatenate([total[low, :], total[high, :]], axis=0)
                if ahead == 0:
                    own_ref[part, rows, :] = piece
                else:
                    (sent_one, sent_two, sent_three)[ahead - 1][part, rows, :] = piece.astype(bf16)


def shifted(value, axis, length, step):
    return lax.ppermute(value, axis, [(i, (i + step) % length) for i in range(length)])


def swapped(value, apart):
    return lax.ppermute(value, "zl", [(i, i ^ apart) for i in range(ZL)])


def across(value):
    return shifted(value, "zh", ZH, 1)


def round_y(pieces):
    return [pieces[0]] + [shifted(pieces[k], "y", Y, k) for k in range(1, Y)]


def body(measured, positions, probe_field, object_field, dual_field, volume, radon_tiles, tile_range):
    zh = lax.axis_index("zh")
    zl = lax.axis_index("zl")
    y = lax.axis_index("y")
    place = jnp.concatenate([jnp.stack([zh, y, zl]).astype(jnp.int32), positions.reshape(FR_DEV)])
    radon = radon_tiles.reshape(ZL * XC, HITS, RAYS, TILE)
    volume_rows = volume.reshape(2 * TILE, NZ)
    object_rows = object_field.reshape(128, NZ)
    dual_rows = dual_field.reshape(128, NZ)

    with jax.named_scope("ray_sums"):
        object_theirs = across(object_rows)
        sums = call(
            ray_sums,
            shape(NEAR, ZL, HITS * QR, 2 * NZ, dtype=bf16),
            0,
            0,
            n_far=2,
            scratch=[pltpu.VMEM(radon.shape, bf16), pltpu.VMEM((2 * TILE, NZ), f32), pltpu.SemaphoreType.DMA((ZL + 1,))],
            flops=2 * 2048 * 256 * 256,
            limit=SUMS_LIMIT,
        )(radon, volume_rows)
        near_sums = lax.all_to_all(sums, CROSS, 0, 0, tiled=True)

    with jax.named_scope("targets"):
        table, sums = lax.optimization_barrier((tile_range.reshape(1, ZL * XC), sums))
        near = jnp.concatenate([table, swapped(table, 1)])
        far = swapped(near, 2)

    with jax.named_scope("fields"):
        object_theirs, sums = lax.optimization_barrier((object_theirs, sums))
        packed = call(
            pack, (shape(SENT_ROWS, NZ),) * Y, 1, 5, scratch=[pltpu.VMEM((128, NZ), f32)], flops=1_000_000
        )(place, object_rows, object_theirs, dual_rows, near, far)
        fields = round_y(packed)

    with jax.named_scope("frames"):
        inter_parts = call(
            frame_gradients,
            (shape(2, 128, NZ),) + (shape(2, 128, NZ, dtype=bf16),) * 3,
            1,
            7,
            scratch=[pltpu.VMEM((NDET, NZ), f32)] * 4,
            flops=FRAMES_COST,
        )(place, *fields, probe_field, measured[0], dft_blocks())
        inter_parts = round_y(inter_parts)

    with jax.named_scope("targets"):
        base = FIELD_ROWS + DRIFT_ROWS
        tables = jnp.concatenate([field[base : base + ZL, : ZL * XC] for field in fields]).astype(jnp.int32)

    with jax.named_scope("near_sum"):
        dense, inter = call(
            add_tiles,
            (shape(DEEP, 128, NZ, dtype=bf16), shape(2, 128, NZ)),
            2,
            9,
            scratch=[pltpu.VMEM((ZL, 128, 2 * NZ), f32)],
            flops=1_000_000,
        )(place, tables, near_sums, *inter_parts, *fields)
        far_sums = lax.all_to_all(dense, ALONG, 0, 0, tiled=True)

    with jax.named_scope("residual"):
        copies, joint = call(
            residual_part, (shape(DEEP, 128, NZ, dtype=bf16), shape(128, NZ)), 0, 1, flops=1_000_000
        )(far_sums)
        residuals = lax.all_to_all(copies, ALONG, 0, 0, tiled=True)
        kept = call(share_out, (shape(ZH, 3, 2 * QR, NZ),) * Y, 1, 2, flops=1_000_000)(place, joint, inter)
        kept = round_y(kept)

    with jax.named_scope("pick"):
        picked = call(
            pick_tiles,
            shape(NEAR, ZL, HITS * QR, 2 * NZ, dtype=bf16),
            2,
            1,
            scratch=[pltpu.VMEM((ZL, 128, 2 * NZ), f32)],
            flops=1_000_000,
        )(place, tables, residuals)
        picked, kept = lax.optimization_barrier((picked, kept))
        returned = lax.all_to_all(picked, CROSS, 0, 0, tiled=True)

    with jax.named_scope("updates"):
        theirs = across(jnp.stack([piece[1] for piece in kept]))
        object_next, dual_next = call(updates, (shape(128, NZ), shape(128, NZ)), 1, 7, flops=1_000_000)(
            place, *kept, theirs, object_rows, dual_rows
        )

    with jax.named_scope("back_project"):
        ordered = radon.reshape(ZL, XC, HITS, Y, QR, TILE).transpose(5, 1, 3, 0, 2, 4).reshape(TILE, -1)
        volume_next = call(back_project, shape(2 * TILE, NZ), 0, 3, flops=2 * 2048 * 256 * 256)(
            ordered, returned, volume_rows
        )
    return (
        object_next.reshape(object_field.shape),
        dual_next.reshape(dual_field.shape),
        volume_next.reshape(volume.shape),
    )


def solution(mesh):
    fine = Mesh(mesh.devices.reshape(ZL, X, C, ZH, Y), ("zl", "x", "c", "zh", "y"))
    ang = ("zl", "x", "c")
    strip = ("zh", "y")
    return jax.shard_map(
        body,
        mesh=fine,
        in_specs=(
            P(ang, strip, None, None),
            P(ang, strip),
            P(),
            P(ang, strip, None, None),
            P(ang, strip, None, None),
            P(ang + strip, None, None),
            P(ang + strip, None, None, None, None),
            P(ang, None, strip, None),
        ),
        out_specs=(
            P(ang, strip, None, None),
            P(ang, strip, None, None),
            P(ang + strip, None, None),
        ),
        check_vma=False,
    )
```

```python
import math

import jax
import jax.numpy as jnp
import numpy as np
from jax import lax
from jax.experimental import pallas as pl
from jax.experimental.pallas import tpu as pltpu
from jax.sharding import Mesh
from jax.sharding import PartitionSpec as P

PROBE = 128
NZ = 128
NDET = 512
RAYS = 32
TILE = 256
HITS = 2
NR = 16

ZL, X, C, ZH, Y = 4, 4, 2, 2, 4
XC = X * C
CROSS = ("x", "c", "y")
ALONG = ("zh", "zl")
NEAR = XC * Y
DEEP = ZH * ZL
QR = RAYS // Y
FR_DEV = 8
FRAMES_COST = 20_000_000_000
SUMS_LIMIT = 62 << 20

penalty = 1.0
object_step = 0.1
volume_step = 1.0
keep = 1.0 - object_step
share = object_step / keep
f32 = jnp.float32
bf16 = jnp.bfloat16

VM = pl.BlockSpec(memory_space=pltpu.VMEM)
SM = pl.BlockSpec(memory_space=pltpu.SMEM)
FAR = pl.BlockSpec(memory_space=pltpu.HBM)


def call(kernel, outs, n_smem, n_vmem, scratch=(), flops=0, moved=1 << 20, limit=48 << 20, n_far=0):
    many = isinstance(outs, tuple)
    return pl.pallas_call(
        kernel,
        out_shape=outs,
        in_specs=[SM] * n_smem + [FAR] * n_far + [VM] * n_vmem,
        out_specs=tuple(VM for _ in outs) if many else VM,
        scratch_shapes=list(scratch),
        compiler_params=pltpu.CompilerParams(vmem_limit_bytes=limit),
        cost_estimate=pl.CostEstimate(flops=flops, bytes_accessed=moved, transcendentals=0),
        name=kernel.__name__,
    )


def shape(*dims, dtype=f32):
    return jax.ShapeDtypeStruct(dims, dtype)


def dft_blocks():
    k = np.arange(PROBE)
    angles = (k[:, None] * k[None, :] % PROBE) * (2.0 * math.pi / PROBE)
    cosine = np.cos(angles) / math.sqrt(PROBE)
    sine = np.sin(angles) / math.sqrt(PROBE)
    both = np.stack([cosine, sine]).astype(np.float32)
    high = both.astype(jnp.bfloat16)
    low = (both - high.astype(np.float32)).astype(jnp.bfloat16)
    return jnp.asarray(np.concatenate([high, low]))


def ray_sums(radon_far, volume_far, target_far, out_ref, target_out, radon_ref, volume_ref, target_ref, sems):
    targets = pltpu.make_async_copy(target_far, target_ref, sems.at[ZL + 1])
    targets.start()
    copies = [pltpu.make_async_copy(volume_far, volume_ref, sems.at[ZL])]
    for zl in range(ZL):
        angles = pl.ds(zl * XC, XC)
        copies.append(pltpu.make_async_copy(radon_far.at[angles], radon_ref.at[angles], sems.at[zl]))
    for copy in copies:
        copy.start()
    copies[0].wait()
    volume_half = jnp.concatenate(
        [volume_ref[pl.ds(0, TILE, stride=2), :], volume_ref[pl.ds(1, TILE, stride=2), :]], axis=1
    ).astype(bf16)
    for zl in range(ZL):
        copies[1 + zl].wait()
        for xc in range(XC):
            rows = radon_ref[zl * XC + xc].reshape(HITS * RAYS, TILE)
            sums = jnp.dot(rows, volume_half, preferred_element_type=f32)
            for y in range(Y):
                low = sums[y * QR : (y + 1) * QR]
                high = sums[RAYS + y * QR : RAYS + (y + 1) * QR]
                out_ref[xc * Y + y, zl] = jnp.concatenate([low, high], axis=0).astype(bf16)
    targets.wait()
    target_out[...] = jnp.zeros(target_out.shape, f32)
    target_out[0:1, : ZL * XC] = target_ref[...].astype(f32)


def each_tile(place_ref, tables):
    zl_here = place_ref[2]
    for back_zl, table in enumerate(tables):
        zl = lax.rem(zl_here + ZL - back_zl, ZL)
        for back_y in range(Y):
            y = lax.rem(place_ref[1] + Y - back_y, Y)
            for xc in range(XC):
                yield zl, xc * Y + y, pl.multiple_of(table[back_y, zl_here * XC + xc] * QR, QR)


def add_tiles(
    place_ref, table_0, table_1, table_2, table_3, sums_ref, inter_0, inter_1, inter_2, inter_3,
    field_0, field_1, field_2, field_3, out_ref, inter_ref, total,
):
    zh = place_ref[0]
    y_here = place_ref[1]
    zl_here = place_ref[2]
    total[...] = jnp.zeros(total.shape, f32)
    for part in range(2):
        inter = (inter_0[part] + inter_1[part].astype(f32)) + (inter_2[part].astype(f32) + inter_3[part].astype(f32))
        inter_ref[part] = inter
        total[zl_here, :, part * NZ : (part + 1) * NZ] = inter * share
    for back, field_ref in enumerate((field_0, field_1, field_2, field_3)):
        owner = zh * Y + lax.rem(y_here + Y - back, Y)
        rows = pl.ds(pl.multiple_of(owner * 2 * QR, 2 * QR), 2 * QR)
        base = FIELD_ROWS
        total[zl_here, rows, :] -= jnp.concatenate(
            [field_ref[base : base + 2 * QR, :], field_ref[base + 2 * QR : base + 4 * QR, :]], axis=1
        )
    for zl, near, row in each_tile(place_ref, (table_0, table_1, table_2, table_3)):
        total[zl, pl.ds(row, HITS * QR), :] += sums_ref[near, zl].astype(f32)
    for zh in range(ZH):
        for zl in range(ZL):
            out_ref[zh * ZL + zl] = total[zl, :, zh * NZ : (zh + 1) * NZ].astype(bf16)


def residual_part(sums_ref, residual_ref, joint_ref):
    total = sums_ref[0].astype(f32)
    for source in range(1, DEEP):
        total = total + sums_ref[source].astype(f32)
    joint_ref[...] = total
    residual = (keep * total).astype(bf16)
    for copy in range(DEEP):
        residual_ref[copy] = residual


def share_out(place_ref, joint_ref, inter_ref, own_ref, one_ref, two_ref, three_ref):
    zh = place_ref[0]
    y = place_ref[1]
    for ahead, ref in enumerate((own_ref, one_ref, two_ref, three_ref)):
        for other in range(ZH):
            owner = lax.rem(zh + other, ZH) * Y + lax.rem(y + ahead, Y)
            rows = pl.ds(pl.multiple_of(owner * 2 * QR, 2 * QR), 2 * QR)
            ref[other, 0] = joint_ref[rows, :]
            for part in range(2):
                ref[other, 1 + part] = inter_ref[part, rows, :]


def pick_tiles(place_ref, table_0, table_1, table_2, table_3, residual_ref, out_far, rows_ref, out_ref, sems):
    tables = (table_0, table_1, table_2, table_3)
    zl_here = place_ref[2]
    for zl in range(ZL):
        rows_ref[zl] = jnp.concatenate(
            [residual_ref[zl].astype(f32), residual_ref[ZL + zl].astype(f32)], axis=1
        )
    copies = []
    for back_y in range(Y):
        y = lax.rem(place_ref[1] + Y - back_y, Y)
        for xc in range(XC):
            near = xc * Y + y
            for back_zl in range(ZL):
                zl = lax.rem(zl_here + ZL - back_zl, ZL)
                row = pl.multiple_of(tables[back_zl][back_y, zl_here * XC + xc] * QR, QR)
                out_ref[near, zl] = rows_ref[zl, pl.ds(row, HITS * QR), :].astype(bf16)
            copies.append(pltpu.make_async_copy(out_ref.at[near], out_far.at[near], sems.at[back_y * XC + xc]))
            copies[-1].start()
    for copy in copies:
        copy.wait()


def back_project(radon_ref, picked_ref, volume_ref, out_ref):
    gradient = jnp.dot(
        radon_ref[...],
        picked_ref[...].reshape(NEAR * ZL * HITS * QR, 2 * NZ),
        preferred_element_type=f32,
    )
    for part in range(2):
        rows = pl.ds(part, TILE, stride=2)
        out_ref[rows, :] = volume_ref[rows, :] - volume_step * gradient[:, part * NZ : (part + 1) * NZ]


def updates(
    place_ref, own_ref, one_ref, two_ref, three_ref, theirs_ref, object_ref, dual_ref, object_out, dual_out
):
    zh = place_ref[0]
    y = place_ref[1]
    for back, ref in enumerate((own_ref, one_ref, two_ref, three_ref)):
        source = lax.rem(y + Y - back, Y)
        for other in range(ZH):
            part = lax.rem(zh + other, ZH)
            for tile in range(2):
                piece = slice(tile * QR, (tile + 1) * QR)
                inter = ref[0, 1 + part, piece, :] + theirs_ref[back, 1 + part, piece, :]
                joint = theirs_ref[back, 0, piece, :] if other else ref[0, 0, piece, :]
                rows = pl.ds((tile * RAYS + source * QR) * 2 + part, QR, stride=2)
                field = object_ref[rows, :]
                dual = dual_ref[rows, :]
                projection = joint + (field + dual) - share * inter
                object_next = field - object_step * (inter + dual + penalty * (field - projection))
                object_out[rows, :] = object_next
                dual_out[rows, :] = dual + penalty * (object_next - projection)


def split(value):
    high = value.astype(bf16)
    return high, (value - high.astype(f32)).astype(bf16)


def complex_blocks(cosine, sine):
    forward = jnp.concatenate(
        [jnp.concatenate([cosine, sine], axis=1), jnp.concatenate([-sine, cosine], axis=1)], axis=0
    )
    backward = jnp.concatenate(
        [jnp.concatenate([cosine, -sine], axis=1), jnp.concatenate([sine, cosine], axis=1)], axis=0
    )
    return forward, backward


def from_left(high_table, low_table, value):
    high, low = split(value)
    return (
        jnp.dot(high_table, high, preferred_element_type=f32)
        + jnp.dot(high_table, low, preferred_element_type=f32)
        + jnp.dot(low_table, high, preferred_element_type=f32)
    )


def from_right(value, high_table, low_table):
    high, low = split(value)
    return (
        jnp.dot(high, high_table, preferred_element_type=f32)
        + jnp.dot(low, high_table, preferred_element_type=f32)
        + jnp.dot(high, low_table, preferred_element_type=f32)
    )


FIELD_ROWS = 2 * 128
DRIFT_ROWS = 4 * QR
SENT_ROWS = FIELD_ROWS + DRIFT_ROWS + QR


def pack(place_ref, object_ref, theirs_ref, dual_ref, target_ref, own_ref, one_ref, two_ref, three_ref, both):
    y = place_ref[1]
    both[...] = object_ref[...] + dual_ref[...]
    for ahead, ref in enumerate((own_ref, one_ref, two_ref, three_ref)):
        ref[0:128, :] = object_ref[...]
        ref[128:256, :] = theirs_ref[...]
        ref[FIELD_ROWS + DRIFT_ROWS :, :] = target_ref[...]
        for part in range(2):
            for tile in range(2):
                start = (tile * RAYS + lax.rem(y + ahead, Y) * QR) * 2 + part
                base = FIELD_ROWS + (part * 2 + tile) * QR
                ref[base : base + QR, :] = both[pl.ds(start, QR, stride=2), :]


def frame_gradients(
    place_ref, field_0, field_1, field_2, field_3, probe_ref, measured_ref, dft_ref, own_ref, sent_one, sent_two, sent_three,
    field_re, field_im, total_re, total_im,
):
    zh = place_ref[0]
    y = place_ref[1]
    for back, field_ref in enumerate((field_0, field_1, field_2, field_3)):
        for other in range(ZH):
            owner = lax.rem(zh + other, ZH) * Y + lax.rem(y + Y - back, Y)
            rows = pl.ds(pl.multiple_of(owner * 64, 64), 64)
            field_re[rows, :] = field_ref[pl.ds(other * 128, 64, stride=2), :]
            field_im[rows, :] = field_ref[pl.ds(other * 128 + 1, 64, stride=2), :]
    total_re[...] = jnp.zeros(total_re.shape, f32)
    total_im[...] = jnp.zeros(total_im.shape, f32)
    probe_re = probe_ref[0]
    probe_im = probe_ref[1]
    ah, bh = complex_blocks(dft_ref[0], dft_ref[1])
    al, bl = complex_blocks(dft_ref[2], dft_ref[3])
    for pair in range(FR_DEV // 2):
        waves = []
        for frame in (2 * pair, 2 * pair + 1):
            rows = pl.ds(place_ref[3 + frame], PROBE)
            object_re = field_re[rows, :]
            object_im = field_im[rows, :]
            waves.append(
                jnp.concatenate(
                    [
                        probe_re * object_re - probe_im * object_im,
                        probe_re * object_im + probe_im * object_re,
                    ],
                    axis=0,
                )
            )
        lefts = from_left(ah, al, jnp.concatenate(waves, axis=1))
        sides = jnp.concatenate(
            [
                jnp.concatenate([lefts[:PROBE, i * NZ : (i + 1) * NZ], lefts[PROBE:, i * NZ : (i + 1) * NZ]], axis=1)
                for i in range(2)
            ],
            axis=0,
        )
        far = from_right(sides, bh, bl)
        far_re = far[:, :NZ]
        far_im = far[:, NZ:]
        modulus = jnp.sqrt(far_re * far_re + far_im * far_im)
        intensity = measured_ref[2 * pair : 2 * pair + 2].reshape(2 * PROBE, NZ)
        shrink = 1.0 - jnp.sqrt(intensity) / jnp.maximum(modulus, 1.0)
        diff = jnp.concatenate([far_re * shrink, far_im * shrink], axis=1)
        half = from_right(diff, ah, al)
        stacked = jnp.concatenate(
            [
                jnp.concatenate([half[i * PROBE : (i + 1) * PROBE, :NZ], half[i * PROBE : (i + 1) * PROBE, NZ:]], axis=0)
                for i in range(2)
            ],
            axis=1,
        )
        backs = from_left(bh, bl, stacked)
        for i in range(2):
            back_re = backs[:PROBE, i * NZ : (i + 1) * NZ]
            back_im = backs[PROBE:, i * NZ : (i + 1) * NZ]
            rows = pl.ds(place_ref[3 + 2 * pair + i], PROBE)
            total_re[rows, :] += probe_re * back_re + probe_im * back_im
            total_im[rows, :] += probe_re * back_im - probe_im * back_re
    for ahead in range(Y):
        owner = lax.rem(y + ahead, Y)
        for tile in range(0, NR, 2):
            low = pl.ds(pl.multiple_of(tile * RAYS + owner * QR, QR), QR)
            high = pl.ds(pl.multiple_of((tile + 1) * RAYS + owner * QR, QR), QR)
            rows = slice(tile * QR, (tile + 2) * QR)
            for part, total in enumerate((total_re, total_im)):
                piece = jnp.concatenate([total[low, :], total[high, :]], axis=0)
                if ahead == 0:
                    own_ref[part, rows, :] = piece
                else:
                    (sent_one, sent_two, sent_three)[ahead - 1][part, rows, :] = piece.astype(bf16)


def shifted(value, axis, length, step):
    return lax.ppermute(value, axis, [(i, (i + step) % length) for i in range(length)])


def across(value):
    return shifted(value, "zh", ZH, 1)


def round_y(pieces):
    return [pieces[0]] + [shifted(pieces[k], "y", Y, k) for k in range(1, Y)]


def body(measured, positions, probe_field, object_field, dual_field, volume, radon_tiles, tile_range):
    zh = lax.axis_index("zh")
    zl = lax.axis_index("zl")
    y = lax.axis_index("y")
    place = jnp.concatenate([jnp.stack([zh, y, zl]).astype(jnp.int32), positions.reshape(FR_DEV)])
    radon = radon_tiles.reshape(ZL * XC, HITS, RAYS, TILE)
    volume_rows = volume.reshape(2 * TILE, NZ)
    object_rows = object_field.reshape(128, NZ)
    dual_rows = dual_field.reshape(128, NZ)

    with jax.named_scope("ray_sums"):
        object_theirs = across(object_rows)
        sums, targets = call(
            ray_sums,
            (shape(NEAR, ZL, HITS * QR, 2 * NZ, dtype=bf16), shape(QR, NZ)),
            0,
            0,
            n_far=3,
            scratch=[
                pltpu.VMEM(radon.shape, bf16),
                pltpu.VMEM((2 * TILE, NZ), f32),
                pltpu.VMEM((1, ZL * XC), jnp.int32),
                pltpu.SemaphoreType.DMA((ZL + 2,)),
            ],
            flops=2 * 2048 * 256 * 256,
            limit=SUMS_LIMIT,
        )(radon, volume_rows, tile_range.reshape(1, ZL * XC))
        near_sums = lax.all_to_all(sums, CROSS, 0, 0, tiled=True)

    with jax.named_scope("fields"):
        object_theirs, sums, targets = lax.optimization_barrier((object_theirs, sums, targets))
        packed = call(
            pack, (shape(SENT_ROWS, NZ),) * Y, 1, 4, scratch=[pltpu.VMEM((128, NZ), f32)], flops=1_000_000
        )(place, object_rows, object_theirs, dual_rows, targets)
        fields = round_y(packed)

    with jax.named_scope("frames"):
        inter_parts = call(
            frame_gradients,
            (shape(2, 128, NZ),) + (shape(2, 128, NZ, dtype=bf16),) * 3,
            1,
            7,
            scratch=[pltpu.VMEM((NDET, NZ), f32)] * 4,
            flops=FRAMES_COST,
        )(place, *fields, probe_field, measured[0], dft_blocks())
        inter_own = inter_parts[0]
        inter_parts = round_y(inter_parts)

    with jax.named_scope("targets"):
        base = FIELD_ROWS + DRIFT_ROWS
        table = jnp.concatenate([field[base : base + 1, : ZL * XC] for field in fields]).astype(jnp.int32)
        table, inter_own = lax.optimization_barrier((table, inter_own))
        tables = [table] + [shifted(table, "zl", ZL, k) for k in range(1, ZL)]

    with jax.named_scope("near_sum"):
        dense, inter = call(
            add_tiles,
            (shape(DEEP, 128, NZ, dtype=bf16), shape(2, 128, NZ)),
            5,
            9,
            scratch=[pltpu.VMEM((ZL, 128, 2 * NZ), f32)],
            flops=1_000_000,
        )(place, *tables, near_sums, *inter_parts, *fields)
        far_sums = lax.all_to_all(dense, ALONG, 0, 0, tiled=True)

    with jax.named_scope("residual"):
        copies, joint = call(
            residual_part, (shape(DEEP, 128, NZ, dtype=bf16), shape(128, NZ)), 0, 1, flops=1_000_000
        )(far_sums)
        residuals = lax.all_to_all(copies, ALONG, 0, 0, tiled=True)
        kept = call(share_out, (shape(ZH, 3, 2 * QR, NZ),) * Y, 1, 2, flops=1_000_000)(place, joint, inter)
        kept = round_y(kept)

    with jax.named_scope("pick"):
        picked = pl.pallas_call(
            pick_tiles,
            out_shape=shape(NEAR, ZL, HITS * QR, 2 * NZ, dtype=bf16),
            in_specs=[SM] * 5 + [VM],
            out_specs=FAR,
            scratch_shapes=[
                pltpu.VMEM((ZL, 128, 2 * NZ), f32),
                pltpu.VMEM((NEAR, ZL, HITS * QR, 2 * NZ), bf16),
                pltpu.SemaphoreType.DMA((NEAR,)),
            ],
            compiler_params=pltpu.CompilerParams(vmem_limit_bytes=48 << 20),
            cost_estimate=pl.CostEstimate(flops=1_000_000, bytes_accessed=1 << 20, transcendentals=0),
            name="pick_tiles",
        )(place, *tables, residuals)
        picked, kept = lax.optimization_barrier((picked, kept))
        returned = lax.all_to_all(picked, CROSS, 0, 0, tiled=True)

    with jax.named_scope("updates"):
        theirs = across(jnp.stack([piece[1] for piece in kept]))
        object_next, dual_next = call(updates, (shape(128, NZ), shape(128, NZ)), 1, 7, flops=1_000_000)(
            place, *kept, theirs, object_rows, dual_rows
        )

    with jax.named_scope("back_project"):
        ordered = radon.reshape(ZL, XC, HITS, Y, QR, TILE).transpose(5, 1, 3, 0, 2, 4).reshape(TILE, -1)
        volume_next = call(back_project, shape(2 * TILE, NZ), 0, 3, flops=2 * 2048 * 256 * 256)(
            ordered, returned, volume_rows
        )
    return (
        object_next.reshape(object_field.shape),
        dual_next.reshape(dual_field.shape),
        volume_next.reshape(volume.shape),
    )


def solution(mesh):
    fine = Mesh(mesh.devices.reshape(ZL, X, C, ZH, Y), ("zl", "x", "c", "zh", "y"))
    ang = ("zl", "x", "c")
    strip = ("zh", "y")
    return jax.shard_map(
        body,
        mesh=fine,
        in_specs=(
            P(ang, strip, None, None),
            P(ang, strip),
            P(),
            P(ang, strip, None, None),
            P(ang, strip, None, None),
            P(ang + strip, None, None),
            P(ang + strip, None, None, None, None),
            P(ang, None, strip, None),
        ),
        out_specs=(
            P(ang, strip, None, None),
            P(ang, strip, None, None),
            P(ang + strip, None, None),
        ),
        check_vma=False,
    )
```

```python
import math

import jax
import jax.numpy as jnp
import numpy as np
from jax import lax
from jax.experimental import pallas as pl
from jax.experimental.pallas import tpu as pltpu
from jax.sharding import Mesh
from jax.sharding import PartitionSpec as P

PROBE = 128
NZ = 128
NDET = 512
RAYS = 32
TILE = 256
HITS = 2
NR = 16

ZL, X, C, ZH, Y = 4, 4, 2, 2, 4
XC = X * C
CROSS = ("x", "c", "y")
ALONG = ("zh", "zl")
NEAR = XC * Y
DEEP = ZH * ZL
QR = RAYS // Y
FR_DEV = 8
FRAMES_COST = 20_000_000_000
SUMS_LIMIT = 62 << 20

penalty = 1.0
object_step = 0.1
volume_step = 1.0
keep = 1.0 - object_step
share = object_step / keep
f32 = jnp.float32
bf16 = jnp.bfloat16

VM = pl.BlockSpec(memory_space=pltpu.VMEM)
SM = pl.BlockSpec(memory_space=pltpu.SMEM)
FAR = pl.BlockSpec(memory_space=pltpu.HBM)


def call(kernel, outs, n_smem, n_vmem, scratch=(), flops=0, moved=1 << 20, limit=48 << 20, n_far=0):
    many = isinstance(outs, tuple)
    return pl.pallas_call(
        kernel,
        out_shape=outs,
        in_specs=[SM] * n_smem + [FAR] * n_far + [VM] * n_vmem,
        out_specs=tuple(VM for _ in outs) if many else VM,
        scratch_shapes=list(scratch),
        compiler_params=pltpu.CompilerParams(vmem_limit_bytes=limit),
        cost_estimate=pl.CostEstimate(flops=flops, bytes_accessed=moved, transcendentals=0),
        name=kernel.__name__,
    )


def shape(*dims, dtype=f32):
    return jax.ShapeDtypeStruct(dims, dtype)


def dft_blocks():
    k = np.arange(PROBE)
    angles = (k[:, None] * k[None, :] % PROBE) * (2.0 * math.pi / PROBE)
    cosine = np.cos(angles) / math.sqrt(PROBE)
    sine = np.sin(angles) / math.sqrt(PROBE)
    both = np.stack([cosine, sine]).astype(np.float32)
    high = both.astype(jnp.bfloat16)
    low = (both - high.astype(np.float32)).astype(jnp.bfloat16)
    return jnp.asarray(np.concatenate([high, low]))


def ray_sums(radon_far, volume_far, target_far, out_ref, target_out, radon_ref, volume_ref, target_ref, sems):
    targets = pltpu.make_async_copy(target_far, target_ref, sems.at[ZL + 1])
    targets.start()
    copies = [pltpu.make_async_copy(volume_far, volume_ref, sems.at[ZL])]
    for zl in range(ZL):
        angles = pl.ds(zl * XC, XC)
        copies.append(pltpu.make_async_copy(radon_far.at[angles], radon_ref.at[angles], sems.at[zl]))
    for copy in copies:
        copy.start()
    copies[0].wait()
    volume_half = jnp.concatenate(
        [volume_ref[pl.ds(0, TILE, stride=2), :], volume_ref[pl.ds(1, TILE, stride=2), :]], axis=1
    ).astype(bf16)
    for zl in range(ZL):
        copies[1 + zl].wait()
        for xc in range(XC):
            rows = radon_ref[zl * XC + xc].reshape(HITS * RAYS, TILE)
            sums = jnp.dot(rows, volume_half, preferred_element_type=f32)
            for y in range(Y):
                low = sums[y * QR : (y + 1) * QR]
                high = sums[RAYS + y * QR : RAYS + (y + 1) * QR]
                out_ref[xc * Y + y, zl] = jnp.concatenate([low, high], axis=0).astype(bf16)
    targets.wait()
    target_out[...] = jnp.zeros(target_out.shape, f32)
    target_out[0:1, : ZL * XC] = target_ref[...].astype(f32)


def tile_groups(place_ref, tables, count):
    zl_here = place_ref[2]
    angles = [lax.rem(zl_here + ZL - back_zl, ZL) for back_zl in range(ZL)]
    groups = []
    for back_y in range(Y):
        y = lax.rem(place_ref[1] + Y - back_y, Y)
        for xc in range(XC):
            for zl, table in zip(angles, tables):
                row = table[back_y, zl_here * XC + xc] * QR
                groups.append((zl, xc * Y + y, pl.ds(pl.multiple_of(row, QR), HITS * QR)))
                if len(groups) == count:
                    yield groups
                    groups = []


def add_tiles(
    place_ref, table_0, table_1, table_2, table_3, sums_ref, inter_0, inter_1, inter_2, inter_3,
    field_0, field_1, field_2, field_3, out_ref, inter_ref, total,
):
    zh = place_ref[0]
    y_here = place_ref[1]
    zl_here = place_ref[2]
    total[...] = jnp.zeros(total.shape, f32)
    for part in range(2):
        inter = (inter_0[part] + inter_1[part].astype(f32)) + (inter_2[part].astype(f32) + inter_3[part].astype(f32))
        inter_ref[part] = inter
        total[zl_here, :, part * NZ : (part + 1) * NZ] = inter * share
    for back, field_ref in enumerate((field_0, field_1, field_2, field_3)):
        owner = zh * Y + lax.rem(y_here + Y - back, Y)
        rows = pl.ds(pl.multiple_of(owner * 2 * QR, 2 * QR), 2 * QR)
        base = FIELD_ROWS
        total[zl_here, rows, :] -= jnp.concatenate(
            [field_ref[base : base + 2 * QR, :], field_ref[base + 2 * QR : base + 4 * QR, :]], axis=1
        )
    for group in tile_groups(place_ref, (table_0, table_1, table_2, table_3), ZL):
        added = [total[zl, rows, :] + sums_ref[near, zl].astype(f32) for zl, near, rows in group]
        for (zl, near, rows), value in zip(group, added):
            total[zl, rows, :] = value
    for zh in range(ZH):
        for zl in range(ZL):
            out_ref[zh * ZL + zl] = total[zl, :, zh * NZ : (zh + 1) * NZ].astype(bf16)


def residual_part(sums_ref, residual_ref, joint_ref):
    total = sums_ref[0].astype(f32)
    for source in range(1, DEEP):
        total = total + sums_ref[source].astype(f32)
    joint_ref[...] = total
    residual = (keep * total).astype(bf16)
    for copy in range(DEEP):
        residual_ref[copy] = residual


def share_out(place_ref, joint_ref, inter_ref, own_ref, one_ref, two_ref, three_ref):
    zh = place_ref[0]
    y = place_ref[1]
    for ahead, ref in enumerate((own_ref, one_ref, two_ref, three_ref)):
        for other in range(ZH):
            owner = lax.rem(zh + other, ZH) * Y + lax.rem(y + ahead, Y)
            rows = pl.ds(pl.multiple_of(owner * 2 * QR, 2 * QR), 2 * QR)
            ref[other, 0] = joint_ref[rows, :]
            for part in range(2):
                ref[other, 1 + part] = inter_ref[part, rows, :]


def pick_tiles(place_ref, table_0, table_1, table_2, table_3, residual_ref, out_ref, rows_ref):
    for zl in range(ZL):
        rows_ref[zl] = jnp.concatenate(
            [residual_ref[zl].astype(f32), residual_ref[ZL + zl].astype(f32)], axis=1
        )

    for group in tile_groups(place_ref, (table_0, table_1, table_2, table_3), 2 * ZL):
        picked = [rows_ref[zl, rows, :].astype(bf16) for zl, near, rows in group]
        for (zl, near, rows), value in zip(group, picked):
            out_ref[near, zl] = value


def back_project(radon_ref, picked_ref, volume_ref, out_ref):
    gradient = jnp.dot(
        radon_ref[...],
        picked_ref[...].reshape(NEAR * ZL * HITS * QR, 2 * NZ),
        preferred_element_type=f32,
    )
    for part in range(2):
        rows = pl.ds(part, TILE, stride=2)
        out_ref[rows, :] = volume_ref[rows, :] - volume_step * gradient[:, part * NZ : (part + 1) * NZ]


def updates(
    place_ref, own_ref, one_ref, two_ref, three_ref, theirs_ref, object_ref, dual_ref, object_out, dual_out
):
    zh = place_ref[0]
    y = place_ref[1]
    for back, ref in enumerate((own_ref, one_ref, two_ref, three_ref)):
        source = lax.rem(y + Y - back, Y)
        for other in range(ZH):
            part = lax.rem(zh + other, ZH)
            for tile in range(2):
                piece = slice(tile * QR, (tile + 1) * QR)
                inter = ref[0, 1 + part, piece, :] + theirs_ref[back, 1 + part, piece, :]
                joint = theirs_ref[back, 0, piece, :] if other else ref[0, 0, piece, :]
                rows = pl.ds((tile * RAYS + source * QR) * 2 + part, QR, stride=2)
                field = object_ref[rows, :]
                dual = dual_ref[rows, :]
                projection = joint + (field + dual) - share * inter
                object_next = field - object_step * (inter + dual + penalty * (field - projection))
                object_out[rows, :] = object_next
                dual_out[rows, :] = dual + penalty * (object_next - projection)


def split(value):
    high = value.astype(bf16)
    return high, (value - high.astype(f32)).astype(bf16)


def complex_blocks(cosine, sine):
    forward = jnp.concatenate(
        [jnp.concatenate([cosine, sine], axis=1), jnp.concatenate([-sine, cosine], axis=1)], axis=0
    )
    backward = jnp.concatenate(
        [jnp.concatenate([cosine, -sine], axis=1), jnp.concatenate([sine, cosine], axis=1)], axis=0
    )
    return forward, backward


def from_left(high_table, low_table, value):
    high, low = split(value)
    return (
        jnp.dot(high_table, high, preferred_element_type=f32)
        + jnp.dot(high_table, low, preferred_element_type=f32)
        + jnp.dot(low_table, high, preferred_element_type=f32)
    )


def from_right(value, high_table, low_table):
    high, low = split(value)
    return (
        jnp.dot(high, high_table, preferred_element_type=f32)
        + jnp.dot(low, high_table, preferred_element_type=f32)
        + jnp.dot(high, low_table, preferred_element_type=f32)
    )


FIELD_ROWS = 2 * 128
DRIFT_ROWS = 4 * QR
SENT_ROWS = FIELD_ROWS + DRIFT_ROWS + QR


def pack(place_ref, object_ref, theirs_ref, dual_ref, target_ref, own_ref, one_ref, two_ref, three_ref, both):
    y = place_ref[1]
    both[...] = object_ref[...] + dual_ref[...]
    for ahead, ref in enumerate((own_ref, one_ref, two_ref, three_ref)):
        ref[0:128, :] = object_ref[...]
        ref[128:256, :] = theirs_ref[...]
        ref[FIELD_ROWS + DRIFT_ROWS :, :] = target_ref[...]
        for part in range(2):
            for tile in range(2):
                start = (tile * RAYS + lax.rem(y + ahead, Y) * QR) * 2 + part
                base = FIELD_ROWS + (part * 2 + tile) * QR
                ref[base : base + QR, :] = both[pl.ds(start, QR, stride=2), :]


def frame_gradients(
    place_ref, field_0, field_1, field_2, field_3, probe_ref, measured_ref, dft_ref, own_ref, sent_one, sent_two, sent_three,
    field_re, field_im, total_re, total_im,
):
    zh = place_ref[0]
    y = place_ref[1]
    for back, field_ref in enumerate((field_0, field_1, field_2, field_3)):
        for other in range(ZH):
            owner = lax.rem(zh + other, ZH) * Y + lax.rem(y + Y - back, Y)
            rows = pl.ds(pl.multiple_of(owner * 64, 64), 64)
            field_re[rows, :] = field_ref[pl.ds(other * 128, 64, stride=2), :]
            field_im[rows, :] = field_ref[pl.ds(other * 128 + 1, 64, stride=2), :]
    total_re[...] = jnp.zeros(total_re.shape, f32)
    total_im[...] = jnp.zeros(total_im.shape, f32)
    probe_re = probe_ref[0]
    probe_im = probe_ref[1]
    ah, bh = complex_blocks(dft_ref[0], dft_ref[1])
    al, bl = complex_blocks(dft_ref[2], dft_ref[3])
    frames = [pl.ds(place_ref[3 + frame], PROBE) for frame in range(FR_DEV)]
    waves = []
    for rows in frames:
        object_re = field_re[rows, :]
        object_im = field_im[rows, :]
        waves.append(
            jnp.concatenate(
                [probe_re * object_re - probe_im * object_im, probe_re * object_im + probe_im * object_re], axis=0
            )
        )
    lefts = from_left(ah, al, jnp.concatenate(waves, axis=1))
    sides = jnp.concatenate(
        [
            jnp.concatenate([lefts[:PROBE, i * NZ : (i + 1) * NZ], lefts[PROBE:, i * NZ : (i + 1) * NZ]], axis=1)
            for i in range(FR_DEV)
        ],
        axis=0,
    )
    far = from_right(sides, bh, bl)
    far_re = far[:, :NZ]
    far_im = far[:, NZ:]
    modulus = jnp.sqrt(far_re * far_re + far_im * far_im)
    intensity = measured_ref[...].reshape(FR_DEV * PROBE, NZ)
    shrink = 1.0 - jnp.sqrt(intensity) / jnp.maximum(modulus, 1.0)
    half = from_right(jnp.concatenate([far_re * shrink, far_im * shrink], axis=1), ah, al)
    stacked = jnp.concatenate(
        [
            jnp.concatenate([half[i * PROBE : (i + 1) * PROBE, :NZ], half[i * PROBE : (i + 1) * PROBE, NZ:]], axis=0)
            for i in range(FR_DEV)
        ],
        axis=1,
    )
    backs = from_left(bh, bl, stacked)
    for i, rows in enumerate(frames):
        back_re = backs[:PROBE, i * NZ : (i + 1) * NZ]
        back_im = backs[PROBE:, i * NZ : (i + 1) * NZ]
        total_re[rows, :] += probe_re * back_re + probe_im * back_im
        total_im[rows, :] += probe_re * back_im - probe_im * back_re
    for ahead in range(Y):
        owner = lax.rem(y + ahead, Y)
        for tile in range(0, NR, 2):
            low = pl.ds(pl.multiple_of(tile * RAYS + owner * QR, QR), QR)
            high = pl.ds(pl.multiple_of((tile + 1) * RAYS + owner * QR, QR), QR)
            rows = slice(tile * QR, (tile + 2) * QR)
            for part, total in enumerate((total_re, total_im)):
                piece = jnp.concatenate([total[low, :], total[high, :]], axis=0)
                if ahead == 0:
                    own_ref[part, rows, :] = piece
                else:
                    (sent_one, sent_two, sent_three)[ahead - 1][part, rows, :] = piece.astype(bf16)


def shifted(value, axis, length, step):
    return lax.ppermute(value, axis, [(i, (i + step) % length) for i in range(length)])


def across(value):
    return shifted(value, "zh", ZH, 1)


def round_y(pieces):
    return [pieces[0]] + [shifted(pieces[k], "y", Y, k) for k in range(1, Y)]


def body(measured, positions, probe_field, object_field, dual_field, volume, radon_tiles, tile_range):
    zh = lax.axis_index("zh")
    zl = lax.axis_index("zl")
    y = lax.axis_index("y")
    place = jnp.concatenate([jnp.stack([zh, y, zl]).astype(jnp.int32), positions.reshape(FR_DEV)])
    radon = radon_tiles.reshape(ZL * XC, HITS, RAYS, TILE)
    volume_rows = volume.reshape(2 * TILE, NZ)
    object_rows = object_field.reshape(128, NZ)
    dual_rows = dual_field.reshape(128, NZ)

    with jax.named_scope("ray_sums"):
        object_theirs = across(object_rows)
        sums, targets = call(
            ray_sums,
            (shape(NEAR, ZL, HITS * QR, 2 * NZ, dtype=bf16), shape(QR, NZ)),
            0,
            0,
            n_far=3,
            scratch=[
                pltpu.VMEM(radon.shape, bf16),
                pltpu.VMEM((2 * TILE, NZ), f32),
                pltpu.VMEM((1, ZL * XC), jnp.int32),
                pltpu.SemaphoreType.DMA((ZL + 2,)),
            ],
            flops=2 * 2048 * 256 * 256,
            limit=SUMS_LIMIT,
        )(radon, volume_rows, tile_range.reshape(1, ZL * XC))
        near_sums = lax.all_to_all(sums, CROSS, 0, 0, tiled=True)

    with jax.named_scope("fields"):
        object_theirs, sums, targets = lax.optimization_barrier((object_theirs, sums, targets))
        packed = call(
            pack, (shape(SENT_ROWS, NZ),) * Y, 1, 4, scratch=[pltpu.VMEM((128, NZ), f32)], flops=1_000_000
        )(place, object_rows, object_theirs, dual_rows, targets)
        fields = round_y(packed)

    with jax.named_scope("frames"):
        inter_parts = call(
            frame_gradients,
            (shape(2, 128, NZ),) + (shape(2, 128, NZ, dtype=bf16),) * 3,
            1,
            7,
            scratch=[pltpu.VMEM((NDET, NZ), f32)] * 4,
            flops=FRAMES_COST,
        )(place, *fields, probe_field, measured[0], dft_blocks())
        inter_own = inter_parts[0]
        inter_parts = round_y(inter_parts)

    with jax.named_scope("targets"):
        base = FIELD_ROWS + DRIFT_ROWS
        table = jnp.concatenate([field[base : base + 1, : ZL * XC] for field in fields]).astype(jnp.int32)
        table, inter_own = lax.optimization_barrier((table, inter_own))
        tables = [table] + [shifted(table, "zl", ZL, k) for k in range(1, ZL)]

    with jax.named_scope("near_sum"):
        dense, inter = call(
            add_tiles,
            (shape(DEEP, 128, NZ, dtype=bf16), shape(2, 128, NZ)),
            5,
            9,
            scratch=[pltpu.VMEM((ZL, 128, 2 * NZ), f32)],
            flops=1_000_000,
        )(place, *tables, near_sums, *inter_parts, *fields)
        far_sums = lax.all_to_all(dense, ALONG, 0, 0, tiled=True)

    with jax.named_scope("residual"):
        copies, joint = call(
            residual_part, (shape(DEEP, 128, NZ, dtype=bf16), shape(128, NZ)), 0, 1, flops=1_000_000
        )(far_sums)
        residuals = lax.all_to_all(copies, ALONG, 0, 0, tiled=True)
        kept = call(share_out, (shape(ZH, 3, 2 * QR, NZ),) * Y, 1, 2, flops=1_000_000)(place, joint, inter)
        kept = round_y(kept)

    with jax.named_scope("pick"):
        picked = call(
            pick_tiles,
            shape(NEAR, ZL, HITS * QR, 2 * NZ, dtype=bf16),
            5,
            1,
            scratch=[pltpu.VMEM((ZL, 128, 2 * NZ), f32)],
            flops=1_000_000,
        )(place, *tables, residuals)
        picked, kept = lax.optimization_barrier((picked, kept))
        returned = lax.all_to_all(picked, CROSS, 0, 0, tiled=True)

    with jax.named_scope("updates"):
        theirs = across(jnp.stack([piece[1] for piece in kept]))
        object_next, dual_next = call(updates, (shape(128, NZ), shape(128, NZ)), 1, 7, flops=1_000_000)(
            place, *kept, theirs, object_rows, dual_rows
        )

    with jax.named_scope("back_project"):
        ordered = radon.reshape(ZL, XC, HITS, Y, QR, TILE).transpose(5, 1, 3, 0, 2, 4).reshape(TILE, -1)
        volume_next = call(back_project, shape(2 * TILE, NZ), 0, 3, flops=2 * 2048 * 256 * 256)(
            ordered, returned, volume_rows
        )
    return (
        object_next.reshape(object_field.shape),
        dual_next.reshape(dual_field.shape),
        volume_next.reshape(volume.shape),
    )


def solution(mesh):
    fine = Mesh(mesh.devices.reshape(ZL, X, C, ZH, Y), ("zl", "x", "c", "zh", "y"))
    ang = ("zl", "x", "c")
    strip = ("zh", "y")
    return jax.shard_map(
        body,
        mesh=fine,
        in_specs=(
            P(ang, strip, None, None),
            P(ang, strip),
            P(),
            P(ang, strip, None, None),
            P(ang, strip, None, None),
            P(ang + strip, None, None),
            P(ang + strip, None, None, None, None),
            P(ang, None, strip, None),
        ),
        out_specs=(
            P(ang, strip, None, None),
            P(ang, strip, None, None),
            P(ang + strip, None, None),
        ),
        check_vma=False,
    )
```

```python
import math

import jax
import jax.numpy as jnp
import numpy as np
from jax import lax
from jax.experimental import pallas as pl
from jax.experimental.pallas import tpu as pltpu
from jax.sharding import Mesh
from jax.sharding import PartitionSpec as P

PROBE = 128
NZ = 128
NDET = 512
RAYS = 32
TILE = 256
HITS = 2
NR = 16

ZL, X, C, ZH, Y = 4, 4, 2, 2, 4
XC = X * C
CROSS = ("x", "c", "y")
ALONG = ("zh", "zl")
NEAR = XC * Y
DEEP = ZH * ZL
QR = RAYS // Y
FR_DEV = 8
FRAMES_COST = 20_000_000_000
SUMS_LIMIT = 62 << 20

penalty = 1.0
object_step = 0.1
volume_step = 1.0
keep = 1.0 - object_step
share = object_step / keep
f32 = jnp.float32
bf16 = jnp.bfloat16
f16 = jnp.float16

VM = pl.BlockSpec(memory_space=pltpu.VMEM)
SM = pl.BlockSpec(memory_space=pltpu.SMEM)
FAR = pl.BlockSpec(memory_space=pltpu.HBM)


def call(kernel, outs, n_smem, n_vmem, scratch=(), flops=0, moved=1 << 20, limit=48 << 20, n_far=0):
    many = isinstance(outs, tuple)
    return pl.pallas_call(
        kernel,
        out_shape=outs,
        in_specs=[SM] * n_smem + [FAR] * n_far + [VM] * n_vmem,
        out_specs=tuple(VM for _ in outs) if many else VM,
        scratch_shapes=list(scratch),
        compiler_params=pltpu.CompilerParams(vmem_limit_bytes=limit),
        cost_estimate=pl.CostEstimate(flops=flops, bytes_accessed=moved, transcendentals=0),
        name=kernel.__name__,
    )


def shape(*dims, dtype=f32):
    return jax.ShapeDtypeStruct(dims, dtype)


def dft_blocks():
    k = np.arange(PROBE)
    angles = (k[:, None] * k[None, :] % PROBE) * (2.0 * math.pi / PROBE)
    cosine = np.cos(angles) / math.sqrt(PROBE)
    sine = np.sin(angles) / math.sqrt(PROBE)
    both = np.stack([cosine, sine]).astype(np.float32)
    high = both.astype(jnp.bfloat16)
    low = (both - high.astype(np.float32)).astype(jnp.bfloat16)
    return jnp.asarray(np.concatenate([high, low]))


def ray_sums(radon_far, volume_far, target_far, out_ref, target_out, radon_ref, volume_ref, target_ref, sems):
    targets = pltpu.make_async_copy(target_far, target_ref, sems.at[ZL + 1])
    targets.start()
    copies = [pltpu.make_async_copy(volume_far, volume_ref, sems.at[ZL])]
    for zl in range(ZL):
        angles = pl.ds(zl * XC, XC)
        copies.append(pltpu.make_async_copy(radon_far.at[angles], radon_ref.at[angles], sems.at[zl]))
    for copy in copies:
        copy.start()
    copies[0].wait()
    volume_half = jnp.concatenate(
        [volume_ref[pl.ds(0, TILE, stride=2), :], volume_ref[pl.ds(1, TILE, stride=2), :]], axis=1
    ).astype(bf16)
    for zl in range(ZL):
        copies[1 + zl].wait()
        for xc in range(XC):
            rows = radon_ref[zl * XC + xc].reshape(HITS * RAYS, TILE)
            sums = jnp.dot(rows, volume_half, preferred_element_type=f32)
            for y in range(Y):
                low = sums[y * QR : (y + 1) * QR]
                high = sums[RAYS + y * QR : RAYS + (y + 1) * QR]
                out_ref[xc * Y + y, zl] = jnp.concatenate([low, high], axis=0).astype(bf16)
    targets.wait()
    target_out[...] = jnp.zeros(target_out.shape, f32)
    target_out[0:1, : ZL * XC] = target_ref[...].astype(f32)


def tile_groups(place_ref, tables, count):
    zl_here = place_ref[2]
    angles = [lax.rem(zl_here + ZL - back_zl, ZL) for back_zl in range(ZL)]
    groups = []
    for back_y in range(Y):
        y = lax.rem(place_ref[1] + Y - back_y, Y)
        for xc in range(XC):
            for zl, table in zip(angles, tables):
                row = table[back_y, zl_here * XC + xc] * QR
                groups.append((zl, xc * Y + y, pl.ds(pl.multiple_of(row, QR), HITS * QR)))
                if len(groups) == count:
                    yield groups
                    groups = []


def add_tiles(
    place_ref, table_0, table_1, table_2, table_3, sums_ref, inter_0, inter_1, inter_2, inter_3,
    field_0, field_1, field_2, field_3, out_ref, inter_ref, total,
):
    zh = place_ref[0]
    y_here = place_ref[1]
    zl_here = place_ref[2]
    total[...] = jnp.zeros(total.shape, f32)
    for part in range(2):
        inter = (inter_0[part] + inter_1[part].astype(f32)) + (inter_2[part].astype(f32) + inter_3[part].astype(f32))
        inter_ref[part] = inter
        total[zl_here, :, part * NZ : (part + 1) * NZ] = inter * share
    for back, field_ref in enumerate((field_0, field_1, field_2, field_3)):
        owner = zh * Y + lax.rem(y_here + Y - back, Y)
        rows = pl.ds(pl.multiple_of(owner * 2 * QR, 2 * QR), 2 * QR)
        base = FIELD_ROWS
        total[zl_here, rows, :] -= jnp.concatenate(
            [field_ref[base : base + 2 * QR, :], field_ref[base + 2 * QR : base + 4 * QR, :]], axis=1
        )
    for group in tile_groups(place_ref, (table_0, table_1, table_2, table_3), ZL):
        added = [total[zl, rows, :] + sums_ref[near, zl].astype(f32) for zl, near, rows in group]
        for (zl, near, rows), value in zip(group, added):
            total[zl, rows, :] = value
    for zh in range(ZH):
        for zl in range(ZL):
            out_ref[zh * ZL + zl] = total[zl, :, zh * NZ : (zh + 1) * NZ].astype(bf16)


def residual_part(sums_ref, residual_ref, joint_ref):
    total = sums_ref[0].astype(f32)
    for source in range(1, DEEP):
        total = total + sums_ref[source].astype(f32)
    joint_ref[...] = total
    residual = (keep * total).astype(bf16)
    for copy in range(DEEP):
        residual_ref[copy] = residual


def share_out(place_ref, joint_ref, inter_ref, own_ref, one_ref, two_ref, three_ref):
    zh = place_ref[0]
    y = place_ref[1]
    for ahead, ref in enumerate((own_ref, one_ref, two_ref, three_ref)):
        for other in range(ZH):
            owner = lax.rem(zh + other, ZH) * Y + lax.rem(y + ahead, Y)
            rows = pl.ds(pl.multiple_of(owner * 2 * QR, 2 * QR), 2 * QR)
            ref[other, 0] = joint_ref[rows, :]
            for part in range(2):
                ref[other, 1 + part] = inter_ref[part, rows, :]


def pick_tiles(place_ref, table_0, table_1, table_2, table_3, residual_ref, out_ref, rows_ref):
    for zl in range(ZL):
        rows_ref[zl] = jnp.concatenate(
            [residual_ref[zl].astype(f32), residual_ref[ZL + zl].astype(f32)], axis=1
        )

    for group in tile_groups(place_ref, (table_0, table_1, table_2, table_3), 2 * ZL):
        picked = [rows_ref[zl, rows, :].astype(bf16) for zl, near, rows in group]
        for (zl, near, rows), value in zip(group, picked):
            out_ref[near, zl] = value


def back_project(radon_ref, picked_ref, volume_ref, out_ref):
    gradient = jnp.dot(
        radon_ref[...],
        picked_ref[...].reshape(NEAR * ZL * HITS * QR, 2 * NZ),
        preferred_element_type=f32,
    )
    for part in range(2):
        rows = pl.ds(part, TILE, stride=2)
        out_ref[rows, :] = volume_ref[rows, :] - volume_step * gradient[:, part * NZ : (part + 1) * NZ]


def updates(
    place_ref, own_ref, one_ref, two_ref, three_ref, theirs_ref, object_ref, dual_ref, object_out, dual_out
):
    zh = place_ref[0]
    y = place_ref[1]
    for back, ref in enumerate((own_ref, one_ref, two_ref, three_ref)):
        source = lax.rem(y + Y - back, Y)
        for other in range(ZH):
            part = lax.rem(zh + other, ZH)
            for tile in range(2):
                piece = slice(tile * QR, (tile + 1) * QR)
                inter = ref[0, 1 + part, piece, :] + theirs_ref[back, 1 + part, piece, :]
                joint = theirs_ref[back, 0, piece, :] if other else ref[0, 0, piece, :]
                rows = pl.ds((tile * RAYS + source * QR) * 2 + part, QR, stride=2)
                field = object_ref[rows, :]
                dual = dual_ref[rows, :]
                projection = joint + (field + dual) - share * inter
                object_next = field - object_step * (inter + dual + penalty * (field - projection))
                object_out[rows, :] = object_next
                dual_out[rows, :] = dual + penalty * (object_next - projection)


def split(value):
    high = value.astype(bf16)
    return high, (value - high.astype(f32)).astype(bf16)


def complex_blocks(cosine, sine):
    forward = jnp.concatenate(
        [jnp.concatenate([cosine, sine], axis=1), jnp.concatenate([-sine, cosine], axis=1)], axis=0
    )
    backward = jnp.concatenate(
        [jnp.concatenate([cosine, -sine], axis=1), jnp.concatenate([sine, cosine], axis=1)], axis=0
    )
    return forward, backward


def from_left(high_table, low_table, value):
    high, low = split(value)
    return (
        jnp.dot(high_table, high, preferred_element_type=f32)
        + jnp.dot(high_table, low, preferred_element_type=f32)
        + jnp.dot(low_table, high, preferred_element_type=f32)
    )


def from_right(value, high_table, low_table):
    high, low = split(value)
    return (
        jnp.dot(high, high_table, preferred_element_type=f32)
        + jnp.dot(low, high_table, preferred_element_type=f32)
        + jnp.dot(high, low_table, preferred_element_type=f32)
    )


FIELD_ROWS = 2 * 128
DRIFT_ROWS = 4 * QR
OWN_ROWS = 128 + DRIFT_ROWS + QR


def pack(place_ref, object_ref, dual_ref, target_ref, own_ref, one_ref, two_ref, three_ref, both):
    y = place_ref[1]
    both[...] = object_ref[...] + dual_ref[...]
    for ahead, ref in enumerate((own_ref, one_ref, two_ref, three_ref)):
        ref[0:128, :] = object_ref[...]
        ref[128 + DRIFT_ROWS :, :] = target_ref[...]
        for part in range(2):
            for tile in range(2):
                start = (tile * RAYS + lax.rem(y + ahead, Y) * QR) * 2 + part
                base = 128 + (part * 2 + tile) * QR
                ref[base : base + QR, :] = both[pl.ds(start, QR, stride=2), :]


def frame_gradients(
    place_ref, field_0, field_1, field_2, field_3, probe_ref, measured_ref, dft_ref, own_ref, sent_one, sent_two, sent_three,
    field_re, field_im, total_re, total_im,
):
    zh = place_ref[0]
    y = place_ref[1]
    for back, field_ref in enumerate((field_0, field_1, field_2, field_3)):
        for other in range(ZH):
            owner = lax.rem(zh + other, ZH) * Y + lax.rem(y + Y - back, Y)
            rows = pl.ds(pl.multiple_of(owner * 64, 64), 64)
            field_re[rows, :] = field_ref[pl.ds((1 - other) * 128, 64, stride=2), :]
            field_im[rows, :] = field_ref[pl.ds((1 - other) * 128 + 1, 64, stride=2), :]
    total_re[...] = jnp.zeros(total_re.shape, f32)
    total_im[...] = jnp.zeros(total_im.shape, f32)
    probe_re = probe_ref[0]
    probe_im = probe_ref[1]
    ah, bh = complex_blocks(dft_ref[0], dft_ref[1])
    al, bl = complex_blocks(dft_ref[2], dft_ref[3])
    frames = [pl.ds(place_ref[3 + frame], PROBE) for frame in range(FR_DEV)]
    waves = []
    for rows in frames:
        object_re = field_re[rows, :]
        object_im = field_im[rows, :]
        waves.append(
            jnp.concatenate(
                [probe_re * object_re - probe_im * object_im, probe_re * object_im + probe_im * object_re], axis=0
            )
        )
    lefts = from_left(ah, al, jnp.concatenate(waves, axis=1))
    sides = jnp.concatenate(
        [
            jnp.concatenate([lefts[:PROBE, i * NZ : (i + 1) * NZ], lefts[PROBE:, i * NZ : (i + 1) * NZ]], axis=1)
            for i in range(FR_DEV)
        ],
        axis=0,
    )
    far = from_right(sides, bh, bl)
    far_re = far[:, :NZ]
    far_im = far[:, NZ:]
    modulus = jnp.sqrt(far_re * far_re + far_im * far_im)
    intensity = measured_ref[...].reshape(FR_DEV * PROBE, NZ)
    shrink = 1.0 - jnp.sqrt(intensity) / jnp.maximum(modulus, 1.0)
    half = from_right(jnp.concatenate([far_re * shrink, far_im * shrink], axis=1), ah, al)
    stacked = jnp.concatenate(
        [
            jnp.concatenate([half[i * PROBE : (i + 1) * PROBE, :NZ], half[i * PROBE : (i + 1) * PROBE, NZ:]], axis=0)
            for i in range(FR_DEV)
        ],
        axis=1,
    )
    backs = from_left(bh, bl, stacked)
    for i, rows in enumerate(frames):
        back_re = backs[:PROBE, i * NZ : (i + 1) * NZ]
        back_im = backs[PROBE:, i * NZ : (i + 1) * NZ]
        total_re[rows, :] += probe_re * back_re + probe_im * back_im
        total_im[rows, :] += probe_re * back_im - probe_im * back_re
    for ahead in range(Y):
        owner = lax.rem(y + ahead, Y)
        for tile in range(0, NR, 2):
            low = pl.ds(pl.multiple_of(tile * RAYS + owner * QR, QR), QR)
            high = pl.ds(pl.multiple_of((tile + 1) * RAYS + owner * QR, QR), QR)
            rows = slice(tile * QR, (tile + 2) * QR)
            for part, total in enumerate((total_re, total_im)):
                piece = jnp.concatenate([total[low, :], total[high, :]], axis=0)
                if ahead == 0:
                    own_ref[part, rows, :] = piece
                else:
                    (sent_one, sent_two, sent_three)[ahead - 1][part, rows, :] = piece.astype(bf16)


def shifted(value, axis, length, step):
    return lax.ppermute(value, axis, [(i, (i + step) % length) for i in range(length)])


def across(value):
    return shifted(value, "zh", ZH, 1)


def round_y(pieces):
    return [pieces[0]] + [shifted(pieces[k], "y", Y, k) for k in range(1, Y)]


def body(measured, positions, probe_field, object_field, dual_field, volume, radon_tiles, tile_range):
    zh = lax.axis_index("zh")
    zl = lax.axis_index("zl")
    y = lax.axis_index("y")
    place = jnp.concatenate([jnp.stack([zh, y, zl]).astype(jnp.int32), positions.reshape(FR_DEV)])
    radon = radon_tiles.reshape(ZL * XC, HITS, RAYS, TILE)
    volume_rows = volume.reshape(2 * TILE, NZ)
    object_rows = object_field.reshape(128, NZ)
    dual_rows = dual_field.reshape(128, NZ)

    with jax.named_scope("ray_sums"):
        object_theirs = across(object_rows.astype(f16))
        sums, targets = call(
            ray_sums,
            (shape(NEAR, ZL, HITS * QR, 2 * NZ, dtype=bf16), shape(QR, NZ)),
            0,
            0,
            n_far=3,
            scratch=[
                pltpu.VMEM(radon.shape, bf16),
                pltpu.VMEM((2 * TILE, NZ), f32),
                pltpu.VMEM((1, ZL * XC), jnp.int32),
                pltpu.SemaphoreType.DMA((ZL + 2,)),
            ],
            flops=2 * 2048 * 256 * 256,
            limit=SUMS_LIMIT,
        )(radon, volume_rows, tile_range.reshape(1, ZL * XC))
        near_sums = lax.all_to_all(sums, CROSS, 0, 0, tiled=True)

    with jax.named_scope("fields"):
        packed = call(
            pack, (shape(OWN_ROWS, NZ),) * Y, 1, 3, scratch=[pltpu.VMEM((128, NZ), f32)], flops=1_000_000
        )(place, object_rows, dual_rows, targets)
        packed = [piece.astype(f16) for piece in packed]
        object_theirs, sums, packed = lax.optimization_barrier((object_theirs, sums, packed))
        fields = round_y([jnp.concatenate([object_theirs, piece]) for piece in packed])
        fields = [field.astype(f32) for field in fields]

    with jax.named_scope("frames"):
        inter_parts = call(
            frame_gradients,
            (shape(2, 128, NZ),) + (shape(2, 128, NZ, dtype=bf16),) * 3,
            1,
            7,
            scratch=[pltpu.VMEM((NDET, NZ), f32)] * 4,
            flops=FRAMES_COST,
        )(place, *fields, probe_field, measured[0], dft_blocks())
        inter_own = inter_parts[0]
        inter_parts = round_y(inter_parts)

    with jax.named_scope("targets"):
        base = FIELD_ROWS + DRIFT_ROWS
        table = jnp.concatenate([field[base : base + 1, : ZL * XC] for field in fields]).astype(jnp.int32)
        table, inter_own = lax.optimization_barrier((table, inter_own))
        tables = [table] + [shifted(table, "zl", ZL, k) for k in range(1, ZL)]

    with jax.named_scope("near_sum"):
        dense, inter = call(
            add_tiles,
            (shape(DEEP, 128, NZ, dtype=bf16), shape(2, 128, NZ)),
            5,
            9,
            scratch=[pltpu.VMEM((ZL, 128, 2 * NZ), f32)],
            flops=1_000_000,
        )(place, *tables, near_sums, *inter_parts, *fields)
        far_sums = lax.all_to_all(dense, ALONG, 0, 0, tiled=True)

    with jax.named_scope("residual"):
        copies, joint = call(
            residual_part, (shape(DEEP, 128, NZ, dtype=bf16), shape(128, NZ)), 0, 1, flops=1_000_000
        )(far_sums)
        residuals = lax.all_to_all(copies, ALONG, 0, 0, tiled=True)
        kept = call(share_out, (shape(ZH, 3, 2 * QR, NZ),) * Y, 1, 2, flops=1_000_000)(place, joint, inter)
        kept = round_y(kept)

    with jax.named_scope("pick"):
        picked = call(
            pick_tiles,
            shape(NEAR, ZL, HITS * QR, 2 * NZ, dtype=bf16),
            5,
            1,
            scratch=[pltpu.VMEM((ZL, 128, 2 * NZ), f32)],
            flops=1_000_000,
        )(place, *tables, residuals)
        picked, kept = lax.optimization_barrier((picked, kept))
        returned = lax.all_to_all(picked, CROSS, 0, 0, tiled=True)

    with jax.named_scope("updates"):
        theirs = across(jnp.stack([piece[1] for piece in kept]))
        object_next, dual_next = call(updates, (shape(128, NZ), shape(128, NZ)), 1, 7, flops=1_000_000)(
            place, *kept, theirs, object_rows, dual_rows
        )

    with jax.named_scope("back_project"):
        ordered = radon.reshape(ZL, XC, HITS, Y, QR, TILE).transpose(5, 1, 3, 0, 2, 4).reshape(TILE, -1)
        volume_next = call(back_project, shape(2 * TILE, NZ), 0, 3, flops=2 * 2048 * 256 * 256)(
            ordered, returned, volume_rows
        )
    return (
        object_next.reshape(object_field.shape),
        dual_next.reshape(dual_field.shape),
        volume_next.reshape(volume.shape),
    )


def solution(mesh):
    fine = Mesh(mesh.devices.reshape(ZL, X, C, ZH, Y), ("zl", "x", "c", "zh", "y"))
    ang = ("zl", "x", "c")
    strip = ("zh", "y")
    return jax.shard_map(
        body,
        mesh=fine,
        in_specs=(
            P(ang, strip, None, None),
            P(ang, strip),
            P(),
            P(ang, strip, None, None),
            P(ang, strip, None, None),
            P(ang + strip, None, None),
            P(ang + strip, None, None, None, None),
            P(ang, None, strip, None),
        ),
        out_specs=(
            P(ang, strip, None, None),
            P(ang, strip, None, None),
            P(ang + strip, None, None),
        ),
        check_vma=False,
    )
```

```python
import math

import jax
import jax.numpy as jnp
import numpy as np
from jax import lax
from jax.experimental import pallas as pl
from jax.experimental.pallas import tpu as pltpu
from jax.sharding import Mesh
from jax.sharding import PartitionSpec as P

PROBE = 128
NZ = 128
NDET = 512
RAYS = 32
TILE = 256
HITS = 2
NR = 16

ZL, X, C, ZH, Y = 4, 4, 2, 2, 4
XC = X * C
CROSS = ("x", "c", "y")
ALONG = ("zh", "zl")
NEAR = XC * Y
DEEP = ZH * ZL
QR = RAYS // Y
FR_DEV = 8
FRAMES_COST = 20_000_000_000
SUMS_LIMIT = 62 << 20

penalty = 1.0
object_step = 0.1
volume_step = 1.0
keep = 1.0 - object_step
share = object_step / keep
f32 = jnp.float32
bf16 = jnp.bfloat16
f16 = jnp.float16

VM = pl.BlockSpec(memory_space=pltpu.VMEM)
SM = pl.BlockSpec(memory_space=pltpu.SMEM)
FAR = pl.BlockSpec(memory_space=pltpu.HBM)


def call(kernel, outs, n_smem, n_vmem, scratch=(), flops=0, moved=1 << 20, limit=48 << 20, n_far=0):
    many = isinstance(outs, tuple)
    return pl.pallas_call(
        kernel,
        out_shape=outs,
        in_specs=[SM] * n_smem + [FAR] * n_far + [VM] * n_vmem,
        out_specs=tuple(VM for _ in outs) if many else VM,
        scratch_shapes=list(scratch),
        compiler_params=pltpu.CompilerParams(vmem_limit_bytes=limit),
        cost_estimate=pl.CostEstimate(flops=flops, bytes_accessed=moved, transcendentals=0),
        name=kernel.__name__,
    )


def shape(*dims, dtype=f32):
    return jax.ShapeDtypeStruct(dims, dtype)


def dft_blocks():
    k = np.arange(PROBE)
    angles = (k[:, None] * k[None, :] % PROBE) * (2.0 * math.pi / PROBE)
    cosine = np.cos(angles) / math.sqrt(PROBE)
    sine = np.sin(angles) / math.sqrt(PROBE)
    both = np.stack([cosine, sine]).astype(np.float32)
    high = both.astype(jnp.bfloat16)
    low = (both - high.astype(np.float32)).astype(jnp.bfloat16)
    return jnp.asarray(np.concatenate([high, low]))


def ray_sums(radon_far, volume_far, target_far, out_ref, target_out, radon_ref, volume_ref, target_ref, sems):
    targets = pltpu.make_async_copy(target_far, target_ref, sems.at[ZL + 1])
    targets.start()
    copies = [pltpu.make_async_copy(volume_far, volume_ref, sems.at[ZL])]
    for zl in range(ZL):
        angles = pl.ds(zl * XC, XC)
        copies.append(pltpu.make_async_copy(radon_far.at[angles], radon_ref.at[angles], sems.at[zl]))
    for copy in copies:
        copy.start()
    copies[0].wait()
    volume_half = jnp.concatenate(
        [volume_ref[pl.ds(0, TILE, stride=2), :], volume_ref[pl.ds(1, TILE, stride=2), :]], axis=1
    ).astype(bf16)
    for zl in range(ZL):
        copies[1 + zl].wait()
        for xc in range(XC):
            rows = radon_ref[zl * XC + xc].reshape(HITS * RAYS, TILE)
            sums = jnp.dot(rows, volume_half, preferred_element_type=f32)
            for y in range(Y):
                low = sums[y * QR : (y + 1) * QR]
                high = sums[RAYS + y * QR : RAYS + (y + 1) * QR]
                out_ref[xc * Y + y, zl] = jnp.concatenate([low, high], axis=0).astype(bf16)
    targets.wait()
    target_out[...] = jnp.zeros(target_out.shape, f32)
    target_out[0:1, : ZL * XC] = target_ref[...].astype(f32)


def tile_groups(place_ref, tables, count):
    zl_here = place_ref[2]
    angles = [lax.rem(zl_here + ZL - back_zl, ZL) for back_zl in range(ZL)]
    groups = []
    for back_y in range(Y):
        y = lax.rem(place_ref[1] + Y - back_y, Y)
        for xc in range(XC):
            for zl, table in zip(angles, tables):
                row = table[back_y, zl_here * XC + xc] * QR
                groups.append((zl, xc * Y + y, pl.ds(pl.multiple_of(row, QR), HITS * QR)))
                if len(groups) == count:
                    yield groups
                    groups = []


def add_tiles(
    place_ref, table_0, table_1, table_2, table_3, sums_ref, inter_0, inter_1, inter_2, inter_3,
    field_0, field_1, field_2, field_3, out_ref, inter_ref, total,
):
    zh = place_ref[0]
    y_here = place_ref[1]
    zl_here = place_ref[2]
    total[...] = jnp.zeros(total.shape, f32)
    for part in range(2):
        inter = (inter_0[part] + inter_1[part].astype(f32)) + (inter_2[part].astype(f32) + inter_3[part].astype(f32))
        inter_ref[part] = inter
        total[zl_here, :, part * NZ : (part + 1) * NZ] = inter * share
    for back, field_ref in enumerate((field_0, field_1, field_2, field_3)):
        owner = zh * Y + lax.rem(y_here + Y - back, Y)
        rows = pl.ds(pl.multiple_of(owner * 2 * QR, 2 * QR), 2 * QR)
        base = FIELD_ROWS
        total[zl_here, rows, :] -= jnp.concatenate(
            [field_ref[base : base + 2 * QR, :], field_ref[base + 2 * QR : base + 4 * QR, :]], axis=1
        )
    for group in tile_groups(place_ref, (table_0, table_1, table_2, table_3), ZL):
        added = [total[zl, rows, :] + sums_ref[near, zl].astype(f32) for zl, near, rows in group]
        for (zl, near, rows), value in zip(group, added):
            total[zl, rows, :] = value
    for zh in range(ZH):
        for zl in range(ZL):
            out_ref[zh * ZL + zl] = total[zl, :, zh * NZ : (zh + 1) * NZ].astype(bf16)


def residual_part(sums_ref, residual_ref, joint_ref):
    total = sums_ref[0].astype(f32)
    for source in range(1, DEEP):
        total = total + sums_ref[source].astype(f32)
    joint_ref[...] = total
    residual = (keep * total).astype(bf16)
    for copy in range(DEEP):
        residual_ref[copy] = residual


def share_out(place_ref, joint_ref, inter_ref, own_ref, one_ref, two_ref, three_ref):
    zh = place_ref[0]
    y = place_ref[1]
    for ahead, ref in enumerate((own_ref, one_ref, two_ref, three_ref)):
        for other in range(ZH):
            owner = lax.rem(zh + other, ZH) * Y + lax.rem(y + ahead, Y)
            rows = pl.ds(pl.multiple_of(owner * 2 * QR, 2 * QR), 2 * QR)
            ref[other, 0] = joint_ref[rows, :]
            for part in range(2):
                ref[other, 1 + part] = inter_ref[part, rows, :]


def pick_tiles(place_ref, table_0, table_1, table_2, table_3, residual_ref, out_ref, rows_ref):
    for zl in range(ZL):
        rows_ref[zl] = jnp.concatenate(
            [residual_ref[zl].astype(f32), residual_ref[ZL + zl].astype(f32)], axis=1
        )

    for group in tile_groups(place_ref, (table_0, table_1, table_2, table_3), 2 * ZL):
        picked = [rows_ref[zl, rows, :].astype(bf16) for zl, near, rows in group]
        for (zl, near, rows), value in zip(group, picked):
            out_ref[near, zl] = value


def back_project(radon_ref, picked_ref, volume_ref, out_ref):
    gradient = jnp.dot(
        radon_ref[...],
        picked_ref[...].reshape(NEAR * ZL * HITS * QR, 2 * NZ),
        preferred_element_type=f32,
    )
    for part in range(2):
        rows = pl.ds(part, TILE, stride=2)
        out_ref[rows, :] = volume_ref[rows, :] - volume_step * gradient[:, part * NZ : (part + 1) * NZ]


def updates(
    place_ref, own_ref, one_ref, two_ref, three_ref, theirs_ref, object_ref, dual_ref, object_out, dual_out
):
    zh = place_ref[0]
    y = place_ref[1]
    for back, ref in enumerate((own_ref, one_ref, two_ref, three_ref)):
        source = lax.rem(y + Y - back, Y)
        for other in range(ZH):
            part = lax.rem(zh + other, ZH)
            for tile in range(2):
                piece = slice(tile * QR, (tile + 1) * QR)
                inter = ref[0, 1 + part, piece, :] + theirs_ref[back, 1 + part, piece, :]
                joint = theirs_ref[back, 0, piece, :] if other else ref[0, 0, piece, :]
                rows = pl.ds((tile * RAYS + source * QR) * 2 + part, QR, stride=2)
                field = object_ref[rows, :]
                dual = dual_ref[rows, :]
                projection = joint + (field + dual) - share * inter
                object_next = field - object_step * (inter + dual + penalty * (field - projection))
                object_out[rows, :] = object_next
                dual_out[rows, :] = dual + penalty * (object_next - projection)


def split(value):
    high = value.astype(bf16)
    return high, (value - high.astype(f32)).astype(bf16)


def complex_blocks(cosine, sine):
    forward = jnp.concatenate(
        [jnp.concatenate([cosine, sine], axis=1), jnp.concatenate([-sine, cosine], axis=1)], axis=0
    )
    backward = jnp.concatenate(
        [jnp.concatenate([cosine, -sine], axis=1), jnp.concatenate([sine, cosine], axis=1)], axis=0
    )
    return forward, backward


def from_left(high_table, low_table, value):
    high, low = split(value)
    return (
        jnp.dot(high_table, high, preferred_element_type=f32)
        + jnp.dot(high_table, low, preferred_element_type=f32)
        + jnp.dot(low_table, high, preferred_element_type=f32)
    )


def from_right(value, high_table, low_table):
    high, low = split(value)
    return (
        jnp.dot(high, high_table, preferred_element_type=f32)
        + jnp.dot(low, high_table, preferred_element_type=f32)
        + jnp.dot(high, low_table, preferred_element_type=f32)
    )


FIELD_ROWS = 2 * 128
DRIFT_ROWS = 4 * QR
OWN_ROWS = 128 + DRIFT_ROWS + QR


def pack(place_ref, object_ref, dual_ref, target_ref, own_ref, one_ref, two_ref, three_ref, both):
    y = place_ref[1]
    both[...] = object_ref[...] + dual_ref[...]
    for ahead, ref in enumerate((own_ref, one_ref, two_ref, three_ref)):
        ref[0:128, :] = object_ref[...]
        ref[128 + DRIFT_ROWS :, :] = target_ref[...]
        for part in range(2):
            for tile in range(2):
                start = (tile * RAYS + lax.rem(y + ahead, Y) * QR) * 2 + part
                base = 128 + (part * 2 + tile) * QR
                ref[base : base + QR, :] = both[pl.ds(start, QR, stride=2), :]


def frame_gradients(
    place_ref, field_0, field_1, field_2, field_3, probe_ref, amplitude_ref, dft_ref, own_ref, sent_one, sent_two, sent_three,
    field_re, field_im, total_re, total_im,
):
    zh = place_ref[0]
    y = place_ref[1]
    for back, field_ref in enumerate((field_0, field_1, field_2, field_3)):
        for other in range(ZH):
            owner = lax.rem(zh + other, ZH) * Y + lax.rem(y + Y - back, Y)
            rows = pl.ds(pl.multiple_of(owner * 64, 64), 64)
            field_re[rows, :] = field_ref[pl.ds((1 - other) * 128, 64, stride=2), :]
            field_im[rows, :] = field_ref[pl.ds((1 - other) * 128 + 1, 64, stride=2), :]
    total_re[...] = jnp.zeros(total_re.shape, f32)
    total_im[...] = jnp.zeros(total_im.shape, f32)
    probe_re = probe_ref[0]
    probe_im = probe_ref[1]
    ah, bh = complex_blocks(dft_ref[0], dft_ref[1])
    al, bl = complex_blocks(dft_ref[2], dft_ref[3])
    frames = [pl.ds(place_ref[3 + frame], PROBE) for frame in range(FR_DEV)]
    waves = []
    for rows in frames:
        object_re = field_re[rows, :]
        object_im = field_im[rows, :]
        waves.append(
            jnp.concatenate(
                [probe_re * object_re - probe_im * object_im, probe_re * object_im + probe_im * object_re], axis=0
            )
        )
    lefts = from_left(ah, al, jnp.concatenate(waves, axis=1))
    sides = jnp.concatenate(
        [
            jnp.concatenate([lefts[:PROBE, i * NZ : (i + 1) * NZ], lefts[PROBE:, i * NZ : (i + 1) * NZ]], axis=1)
            for i in range(FR_DEV)
        ],
        axis=0,
    )
    far = from_right(sides, bh, bl)
    far_re = far[:, :NZ]
    far_im = far[:, NZ:]
    modulus = jnp.sqrt(far_re * far_re + far_im * far_im)
    amplitude = amplitude_ref[...].reshape(FR_DEV * PROBE, NZ)
    shrink = 1.0 - amplitude / jnp.maximum(modulus, 1.0)
    half = from_right(jnp.concatenate([far_re * shrink, far_im * shrink], axis=1), ah, al)
    stacked = jnp.concatenate(
        [
            jnp.concatenate([half[i * PROBE : (i + 1) * PROBE, :NZ], half[i * PROBE : (i + 1) * PROBE, NZ:]], axis=0)
            for i in range(FR_DEV)
        ],
        axis=1,
    )
    backs = from_left(bh, bl, stacked)
    for i, rows in enumerate(frames):
        back_re = backs[:PROBE, i * NZ : (i + 1) * NZ]
        back_im = backs[PROBE:, i * NZ : (i + 1) * NZ]
        total_re[rows, :] += probe_re * back_re + probe_im * back_im
        total_im[rows, :] += probe_re * back_im - probe_im * back_re
    for ahead in range(Y):
        owner = lax.rem(y + ahead, Y)
        for tile in range(0, NR, 2):
            low = pl.ds(pl.multiple_of(tile * RAYS + owner * QR, QR), QR)
            high = pl.ds(pl.multiple_of((tile + 1) * RAYS + owner * QR, QR), QR)
            rows = slice(tile * QR, (tile + 2) * QR)
            for part, total in enumerate((total_re, total_im)):
                piece = jnp.concatenate([total[low, :], total[high, :]], axis=0)
                if ahead == 0:
                    own_ref[part, rows, :] = piece
                else:
                    (sent_one, sent_two, sent_three)[ahead - 1][part, rows, :] = piece.astype(bf16)


def shifted(value, axis, length, step):
    return lax.ppermute(value, axis, [(i, (i + step) % length) for i in range(length)])


def across(value):
    return shifted(value, "zh", ZH, 1)


def round_y(pieces):
    return [pieces[0]] + [shifted(pieces[k], "y", Y, k) for k in range(1, Y)]


def body(measured, positions, probe_field, object_field, dual_field, volume, radon_tiles, tile_range):
    zh = lax.axis_index("zh")
    zl = lax.axis_index("zl")
    y = lax.axis_index("y")
    place = jnp.concatenate([jnp.stack([zh, y, zl]).astype(jnp.int32), positions.reshape(FR_DEV)])
    radon = radon_tiles.reshape(ZL * XC, HITS, RAYS, TILE)
    volume_rows = volume.reshape(2 * TILE, NZ)
    object_rows = object_field.reshape(128, NZ)
    dual_rows = dual_field.reshape(128, NZ)

    with jax.named_scope("ray_sums"):
        object_theirs = across(object_rows.astype(f16))
        sums, targets = call(
            ray_sums,
            (shape(NEAR, ZL, HITS * QR, 2 * NZ, dtype=bf16), shape(QR, NZ)),
            0,
            0,
            n_far=3,
            scratch=[
                pltpu.VMEM(radon.shape, bf16),
                pltpu.VMEM((2 * TILE, NZ), f32),
                pltpu.VMEM((1, ZL * XC), jnp.int32),
                pltpu.SemaphoreType.DMA((ZL + 2,)),
            ],
            flops=2 * 2048 * 256 * 256,
            limit=SUMS_LIMIT,
        )(radon, volume_rows, tile_range.reshape(1, ZL * XC))
        near_sums = lax.all_to_all(sums, CROSS, 0, 0, tiled=True)

    with jax.named_scope("fields"):
        packed = call(
            pack, (shape(OWN_ROWS, NZ),) * Y, 1, 3, scratch=[pltpu.VMEM((128, NZ), f32)], flops=1_000_000
        )(place, object_rows, dual_rows, targets)
        packed = [piece.astype(f16) for piece in packed]
        amplitude = jnp.sqrt(measured[0])
        object_theirs, sums, packed, amplitude = lax.optimization_barrier((object_theirs, sums, packed, amplitude))
        fields = round_y([jnp.concatenate([object_theirs, piece]) for piece in packed])
        fields = [field.astype(f32) for field in fields]

    with jax.named_scope("frames"):
        inter_parts = call(
            frame_gradients,
            (shape(2, 128, NZ),) + (shape(2, 128, NZ, dtype=bf16),) * 3,
            1,
            7,
            scratch=[pltpu.VMEM((NDET, NZ), f32)] * 4,
            flops=FRAMES_COST,
        )(place, *fields, probe_field, amplitude, dft_blocks())
        inter_own = inter_parts[0]
        inter_parts = round_y(inter_parts)

    with jax.named_scope("targets"):
        base = FIELD_ROWS + DRIFT_ROWS
        table = jnp.concatenate([field[base : base + 1, : ZL * XC] for field in fields]).astype(jnp.int32)
        table, inter_own = lax.optimization_barrier((table, inter_own))
        tables = [table] + [shifted(table, "zl", ZL, k) for k in range(1, ZL)]

    with jax.named_scope("near_sum"):
        dense, inter = call(
            add_tiles,
            (shape(DEEP, 128, NZ, dtype=bf16), shape(2, 128, NZ)),
            5,
            9,
            scratch=[pltpu.VMEM((ZL, 128, 2 * NZ), f32)],
            flops=1_000_000,
        )(place, *tables, near_sums, *inter_parts, *fields)
        far_sums = lax.all_to_all(dense, ALONG, 0, 0, tiled=True)

    with jax.named_scope("residual"):
        copies, joint = call(
            residual_part, (shape(DEEP, 128, NZ, dtype=bf16), shape(128, NZ)), 0, 1, flops=1_000_000
        )(far_sums)
        residuals = lax.all_to_all(copies, ALONG, 0, 0, tiled=True)
        kept = call(share_out, (shape(ZH, 3, 2 * QR, NZ),) * Y, 1, 2, flops=1_000_000)(place, joint, inter)
        kept = round_y(kept)

    with jax.named_scope("pick"):
        picked = call(
            pick_tiles,
            shape(NEAR, ZL, HITS * QR, 2 * NZ, dtype=bf16),
            5,
            1,
            scratch=[pltpu.VMEM((ZL, 128, 2 * NZ), f32)],
            flops=1_000_000,
        )(place, *tables, residuals)
        picked, kept = lax.optimization_barrier((picked, kept))
        returned = lax.all_to_all(picked, CROSS, 0, 0, tiled=True)

    with jax.named_scope("updates"):
        theirs = across(jnp.stack([piece[1] for piece in kept]))
        object_next, dual_next = call(updates, (shape(128, NZ), shape(128, NZ)), 1, 7, flops=1_000_000)(
            place, *kept, theirs, object_rows, dual_rows
        )

    with jax.named_scope("back_project"):
        ordered = radon.reshape(ZL, XC, HITS, Y, QR, TILE).transpose(5, 1, 3, 0, 2, 4).reshape(TILE, -1)
        volume_next = call(back_project, shape(2 * TILE, NZ), 0, 3, flops=2 * 2048 * 256 * 256)(
            ordered, returned, volume_rows
        )
    return (
        object_next.reshape(object_field.shape),
        dual_next.reshape(dual_field.shape),
        volume_next.reshape(volume.shape),
    )


def solution(mesh):
    fine = Mesh(mesh.devices.reshape(ZL, X, C, ZH, Y), ("zl", "x", "c", "zh", "y"))
    ang = ("zl", "x", "c")
    strip = ("zh", "y")
    return jax.shard_map(
        body,
        mesh=fine,
        in_specs=(
            P(ang, strip, None, None),
            P(ang, strip),
            P(),
            P(ang, strip, None, None),
            P(ang, strip, None, None),
            P(ang + strip, None, None),
            P(ang + strip, None, None, None, None),
            P(ang, None, strip, None),
        ),
        out_specs=(
            P(ang, strip, None, None),
            P(ang, strip, None, None),
            P(ang + strip, None, None),
        ),
        check_vma=False,
    )
```
